128 devices in a mesh: section: 4 (over y), gy: 4 (over z_lo, core), gx: 8 (over z_hi, x).
Axes of the slice: x: 4, y: 4, z: 4 (z_hi: 2, z_lo: 2; z = z_hi * 2 + z_lo), core: 2. Of those that a mesh axis runs over, the one named last changes fastest.
Arguments:
- fields: float32 [4, 15, 16, 32, 2048], P('section', None, None, 'gy', 'gx'), may hold values from -2 to 2, as said below
- sea_mask: int32 [96, 2048], replicated, may hold values 0 or 1
- bottom: int32 [96, 2048], replicated, may hold values from 2 to 16
- reaction: float32 [15, 15], replicated, may hold values from -1.5 to 1.5
- growth: float32 [15], replicated, may hold values from 0.3 to 3
Outputs:
- advanced: float32 [4, 15, 16, 32, 2048], P('section', None, None, 'gy', 'gx')
The draws below stay inside these ranges and needn't reach their ends.
Inputs may be any that keep to these rules, and one draw needn't show every extreme that they name: `fields`: in slab 0 the velocity channels lie within -1 to 1 and the turbulent energy channels within 0 to 1.5; tracer slabs are positive.
All inputs are finite; a program needn't handle non-finite values.
Results may differ from the reference program's by a relative error of at most 0.0003.
Values sent between devices are 32-bit elements; how exact they have to be, the bound alone decides.
No kernel may reach another device: no remote copies, remote signals or barrier semaphores. Data moves between devices by JAX's collectives and lax.ppermute only.
A program may use at most 128 MiB of HBM per device.

```python
import math
import jax
import jax.numpy as jnp
from jax import lax

FIELDS = 5
TRACERS = 15
NZ = 16
TY = 8
STEPS = 2
ROWS = 32
NY = 96
NX = 2048
N_GY = 4


def draw_fields(key, part):
    keys = jax.random.split(key, 4)
    extent = (3, NZ, ROWS, NX)
    velocity = jnp.clip(0.4 * jax.random.normal(keys[0], (6, NZ, ROWS, NX)), -1.0, 1.0)
    scalars = jnp.clip(jax.random.normal(keys[1], (6, NZ, ROWS, NX)), -2.0, 2.0)
    energy = 1.5 * jax.random.uniform(keys[2], extent)
    tracers = jax.random.uniform(keys[3], (3, TRACERS, NZ, ROWS, NX), minval=0.05, maxval=2.0)
    ocean_part = jnp.concatenate([velocity, scalars, energy], axis=0)
    return jnp.concatenate([ocean_part[None], tracers], axis=0).astype(jnp.float32)


def set_ends(drawn, own_key, smallest, top_value):
    index_at = [jax.random.randint(jax.random.fold_in(own_key, axis), (), 0, length) for axis, length in enumerate(drawn.shape)]
    widest = drawn.shape.index(max(drawn.shape))
    beside = index_at[:widest] + [(index_at[widest] + 1) % drawn.shape[widest]] + index_at[widest + 1:]
    return drawn.at[tuple(index_at)].set(smallest).at[tuple(beside)].set(top_value)


def scatter_about(key, shape, scale, reach, kind=jnp.bfloat16):
    result = scale * jax.random.normal(key, shape, jnp.float32)
    return jnp.clip(result, min=-reach, max=reach).astype(kind)


def setup_inputs(seed: int = 0) -> dict:
    key_list = jax.random.split(jax.random.key(seed), 6)
    fields = draw_fields(jax.random.fold_in(key_list[5], 71), 0)
    sea_mask = set_ends((jax.random.randint(key_list[1], (NY, NX), 0, 8) < 7).astype(jnp.int32), jax.random.fold_in(key_list[1], 1), 0, 1)
    bottom = set_ends(jax.random.randint(key_list[2], (NY, NX), 2, NZ + 1), jax.random.fold_in(key_list[2], 1), 2, NZ).astype(jnp.int32)
    reaction = scatter_about(key_list[3], (TRACERS, TRACERS), TRACERS ** -0.5, 1.5, jnp.float32)
    growth = jnp.clip(jnp.exp(jax.random.uniform(key_list[4], (TRACERS,), jnp.float32, math.log(0.3), math.log(3.0))), 0.3, 3.0)
    return {"fields": fields, "sea_mask": sea_mask, "bottom": bottom, "reaction": reaction, "growth": growth}


TIME_INCREMENT = 0.2
CORIOLIS = 0.5
PRESSURE = 0.5
VISCOSITY = 0.15
DRAG_RATE = 0.1
DIFFUSION_RATE = 0.15
THERMAL_FORCING = 3.0
SHEAR_GAIN = 0.5
DISSIPATION = 0.5
KAPPA_BASE = 0.05
KAPPA_GAIN = 0.15
EXPANSION = 0.2
CONTRACTION = 0.8
WATER_SHADE = 0.05
CHLOROPHYLL_SHADE = 0.1
HALF_SAT = 0.5


def limited(forward, backward):
    return 0.5 * (jnp.sign(forward) + jnp.sign(backward)) * jnp.minimum(jnp.abs(forward), jnp.abs(backward))


def face_flux(values, speeds, kappas, wetness, dimension):
    face_count = values.shape[dimension] - 3

    def window(source, offset):
        return lax.slice_in_dim(source, offset, offset + face_count, axis=dimension)

    before = window(values, 0)
    inside = window(values, 1)
    beyond = window(values, 2)
    farther = window(values, 3)
    opened = window(wetness, 1) * window(wetness, 2)
    speeds_open = window(speeds, 1) * opened
    upwind = inside + 0.5 * limited(beyond - inside, inside - before)
    downwind = beyond - 0.5 * limited(farther - beyond, beyond - inside)
    carried = jnp.maximum(speeds_open, 0.0) * upwind + jnp.minimum(speeds_open, 0.0) * downwind
    spread = 0.5 * (window(kappas, 1) + window(kappas, 2)) * (beyond - inside) * opened
    return carried - spread


def shading(tracers):
    chlorophyll = jnp.maximum(tracers[2], 0.0)
    absorbed = WATER_SHADE + CHLOROPHYLL_SHADE * chlorophyll
    optical = jnp.cumsum(absorbed, axis=0) - absorbed
    sunlight = jnp.exp(-optical)
    return sunlight, CHLOROPHYLL_SHADE * chlorophyll * sunlight


def tracer_update(padded, east_speed, north_speed, kappas, wetness, sunlight, reaction, growth):
    height = padded.shape[2] - 4
    breadth = padded.shape[3] - 4
    across = face_flux(padded[:, :, 2:height + 2, :], east_speed[:, :, 2:height + 2, :], kappas[:, :, 2:height + 2, :], wetness[:, :, 2:height + 2, :], 3)
    upward = face_flux(padded[:, :, :, 2:breadth + 2], north_speed[:, :, :, 2:breadth + 2], kappas[:, :, :, 2:breadth + 2], wetness[:, :, :, 2:breadth + 2], 2)
    tracers = padded[:, :, 2:height + 2, 2:breadth + 2]
    grid_point_is_wet = wetness[:, :, 2:height + 2, 2:breadth + 2]
    cell_kappa = kappas[:, :, 2:height + 2, 2:breadth + 2]
    horizontal = across[:, :, :, :-1] - across[:, :, :, 1:] + upward[:, :, :-1, :] - upward[:, :, 1:, :]
    level_open = grid_point_is_wet[:, 1:] * grid_point_is_wet[:, :-1]
    level_kappa = 0.5 * (cell_kappa[:, 1:] + cell_kappa[:, :-1])
    level_flux = level_kappa * (tracers[:, 1:] - tracers[:, :-1]) * level_open
    bounded = jnp.zeros_like(level_flux[:, :1])
    vertical = jnp.concatenate([level_flux, bounded], axis=1) - jnp.concatenate([bounded, level_flux], axis=1)
    nutrient = jnp.maximum(tracers[0], 0.0)
    uptake = nutrient / (nutrient + HALF_SAT) * sunlight
    growing = growth[:, None, None, None] * jnp.maximum(tracers, 0.0) * uptake[None]
    reacted = jnp.einsum('cd,dzyx->czyx', reaction, growing, precision=lax.Precision.HIGHEST)
    return grid_point_is_wet * (tracers + TIME_INCREMENT * (horizontal + vertical + reacted))


def ocean_update(padded, wetness, thermal_forcing_rate):
    height = padded.shape[2] - 4
    breadth = padded.shape[3] - 4

    def shifted(source, row_step, col_step):
        return source[:, :, 2 + row_step:height + 2 + row_step, 2 + col_step:breadth + 2 + col_step]

    central_entry = shifted(padded, 0, 0)
    wet_centre = shifted(wetness, 0, 0)
    neighbours = ((0, 1), (0, -1), (1, 0), (-1, 0))
    diffusive_curvature = jnp.zeros_like(central_entry)
    for row_step, col_step in neighbours:
        diffusive_curvature = diffusive_curvature + shifted(wetness, row_step, col_step) * (shifted(padded, row_step, col_step) - central_entry)
    diffusive_curvature = wet_centre * diffusive_curvature
    density = CONTRACTION * padded[3:4] - EXPANSION * padded[2:3]
    rho_centre = shifted(density, 0, 0)
    east_grad = 0.5 * (shifted(wetness, 0, 1) * (shifted(density, 0, 1) - rho_centre) + shifted(wetness, 0, -1) * (rho_centre - shifted(density, 0, -1)))
    north_grad = 0.5 * (shifted(wetness, 1, 0) * (shifted(density, 1, 0) - rho_centre) + shifted(wetness, -1, 0) * (rho_centre - shifted(density, -1, 0)))
    east_flow = central_entry[0]
    meridional = central_entry[1]
    seawater_warmth = central_entry[2]
    salinity = central_entry[3]
    energy = central_entry[4]
    grid_point_is_wet = wet_centre[0]
    level_open = grid_point_is_wet[1:] * grid_point_is_wet[:-1]
    sheared = ((east_flow[1:] - east_flow[:-1]) ** 2 + (meridional[1:] - meridional[:-1]) ** 2) * level_open
    sheared = jnp.concatenate([sheared, jnp.zeros_like(sheared[:1])], axis=0)
    fresh_zonal_speed = grid_point_is_wet * (east_flow + TIME_INCREMENT * (CORIOLIS * meridional - PRESSURE * east_grad[0] + VISCOSITY * diffusive_curvature[0] - DRAG_RATE * east_flow))
    fresh_poleward_speed = grid_point_is_wet * (meridional + TIME_INCREMENT * (-CORIOLIS * east_flow - PRESSURE * north_grad[0] + VISCOSITY * diffusive_curvature[1] - DRAG_RATE * meridional))
    fresh_thermal_state = grid_point_is_wet * (seawater_warmth + TIME_INCREMENT * (DIFFUSION_RATE * diffusive_curvature[2] + THERMAL_FORCING * thermal_forcing_rate))
    fresh_saltiness = grid_point_is_wet * (salinity + TIME_INCREMENT * (DIFFUSION_RATE * diffusive_curvature[3]))
    fresh_kinetic_budget = grid_point_is_wet * (energy + TIME_INCREMENT * (SHEAR_GAIN * sheared - DISSIPATION * energy))
    return jnp.stack([fresh_zonal_speed, fresh_poleward_speed, fresh_thermal_state, fresh_saltiness, fresh_kinetic_budget])


def reference(fields, sea_mask, bottom, reaction, growth):
    ocean_state = fields[0].reshape(FIELDS, 3, NZ, N_GY, TY, NX).transpose(0, 2, 3, 1, 4, 5).reshape(FIELDS, NZ, NY, NX)
    even_rows = (jnp.arange(N_GY) % 2 == 0)[None, None, None, :, None, None]
    groups = fields[1:].reshape(3, TRACERS, NZ, N_GY, TY, NX)
    ordered = jnp.where(even_rows, groups, groups[::-1])
    tracers = ordered.transpose(1, 2, 3, 0, 4, 5).reshape(TRACERS, NZ, NY, NX)
    levels = jnp.arange(NZ)[:, None, None]
    wet_cells = (sea_mask[None, :, :] * (levels < bottom[None, :, :])).astype(jnp.float32)
    wetness = jnp.pad(wet_cells, ((0, 0), (2, 2), (2, 2)))[None]
    margin = ((0, 0), (0, 0), (2, 2), (2, 2))
    for step_index in range(STEPS):
        kappas = KAPPA_BASE + KAPPA_GAIN * ocean_state[4]
        flow_pad = jnp.pad(jnp.stack([ocean_state[0], ocean_state[1], kappas]), margin)
        sunlight, thermal_forcing_rate = shading(tracers)
        next_ocean = ocean_update(jnp.pad(ocean_state, margin), wetness, thermal_forcing_rate)
        tracers = tracer_update(jnp.pad(tracers, margin), flow_pad[0:1], flow_pad[1:2], flow_pad[2:3], wetness, sunlight, reaction, growth)
        ocean_state = next_ocean
    ocean_slab = ocean_state.reshape(FIELDS, NZ, N_GY, 3, TY, NX).transpose(0, 3, 1, 2, 4, 5).reshape(TRACERS, NZ, N_GY * TY, NX)
    blocks = tracers.reshape(TRACERS, NZ, N_GY, 3, TY, NX).transpose(3, 0, 1, 2, 4, 5)
    tracer_slabs = jnp.where(even_rows, blocks, blocks[::-1]).reshape(3, TRACERS, NZ, N_GY * TY, NX)
    return jnp.concatenate([ocean_slab[None], tracer_slabs], axis=0)
```

```python
import functools

import jax
import jax.numpy as jnp
from jax import lax
from jax.experimental import pallas as pl
from jax.experimental.pallas import tpu as pltpu
from jax.sharding import PartitionSpec as P

AXES = ("section", "gy", "gx")
NC, NZ, TY, NX = 15, 16, 8, 256
DT = 0.2
F32 = jnp.float32
BF16 = jnp.bfloat16
VMEM_LIMIT = 60 * 1024 * 1024


def minmod(a, b):
    return jnp.maximum(jnp.minimum(a, b), jnp.minimum(jnp.maximum(a, b), 0.0))


def lanes():
    return lax.broadcasted_iota(jnp.int32, (NZ, 128), 1)


def levels():
    return lax.broadcasted_iota(jnp.int32, (NZ, 128), 0).astype(F32)


def halves(row):
    return row[:, :128], row[:, 128:]


def place():
    section = lax.axis_index("section")
    tile = lax.axis_index("gy")
    even = tile % 2 == 0
    third = jnp.where(even, section - 1, 3 - section)
    return section, even, third


def shade(read, sun_ref, heat_ref):
    for h in range(2):
        depth = jnp.zeros((TY, 128), F32)
        for k in range(NZ):
            chlorophyll = jnp.maximum(read(h, k), 0.0)
            sunlight = jnp.exp(-depth)
            depth = depth + (0.05 + 0.1 * chlorophyll)
            sun_ref[h, pl.ds(k, TY, stride=NZ), :] = sunlight
            heat_ref[h, pl.ds(k, TY, stride=NZ), :] = 0.1 * chlorophyll * sunlight


def pack_columns(read, per):
    lane = lanes()

    def body(c, packs):
        packs = list(packs)
        for y in range(TY):
            left, right = read(c, y)
            spot = 32 * (y % 4) + per * c
            here = (lane >= spot) & (lane < spot + per)
            g = y // 4
            packs[g] = jnp.where(here, pltpu.roll(left, spot, 1), packs[g])
            packs[2 + g] = jnp.where(here, pltpu.roll(right, lax.rem(spot + per, 128), 1), packs[2 + g])
        return tuple(packs)

    zero = jnp.zeros((NZ, 128), F32)
    return lax.fori_loop(0, NC, body, (zero,) * 4)


def first_kernel(x_hbm, state_ref, a_ref, zu_ref, zd_ref, right_ref, left_ref, sun_ref, x_ref, sun2, heat2, sems):
    section, even, third = place()
    loads = [
        pltpu.make_async_copy(x_hbm.at[:, :, pl.ds(128 * h, 128)], x_ref.at[h], sems.at[h]) for h in range(2)
    ]
    for load in loads:
        load.start()
    for load in loads:
        load.wait()
    is_ocean = section == 0
    per = jnp.where(is_ocean, 1, 2)

    def read(c, y):
        pair = [x_ref[h, c, pl.ds(y, NZ, stride=TY), :] for h in range(2)]
        put(state_ref, (c, y), pair)
        return pair

    packs = pack_columns(read, per)
    left_ref[:, :128] = packs[0]
    left_ref[:, 128:] = packs[1]
    right_ref[:, :128] = packs[2]
    right_ref[:, 128:] = packs[3]

    @pl.when(is_ocean)
    def _():
        for f in range(5):
            zu_ref[f, 0] = state_ref[3 * f + 2, TY - 1]
            zd_ref[f, 0] = state_ref[3 * f, 0]
        for s in (1, 2, 3):
            t = jnp.where(even, s - 1, 3 - s)

            def body(i, carry):
                for j in range(2):
                    y = 2 * i + j
                    a_ref[s, i, j] = state_ref[t, y]
                    a_ref[s, 4 + i, j] = state_ref[3 + t, y]
                    a_ref[s, 8 + i, j] = 0.8 * state_ref[9 + t, y] - 0.2 * state_ref[6 + t, y]
                    a_ref[s, 12 + i, j] = state_ref[12 + t, y]
                return carry

            lax.fori_loop(0, 4, body, 0)

    @pl.when(section > 0)
    def _():
        above = jnp.where(even, section + 1, section - 1)
        below = jnp.where(even, section - 1, section + 1)
        above = jnp.where((above < 1) | (above > 3), section, above)
        below = jnp.where((below < 1) | (below > 3), section, below)

        def body(c, carry):
            for j in range(2):
                top = state_ref[c, TY - 2 + j]
                base = state_ref[c, j]
                a_ref[above, c, j] = top
                zu_ref[c, j] = top
                a_ref[below, c, j] = base
                zd_ref[c, j] = base
            return carry

        lax.fori_loop(0, NC, body, 0)
        shade(lambda h, k: x_ref[h, 2, TY * k : TY * k + TY, :], sun2, heat2)
        for y in range(TY):
            rows = slice(NZ * y, NZ * y + NZ)
            put(sun_ref, (y,), [sun2[h, rows] for h in range(2)])
            put(a_ref, (0, y // 2, y % 2), [heat2[h, rows] for h in range(2)])


def rim_kernel(state_ref, zu_ref, zd_ref, right_ref, left_ref, r1_ref, r2_ref, r3_ref):
    section, even, _ = place()

    @pl.when(section == 0)
    def _():
        def row(t, f, y):
            if y < 0:
                return zu_ref[f, 0] if t == 0 else state_ref[3 * f + t - 1, TY - 1]
            return zd_ref[f, 0] if t == 2 else state_ref[3 * f + t + 1, 0]

        def fill(out, t):
            for n, y in ((0, -1), (4, TY)):
                out[n] = row(t, 0, y)
                out[n + 1] = row(t, 1, y)
                out[n + 2] = 0.8 * row(t, 3, y) - 0.2 * row(t, 2, y)
                out[n + 3] = row(t, 4, y)
            out[8] = right_ref[...]
            out[9] = left_ref[...]

        fill(r2_ref, 1)

        @pl.when(even)
        def _():
            fill(r1_ref, 0)
            fill(r3_ref, 2)

        @pl.when(jnp.logical_not(even))
        def _():
            fill(r1_ref, 2)
            fill(r3_ref, 0)


def wet(nb_ref, shift, y):
    k = levels()
    row = nb_ref[shift, pl.ds(y + 8, 1), :]
    return tuple(jnp.where(k < row[:, h * 128 : h * 128 + 128], 1.0, 0.0) for h in range(2))


def east_of(pair, edge, last):
    a, b = (pltpu.roll(v, 127, 1) for v in pair)
    return jnp.where(last, b, a), jnp.where(last, edge, b)


def west_of(pair, edge, first):
    a, b = (pltpu.roll(v, 1, 1) for v in pair)
    return jnp.where(first, edge, a), jnp.where(first, a, b)


def level_down(v):
    return pltpu.roll(v, NZ - 1, 0)


def flow_update(get, edge, nb_ref, y, names):
    lane = lanes()
    first, last = lane == 0, lane == 127
    centre, east, west = (wet(nb_ref, s, y) for s in range(3))
    north, south = wet(nb_ref, 0, y + 1), wet(nb_ref, 0, y - 1)
    here = {f: get(f, y) for f in names}
    around = {}
    for f in names:
        if f == "E":
            continue
        around[f] = (
            east_of(here[f], edge(f, y, 1), last),
            west_of(here[f], edge(f, y, 0), first),
            get(f, y + 1),
            get(f, y - 1),
        )
    out = {f: [] for f in names}
    for h in range(2):
        m = centre[h]
        sides = (east[h], west[h], north[h], south[h])

        def lap(f):
            c = here[f][h]
            total = 0.0
            for w, v in zip(sides, around[f]):
                total = total + w * (v[h] - c)
            return m * total

        u, v, e = here["U"][h], here["V"][h], here["E"][h]
        if "T" in names:
            rho = 0.8 * here["S"][h] - 0.2 * here["T"][h]
            near = [0.8 * s[h] - 0.2 * t[h] for s, t in zip(around["S"], around["T"])]
        else:
            rho = here["rho"][h]
            near = [r[h] for r in around["rho"]]
        grad_x = 0.5 * (sides[0] * (near[0] - rho) + sides[1] * (rho - near[1]))
        grad_y = 0.5 * (sides[2] * (near[2] - rho) + sides[3] * (rho - near[3]))
        out["U"].append(m * (u + DT * (0.5 * v - 0.5 * grad_x + 0.15 * lap("U") - 0.1 * u)))
        out["V"].append(m * (v + DT * (-0.5 * u - 0.5 * grad_y + 0.15 * lap("V") - 0.1 * v)))
        inner = jnp.where(levels() < NZ - 1.0, 1.0, 0.0)
        open_below = m * level_down(m) * inner
        du, dv = level_down(u) - u, level_down(v) - v
        shear = (du * du + dv * dv) * open_below
        out["E"].append(m * (e + DT * (0.5 * shear - 0.5 * e)))
        if "T" in names:
            out["T"].append(here["T"][h] * m + m * (DT * (0.15 * lap("T"))))
            out["S"].append(m * (here["S"][h] + DT * (0.15 * lap("S"))))
    return out


def put(ref, index, pair):
    ref[index + (slice(None), slice(0, 128))] = pair[0]
    ref[index + (slice(None), slice(128, 256))] = pair[1]


def column_edges(right_in, left_in):
    slot = {"U": 0, "V": 1, "T": 2, "S": 3, "E": 4}

    def edge(name, y, side, third):
        if name == "rho":
            return 0.8 * edge("S", y, side, third) - 0.2 * edge("T", y, side, third)
        ref = (right_in, left_in)[side]
        spot = 32 * lax.rem(y, 4) + 3 * slot[name] + third
        target = 0 if side == 0 else 127
        return pltpu.roll(ref[lax.div(y, 4)], lax.rem(target - spot + 256, 128), 1)

    return edge


def step_kernel(first_step, *refs):
    if first_step:
        (state_ref, recv_ref, zu_ref, zd_ref, right_ref, left_ref, rim1, rim2, rim3, nb_ref, sun_ref, own_r, own_l,
         wh_ref, wl_ref,
         out_ref, up_ref, down_ref, right_out, left_out, heat_ref, sun_out, flow_out,
         qx, fx, wx, dx, wy, dy, dz, mm, racc, cin, sun2, heat2, green, sems) = refs
    else:
        (state_ref, zu_ref, zd_ref, right_ref, left_ref, heat1, heat2_in, heat3, nb_ref, sun_ref, own_r, own_l,
         wh_ref, wl_ref, flow_ref,
         out_hbm,
         qx, fx, wx, dx, wy, dy, dz, mm, racc, cin, out_ref, sems) = refs
    section, even, third = place()
    lane = lanes()
    first, last = lane == 0, lane == 127

    def copies(pairs):
        started = [pltpu.make_async_copy(s, d, sems.at[i]) for i, (s, d) in enumerate(pairs)]
        for c in started:
            c.start()
        for c in started:
            c.wait()

    for g in range(2):
        cin[0, g] = right_ref[:, g * 128 : g * 128 + 128]
        cin[1, g] = left_ref[:, g * 128 : g * 128 + 128]
    edges = column_edges(cin.at[0], cin.at[1])

    @pl.when(section == 0)
    def _():
        pairs = [(zu_ref.at[pl.ds(0, 5), 0], fx.at[:, 0]), (zd_ref.at[pl.ds(0, 5), 0], fx.at[:, 25])]
        for t in range(3):
            pairs += [(state_ref.at[3 * f + t], fx.at[f, pl.ds(1 + TY * t, TY)]) for f in range(5)]
        copies(pairs)
        names = ("U", "V", "T", "S", "E")

        def get(f, y):
            return halves(fx[names.index(f), y + 1])

        for t in range(3):
            def body(y, carry):
                r = TY * t + y
                out = flow_update(get, lambda f, row, side: edges(f, y, side, t), nb_ref, r, names)
                source = jnp.where(even, t + 1, 3 - t)
                if first_step:
                    heat = recv_ref[source, lax.div(y, 2), lax.rem(y, 2)]
                else:
                    ends = jnp.where(even, heat1[y], heat3[y]) if t == 0 else jnp.where(even, heat3[y], heat1[y])
                    heat = heat2_in[y] if t == 1 else ends
                m = wet(nb_ref, 0, r)
                warm = halves(heat)
                out["T"] = [out["T"][h] + m[h] * (DT * 3.0 * warm[h]) for h in range(2)]
                for f, name in enumerate(names):
                    if first_step:
                        put(out_ref, (3 * f + t, y), out[name])
                    else:
                        for h in range(2):
                            out_ref[h, 3 * f + t, pl.ds(y, NZ, stride=TY), :] = out[name][h]
                return carry

            lax.fori_loop(0, TY, body, 0)
        if first_step:
            for f in range(5):
                up_ref[f, 0] = out_ref[3 * f + 2, TY - 1]
                down_ref[f, 0] = out_ref[3 * f, 0]

    @pl.when(section > 0)
    def _():
        own = [(state_ref, qx.at[pl.ds(0, NC), pl.ds(2, TY)])]
        low, high = qx.at[pl.ds(0, NC), pl.ds(0, 2)], qx.at[pl.ds(0, NC), pl.ds(10, 2)]
        if first_step:
            own += [
                (recv_ref.at[0, pl.ds(4 * f, 4)], fx.at[f, pl.ds(1, TY)].reshape(4, 2, NZ, NX)) for f in range(4)
            ]
            copies(own)
            below = jnp.where(even, section - 1, section + 1)
            above = jnp.where(even, section + 1, section - 1)
            bottom_end, top_end = (below < 1) | (below > 3), (above < 1) | (above > 3)
            for end, z, index, dest in ((bottom_end, zu_ref, below, low), (top_end, zd_ref, above, high)):
                @pl.when(end)
                def _():
                    copies([(z.at[pl.ds(0, NC)], dest)])

                @pl.when(jnp.logical_not(end))
                def _():
                    copies([(recv_ref.at[jnp.clip(index, 0, 3), pl.ds(0, NC)], dest)])

            for s, rim in ((1, rim1), (2, rim2), (3, rim3)):
                @pl.when(section == s)
                def _():
                    for f in range(4):
                        fx[f, 0] = rim[f]
                        fx[f, TY + 1] = rim[4 + f]
                    for side in range(2):
                        for g in range(2):
                            cin[2 + side, g] = rim[8 + side, :, g * 128 : g * 128 + 128]
            for y in range(TY + 2):
                fx[4, y] = 0.05 + 0.15 * fx[3, y]
        else:
            own += [(flow_ref.at[f], fx.at[(0, 1, 4)[f], pl.ds(1, TY)]) for f in range(3)]
            own += [(zu_ref.at[pl.ds(0, NC)], low), (zd_ref.at[pl.ds(0, NC)], high)]
            copies(own)
            fx[1, 0] = zu_ref[NC, 0]
            fx[4, 0] = zu_ref[NC, 1]
            fx[4, TY + 1] = zd_ref[NC, 1]
        flow_edges = column_edges(cin.at[2], cin.at[3])
        fields = {"U": 0, "V": 1, "rho": 2, "E": 3, "K": 4}

        def get(f, y):
            return halves(fx[fields[f], y + 1])

        def spread_lane(ref, side, y, spot):
            v = ref[side, y // 4]
            return jnp.broadcast_to(v[:, spot : spot + 1], (NZ, 128))

        edge_w = [jnp.zeros((NZ, 128), F32)] * 2
        edge_d = [jnp.zeros((NZ, 128), F32)] * 2
        k_index = levels()
        east_k = []
        if first_step:
            turned = [[pltpu.roll(cin[2 + side, g], lax.rem(128 - third, 128), 1) for g in range(2)] for side in range(2)]
        for y in range(TY):
            g, base = y // 4, 32 * (y % 4)
            if first_step:
                def column(side, slot):
                    v = turned[side][g]
                    return jnp.broadcast_to(v[:, base + 3 * slot : base + 3 * slot + 1], (NZ, 128))

                u_west = column(0, 0)
                k_west = 0.05 + 0.15 * column(0, 4)
                k_east = 0.05 + 0.15 * column(1, 4)
            else:
                u_west = spread_lane(cin, 0, y, base + 30)
                k_west = spread_lane(cin, 0, y, base + 31)
                k_east = spread_lane(cin, 1, y, base + 31)
            east_k.append(k_east)
            k_here = jnp.broadcast_to(fx[4, y + 1, :, 0:1], (NZ, 128))
            m_here = jnp.where(k_index < nb_ref[0, y + 8 : y + 9, 0:1], 1.0, 0.0)
            m_west = jnp.where(k_index < nb_ref[2, y + 8 : y + 9, 0:1], 1.0, 0.0)
            both = m_here * m_west
            group = (lane >= base) & (lane < base + 32)
            edge_w[g] = jnp.where(group, DT * both * u_west, edge_w[g])
            edge_d[g] = jnp.where(group, DT * both * (k_west + k_here), edge_d[g])
        packed = []
        for g in range(2):
            half = slice(g * 128, g * 128 + 128)
            q_1 = cin[0, g]
            q_2 = pltpu.roll(q_1, 1, 1)
            q1 = own_l[:, half]
            q0 = pltpu.roll(q1, 1, 1)
            d_2, d_1, d0 = 0.5 * (q_1 - q_2), 0.5 * (q0 - q_1), 0.5 * (q1 - q0)
            h_1, h0 = minmod(d_1, d_2), minmod(d0, d_1)
            w = edge_w[g]
            flux = w * jnp.where(w > 0, q_1 + h_1, q0 - h0) - edge_d[g] * d_1
            q255 = own_r[:, half]
            q257 = cin[1, g]
            q256 = pltpu.roll(q257, 1, 1)
            high_east = q256 - minmod(0.5 * (q257 - q256), 0.5 * (q256 - q255))
            packed.append((d_1, flux, 0.5 * q256, high_east))
        for g in range(2):
            for n in range(4):
                cin[4 + n, g] = packed[g][n]

        for y in range(-1, TY):
            m, m_n = wet(nb_ref, 0, y), wet(nb_ref, 0, y + 1)
            v, k, k_n = get("V", y), get("K", y), get("K", y + 1)
            both = [m[h] * m_n[h] for h in range(2)]
            put(wy, (y + 1,), [DT * both[h] * v[h] for h in range(2)])
            put(dy, (y + 1,), [DT * both[h] * (k[h] + k_n[h]) for h in range(2)])
            if y < 0:
                continue
            m_e = wet(nb_ref, 1, y)
            both = [m[h] * m_e[h] for h in range(2)]
            u = get("U", y)
            k_e = east_of(k, east_k[y], last)
            put(wx, (y,), [DT * both[h] * u[h] for h in range(2)])
            put(dx, (y,), [DT * both[h] * (k[h] + k_e[h]) for h in range(2)])
            inner = jnp.where(k_index < NZ - 1.0, 0.5 * DT, 0.0)
            put(dz, (y,), [inner * (m[h] * level_down(m[h])) * (k[h] + level_down(k[h])) for h in range(2)])
            put(mm, (y,), m)

        def react(y, carry):
            q = qx[pl.ds(0, NC), y + 2]
            x = jnp.maximum(q, 0.0).reshape(NC * NZ, NX)
            x_high = x.astype(BF16)
            x_low = (x - x_high.astype(F32)).astype(BF16)
            total = jnp.dot(wh_ref[...], x_high, preferred_element_type=F32)
            total = total + jnp.dot(wh_ref[...], x_low, preferred_element_type=F32)
            total = total + jnp.dot(wl_ref[...], x_high, preferred_element_type=F32)
            nutrient = jnp.maximum(q[0], 0.0)
            uptake = DT * (nutrient / (nutrient + 0.5) * sun_ref[y])
            racc[:, y] = q + total.reshape(NC, NZ, NX) * uptake[None]
            return carry

        lax.fori_loop(0, TY, react, 0)

        def tracer(c, carry):
            q = {y: halves(qx[c, y + 2]) for y in range(-2, TY + 2)}
            p = {y: [0.5 * v for v in q[y]] for y in q}
            d = {y: [p[y + 1][h] - p[y][h] for h in range(2)] for y in range(-2, TY + 1)}
            s = {y: [minmod(d[y][h], d[y - 1][h]) for h in range(2)] for y in range(-1, TY + 1)}
            north = {}
            for y in range(-1, TY):
                w, f = halves(wy[y + 1]), halves(dy[y + 1])
                north[y] = [
                    w[h] * jnp.where(w[h] > 0, q[y][h] + s[y][h], q[y + 1][h] - s[y + 1][h]) - f[h] * d[y][h]
                    for h in range(2)
                ]
            for y in range(TY):
                g, spot = y // 4, 32 * (y % 4) + 2 * c
                to_first, to_last = 127 - spot, 126 - spot
                p_e = east_of(p[y], pltpu.roll(cin[6, g], to_last, 1), last)
                dxx = [p_e[h] - p[y][h] for h in range(2)]
                d_w = west_of(dxx, pltpu.roll(cin[4, g], to_first, 1), first)
                slope = [minmod(dxx[h], d_w[h]) for h in range(2)]
                low = [q[y][h] + slope[h] for h in range(2)]
                high = [q[y][h] - slope[h] for h in range(2)]
                high_e = east_of(high, pltpu.roll(cin[7, g], to_last, 1), last)
                w, f = halves(wx[y]), halves(dx[y])
                flux = [w[h] * jnp.where(w[h] > 0, low[h], high_e[h]) - f[h] * dxx[h] for h in range(2)]
                flux_w = west_of(flux, pltpu.roll(cin[5, g], to_first, 1), first)
                base, z, m = halves(racc[c, y]), halves(dz[y]), halves(mm[y])
                new = []
                for h in range(2):
                    down = z[h] * (level_down(q[y][h]) - q[y][h])
                    vert = down - pltpu.roll(down, 1, 0)
                    new.append(m[h] * (base[h] + (flux_w[h] - flux[h]) + (north[y - 1][h] - north[y][h]) + vert))
                if first_step:
                    put(out_ref, (c, y), new)
                else:
                    for h in range(2):
                        out_ref[h, c, pl.ds(y, NZ, stride=TY), :] = new[h]
            return carry

        lax.fori_loop(0, NC, tracer, 0)

        if first_step:
            def flow(y, carry):
                out = flow_update(get, lambda f, row, side: flow_edges(f, y, side, third), nb_ref, y, ("U", "V", "rho", "E")[:2] + ("rho", "E"))
                put(flow_out, (0, y), out["U"])
                put(flow_out, (1, y), out["V"])
                put(flow_out, (2, y), [0.05 + 0.15 * e for e in out["E"]])
                return carry

            lax.fori_loop(0, TY, flow, 0)

            def edge_rows(c, carry):
                for j in range(2):
                    up_ref[c, j] = out_ref[c, TY - 2 + j]
                    down_ref[c, j] = out_ref[c, j]
                return carry

            lax.fori_loop(0, NC, edge_rows, 0)
            up_ref[NC, 0] = flow_out[1, TY - 1]
            up_ref[NC, 1] = flow_out[2, TY - 1]
            down_ref[NC, 1] = flow_out[2, 0]
            for y in range(TY):
                for h in range(2):
                    green[h, NZ * y : NZ * y + NZ, :] = out_ref[2, y, :, h * 128 : h * 128 + 128]
            shade(lambda h, k: green[h, pl.ds(k, TY, stride=NZ), :], sun2, heat2)
            for y in range(TY):
                rows = slice(NZ * y, NZ * y + NZ)
                put(sun_out, (y,), [sun2[h, rows] for h in range(2)])
                put(heat_ref, (y,), [heat2[h, rows] for h in range(2)])

    if not first_step:
        copies([(out_ref.at[h], out_hbm.at[:, :, pl.ds(128 * h, 128)]) for h in range(2)])
    if first_step:
        per = jnp.where(section == 0, 1, 2)
        packs = list(pack_columns(lambda c, y: halves(out_ref[c, y]), per))

        @pl.when(section == 0)
        def _():
            for g in range(2):
                left_out[:, g * 128 : g * 128 + 128] = packs[g]
                right_out[:, g * 128 : g * 128 + 128] = packs[2 + g]

        @pl.when(section > 0)
        def _():
            tiles = list(packs)
            for y in range(TY):
                g, base = y // 4, 32 * (y % 4)
                k0 = jnp.broadcast_to(flow_out[2, y, :, 0:1], (NZ, 128))
                u255 = jnp.broadcast_to(flow_out[0, y, :, 255:256], (NZ, 128))
                k255 = jnp.broadcast_to(flow_out[2, y, :, 255:256], (NZ, 128))
                tiles[g] = jnp.where(lane == base + 31, k0, tiles[g])
                tiles[2 + g] = jnp.where(lane == base + 30, u255, tiles[2 + g])
                tiles[2 + g] = jnp.where(lane == base + 31, k255, tiles[2 + g])
            for g in range(2):
                left_out[:, g * 128 : g * 128 + 128] = tiles[g]
                right_out[:, g * 128 : g * 128 + 128] = tiles[2 + g]


def sds(*shape):
    return jax.ShapeDtypeStruct(shape, F32)


def vmem(n):
    return [pl.BlockSpec(memory_space=pltpu.VMEM)] * n


def step_scratch(first_step):
    row = (NZ, NX)
    scratch = [
        pltpu.VMEM((NC, TY + 4) + row, F32),
        pltpu.VMEM((5, 26) + row, F32),
        pltpu.VMEM((TY,) + row, F32),
        pltpu.VMEM((TY,) + row, F32),
        pltpu.VMEM((TY + 1,) + row, F32),
        pltpu.VMEM((TY + 1,) + row, F32),
        pltpu.VMEM((TY,) + row, F32),
        pltpu.VMEM((TY,) + row, F32),
        pltpu.VMEM((NC, TY) + row, F32),
        pltpu.VMEM((8, 2, NZ, 128), F32),
    ]
    if first_step:
        scratch += [pltpu.VMEM((2, TY * NZ, 128), F32)] * 3
    else:
        scratch += [pltpu.VMEM((2, NC, NZ * TY, 128), F32)]
    return scratch + [pltpu.SemaphoreType.DMA((24,))]


def pairs_of(mesh):
    ns, ngy, ngx = (mesh.shape[a] for a in AXES)

    def at(s, g, x):
        return (s * ngy + g) * ngx + x

    cross, inside, right, heat = [], [], [], {1: [], 2: [], 3: []}
    for x in range(ngx):
        for g in range(ngy):
            order = (1, 2, 3) if g % 2 == 0 else (3, 2, 1)
            inside += [(at(a, g, x), at(b, g, x)) for a, b in zip(order, order[1:])]
            if g + 1 < ngy:
                cross += [(at(0, g, x), at(0, g + 1, x)), (at(order[2], g, x), at(order[2], g + 1, x))]
            for s in heat:
                heat[s].append((at(s, g, x), at(0, g, x)))
            if x + 1 < ngx:
                right += [(at(s, g, x), at(s, g, x + 1)) for s in range(ns)]
    return cross, inside + cross, right, heat


def turn(pairs):
    return [(b, a) for a, b in pairs]


def solution(mesh):
    cross, chain, right, heat_pairs = pairs_of(mesh)

    def send(value, pairs):
        return lax.ppermute(value, AXES, pairs)

    def on_device(fields, sea_mask, bottom, reaction, growth):
        section, even, third = place()
        tile, column = lax.axis_index("gy"), lax.axis_index("gx")
        x = fields.reshape(NC, NZ * TY, NX)
        params = pltpu.CompilerParams(vmem_limit_bytes=VMEM_LIMIT)
        row = (NZ, NX)
        state, a_out, zu, zd, east, west, sun = pl.pallas_call(
            first_kernel,
            out_shape=(sds(NC, TY, *row), sds(4, 16, 2, *row), sds(16, 2, *row), sds(16, 2, *row), sds(*row), sds(*row), sds(TY, *row)),
            in_specs=[pl.BlockSpec(memory_space=pl.ANY)],
            out_specs=tuple(vmem(7)),
            scratch_shapes=[pltpu.VMEM((2, NC, NZ * TY, 128), F32)]
            + [pltpu.VMEM((2, TY * NZ, 128), F32)] * 2
            + [pltpu.SemaphoreType.DMA((2,))],
            compiler_params=params,
            name="first",
        )(x)
        recv = lax.all_to_all(a_out, "section", split_axis=0, concat_axis=0, tiled=True)
        zu_in, zd_in = send(zu, cross), send(zd, turn(cross))
        east_in, west_in = send(east, right), send(west, turn(right))
        rims = pl.pallas_call(
            rim_kernel,
            out_shape=tuple([sds(10, *row)] * 3),
            in_specs=vmem(5),
            out_specs=tuple(vmem(3)),
            compiler_params=params,
            name="rims",
        )(state, zu_in, zd_in, east_in, west_in)
        rims = [send(r, turn(heat_pairs[s])) for s, r in zip((1, 2, 3), rims)]

        depth = (sea_mask * bottom).astype(F32)
        start = jnp.where(section == 0, tile * 3, tile * 3 + third) * TY
        window = lax.dynamic_slice(jnp.pad(depth, ((8, 24), (1, 1))), (start, column * NX), (40, NX + 2))
        nb = jnp.stack([window[:, 1 : NX + 1], window[:, 2:], window[:, :NX]])
        weights = (reaction * growth[None, :])[:, None, :, None] * jnp.eye(NZ, dtype=F32)[None, :, None, :]
        weights = weights.reshape(NC * NZ, NC * NZ)
        high = lax.reduce_precision(weights, 8, 7)
        w_high, w_low = high.astype(BF16), (weights - high).astype(BF16)

        state1, up, down, east1, west1, heat1, sun1, flow1 = pl.pallas_call(
            functools.partial(step_kernel, True),
            out_shape=(sds(NC, TY, *row), sds(16, 2, *row), sds(16, 2, *row), sds(*row), sds(*row), sds(TY, *row), sds(TY, *row), sds(3, TY, *row)),
            in_specs=vmem(15),
            out_specs=tuple(vmem(8)),
            scratch_shapes=step_scratch(True),
            compiler_params=params,
            name="step1",
        )(state, recv, zu_in, zd_in, east_in, west_in, *rims, nb, sun, east, west, w_high, w_low)

        up_in, down_in = send(up, chain), send(down, turn(chain))
        east1_in, west1_in = send(east1, right), send(west1, turn(right))
        heats = [send(heat1, heat_pairs[s]) for s in (1, 2, 3)]
        out = pl.pallas_call(
            functools.partial(step_kernel, False),
            out_shape=sds(NC, NZ * TY, NX),
            in_specs=vmem(15),
            out_specs=pl.BlockSpec(memory_space=pl.ANY),
            scratch_shapes=step_scratch(False),
            compiler_params=params,
            name="step2",
        )(state1, up_in, down_in, east1_in, west1_in, *heats, nb, sun1, east1, west1, w_high, w_low, flow1)
        return out.reshape(1, NC, NZ, TY, NX)

    return jax.shard_map(
        on_device,
        mesh=mesh,
        in_specs=(P("section", None, None, "gy", "gx"), P(), P(), P(), P()),
        out_specs=P("section", None, None, "gy", "gx"),
        check_vma=False,
    )
```

```python
import functools

import jax
import jax.numpy as jnp
from jax import lax
from jax.experimental import pallas as pl
from jax.experimental.pallas import tpu as pltpu
from jax.sharding import PartitionSpec as P

AXES = ("section", "gy", "gx")
NC, NZ, TY, NX = 15, 16, 8, 256
DT = 0.2
F32 = jnp.float32
BF16 = jnp.bfloat16
VMEM_LIMIT = 24 * 1024 * 1024


def minmod(a, b):
    return jnp.maximum(jnp.minimum(a, b), jnp.minimum(jnp.maximum(a, b), 0.0))


def lanes():
    return lax.broadcasted_iota(jnp.int32, (NZ, 128), 1)


def levels():
    return lax.broadcasted_iota(jnp.int32, (NZ, 128), 0).astype(F32)


def halves(row):
    return row[:, :128], row[:, 128:]


def place():
    section = lax.axis_index("section")
    tile = lax.axis_index("gy")
    even = tile % 2 == 0
    third = jnp.where(even, section - 1, 3 - section)
    return section, even, third


def shade(read, sun_ref, heat_ref):
    for h in range(2):
        depth = jnp.zeros((TY, 128), F32)
        for k in range(NZ):
            chlorophyll = jnp.maximum(read(h, k), 0.0)
            sunlight = jnp.exp(-depth)
            depth = depth + (0.05 + 0.1 * chlorophyll)
            sun_ref[h, pl.ds(k, TY, stride=NZ), :] = sunlight
            heat_ref[h, pl.ds(k, TY, stride=NZ), :] = 0.1 * chlorophyll * sunlight


def pack_columns(read, per):
    lane = lanes()

    def body(c, packs):
        packs = list(packs)
        for y in range(TY):
            left, right = read(c, y)
            spot = 32 * (y % 4) + per * c
            here = (lane >= spot) & (lane < spot + per)
            g = y // 4
            packs[g] = jnp.where(here, pltpu.roll(left, spot, 1), packs[g])
            packs[2 + g] = jnp.where(here, pltpu.roll(right, lax.rem(spot + per, 128), 1), packs[2 + g])
        return tuple(packs)

    zero = jnp.zeros((NZ, 128), F32)
    return lax.fori_loop(0, NC, body, (zero,) * 4)


def load_block(x_hbm, x_ref, sems):
    loads = [
        pltpu.make_async_copy(x_hbm.at[:, :, pl.ds(128 * h, 128)], x_ref.at[h], sems.at[h]) for h in range(2)
    ]
    for load in loads:
        load.start()
    for load in loads:
        load.wait()


def send_kernel(x_hbm, a_hbm, zu_hbm, zd_hbm, sun_ref, x_ref, top_ref, base_ref, flow_ref, sun2, heat2, sems):
    section, even, _ = place()
    is_ocean = section == 0
    load_block(x_hbm, x_ref, sems)

    def turned(c, y):
        return [x_ref[h, c, pl.ds(y, NZ, stride=TY), :] for h in range(2)]

    @pl.when(is_ocean)
    def _():
        for f in range(5):
            put(top_ref, (f, 0), turned(3 * f + 2, TY - 1))
            put(base_ref, (f, 0), turned(3 * f, 0))
        for t in range(3):
            def body(y, carry):
                i, j = lax.div(y, 2), lax.rem(y, 2)
                salt, warm = turned(9 + t, y), turned(6 + t, y)
                put(flow_ref, (t, i, j), turned(t, y))
                put(flow_ref, (t, 4 + i, j), turned(3 + t, y))
                put(flow_ref, (t, 8 + i, j), [0.8 * salt[h] - 0.2 * warm[h] for h in range(2)])
                put(flow_ref, (t, 12 + i, j), turned(12 + t, y))
                return carry

            lax.fori_loop(0, TY, body, 0)
        outs = [pltpu.make_async_copy(top_ref, zu_hbm, sems.at[0]), pltpu.make_async_copy(base_ref, zd_hbm, sems.at[1])]
        for t in range(3):
            target = jnp.where(even, t + 1, 3 - t)
            outs.append(pltpu.make_async_copy(flow_ref.at[t], a_hbm.at[target], sems.at[2 + t]))
        for out in outs:
            out.start()
        for out in outs:
            out.wait()

    @pl.when(jnp.logical_not(is_ocean))
    def _():
        above = jnp.where(even, section + 1, section - 1)
        below = jnp.where(even, section - 1, section + 1)
        above = jnp.where((above < 1) | (above > 3), section, above)
        below = jnp.where((below < 1) | (below > 3), section, below)

        def body(c, carry):
            for j in range(2):
                put(top_ref, (c, j), turned(c, TY - 2 + j))
                put(base_ref, (c, j), turned(c, j))
            return carry

        lax.fori_loop(0, NC, body, 0)
        outs = [
            pltpu.make_async_copy(top_ref, a_hbm.at[above], sems.at[0]),
            pltpu.make_async_copy(base_ref, a_hbm.at[below], sems.at[1]),
            pltpu.make_async_copy(top_ref, zu_hbm, sems.at[2]),
            pltpu.make_async_copy(base_ref, zd_hbm, sems.at[3]),
        ]
        for out in outs:
            out.start()
        shade(lambda h, k: x_ref[h, 2, TY * k : TY * k + TY, :], sun2, heat2)
        for y in range(TY):
            rows = slice(NZ * y, NZ * y + NZ)
            put(sun_ref, (y,), [sun2[h, rows] for h in range(2)])
            put(flow_ref, (0, y // 2, y % 2), [heat2[h, rows] for h in range(2)])
        warmth = pltpu.make_async_copy(flow_ref.at[0, pl.ds(0, 4)], a_hbm.at[0, pl.ds(0, 4)], sems.at[4])
        warmth.start()
        for out in outs:
            out.wait()
        warmth.wait()


def turn_kernel(x_hbm, sea_hbm, bottom_hbm, state_ref, right_ref, left_ref, nb_ref, x_ref, sea_buf, bottom_buf, sems, wins):
    section, _, third = place()
    tile, column = lax.axis_index("gy"), lax.axis_index("gx")
    is_ocean = section == 0
    per = jnp.where(is_ocean, 1, 2)
    group = jnp.where(is_ocean, 3 * tile, 3 * tile + third)
    n_groups, n_cols = sea_hbm.shape[0] // TY, sea_hbm.shape[1]
    pieces = ((-128, 128), (0, 256), (256, 128))
    copies = []
    for n, (hbm, buf) in enumerate(((sea_hbm, sea_buf), (bottom_hbm, bottom_buf))):
        for g in range(5):
            row = pl.multiple_of(jnp.clip(group + g - 1, 0, n_groups - 1) * TY, TY)
            for i, (offset, width) in enumerate(pieces):
                col = pl.multiple_of(jnp.clip(column * NX + offset, 0, n_cols - width), 128)
                copies.append(
                    pltpu.make_async_copy(
                        hbm.at[pl.ds(row, TY), pl.ds(col, width)],
                        buf.at[g, :, pl.ds(offset + 128, width)],
                        wins.at[n, g, i],
                    )
                )
    for copy in copies:
        copy.start()
    load_block(x_hbm, x_ref, sems)

    def read(c, y):
        pair = [x_ref[h, c, pl.ds(y, NZ, stride=TY), :] for h in range(2)]
        put(state_ref, (c, y), pair)
        return pair

    packs = pack_columns(read, per)
    for g in range(2):
        left_ref[:, g * 128 : g * 128 + 128] = packs[g]
        right_ref[:, g * 128 : g * 128 + 128] = packs[2 + g]
    for copy in copies:
        copy.wait()
    lane = lax.broadcasted_iota(jnp.int32, (TY, 128), 1)
    for g in range(5):
        inside = (group + g - 1 >= 0) & (group + g - 1 < n_groups)
        valid = (column > 0, True, True, column * NX + NX < n_cols)
        depth = []
        for i in range(4):
            part = slice(128 * i, 128 * i + 128)
            value = (sea_buf[g, :, part] * bottom_buf[g, :, part]).astype(F32)
            depth.append(jnp.where(inside & valid[i], value, 0.0))
        rows = slice(TY * g, TY * g + TY)
        for h in range(2):
            cols = slice(128 * h, 128 * h + 128)
            nb_ref[0, rows, cols] = depth[1 + h]
            nb_ref[1, rows, cols] = jnp.where(lane == 127, pltpu.roll(depth[2 + h], 127, 1), pltpu.roll(depth[1 + h], 127, 1))
            nb_ref[2, rows, cols] = jnp.where(lane == 0, pltpu.roll(depth[h], 1, 1), pltpu.roll(depth[1 + h], 1, 1))


def build_weights(reaction_ref, growth_ref, wh_ref, wl_ref):
    size = NC * NZ
    matrix = reaction_ref[...] * growth_ref[...]
    level_of = lax.rem(lax.broadcasted_iota(jnp.int32, (size, size), 0), NZ)
    same = level_of == lax.rem(lax.broadcasted_iota(jnp.int32, (size, size), 1), NZ)
    up = lax.div(lax.broadcasted_iota(jnp.int32, (size, NC), 0), NZ) == lax.broadcasted_iota(jnp.int32, (size, NC), 1)
    across = lax.broadcasted_iota(jnp.int32, (NC, size), 0) == lax.div(lax.broadcasted_iota(jnp.int32, (NC, size), 1), NZ)
    up = jnp.where(up, 1.0, 0.0).astype(BF16)
    across = jnp.where(across, 1.0, 0.0).astype(BF16)
    high = matrix.astype(BF16)
    low = (matrix - high.astype(F32)).astype(BF16)
    for part, out in ((high, wh_ref), (low, wl_ref)):
        wide = jnp.dot(part, across, preferred_element_type=F32).astype(BF16)
        full = jnp.dot(up, wide, preferred_element_type=F32)
        out[...] = jnp.where(same, full, 0.0).astype(BF16)


def react_kernel(build, *refs):
    if build:
        state_ref, sun_ref, reaction_ref, growth_ref, out_ref, wh_ref, wl_ref = refs
    else:
        state_ref, sun_ref, wh_ref, wl_ref, out_ref = refs

    @pl.when(lax.axis_index("section") > 0)
    def _():
        if build:
            build_weights(reaction_ref, growth_ref, wh_ref, wl_ref)

        def react(y, carry):
            q = state_ref[:, y]
            x = jnp.maximum(q, 0.0).reshape(NC * NZ, NX)
            x_high = x.astype(BF16)
            x_low = (x - x_high.astype(F32)).astype(BF16)
            total = jnp.dot(wh_ref[...], x_high, preferred_element_type=F32)
            total = total + jnp.dot(wh_ref[...], x_low, preferred_element_type=F32)
            total = total + jnp.dot(wl_ref[...], x_high, preferred_element_type=F32)
            nutrient = jnp.maximum(q[0], 0.0)
            uptake = DT * (nutrient / (nutrient + 0.5) * sun_ref[y])
            out_ref[:, y] = q + total.reshape(NC, NZ, NX) * uptake[None]
            return carry

        lax.fori_loop(0, TY, react, 0)


def rim_kernel(state_ref, zu_ref, zd_ref, right_ref, left_ref, r1_ref, r2_ref, r3_ref):
    section, even, _ = place()

    @pl.when(section == 0)
    def _():
        def row(t, f, y):
            if y < 0:
                return zu_ref[f, 0] if t == 0 else state_ref[3 * f + t - 1, TY - 1]
            return zd_ref[f, 0] if t == 2 else state_ref[3 * f + t + 1, 0]

        def fill(out, t):
            for n, y in ((0, -1), (4, TY)):
                out[n] = row(t, 0, y)
                out[n + 1] = row(t, 1, y)
                out[n + 2] = 0.8 * row(t, 3, y) - 0.2 * row(t, 2, y)
                out[n + 3] = row(t, 4, y)
            for g in range(2):
                half = slice(g * 128, g * 128 + 128)
                out[8, :, half] = right_ref[:, half] + pltpu.roll(left_ref[:, half], 16, 1)

        fill(r2_ref, 1)

        @pl.when(even)
        def _():
            fill(r1_ref, 0)
            fill(r3_ref, 2)

        @pl.when(jnp.logical_not(even))
        def _():
            fill(r1_ref, 2)
            fill(r3_ref, 0)


def wet(nb_ref, shift, y):
    k = levels()
    row = nb_ref[shift, pl.ds(y + 8, 1), :]
    return tuple(jnp.where(k < row[:, h * 128 : h * 128 + 128], 1.0, 0.0) for h in range(2))


def east_of(pair, edge, last):
    a, b = (pltpu.roll(v, 127, 1) for v in pair)
    return jnp.where(last, b, a), jnp.where(last, edge, b)


def west_of(pair, edge, first):
    a, b = (pltpu.roll(v, 1, 1) for v in pair)
    return jnp.where(first, edge, a), jnp.where(first, a, b)


def level_down(v):
    return pltpu.roll(v, NZ - 1, 0)


def flow_update(get, edge, nb_ref, y, names):
    lane = lanes()
    first, last = lane == 0, lane == 127
    centre, east, west = (wet(nb_ref, s, y) for s in range(3))
    north, south = wet(nb_ref, 0, y + 1), wet(nb_ref, 0, y - 1)
    here = {f: get(f, y) for f in names}
    around = {}
    for f in names:
        if f == "E":
            continue
        around[f] = (
            east_of(here[f], edge(f, y, 1), last),
            west_of(here[f], edge(f, y, 0), first),
            get(f, y + 1),
            get(f, y - 1),
        )
    out = {f: [] for f in names}
    for h in range(2):
        m = centre[h]
        sides = (east[h], west[h], north[h], south[h])

        def lap(f):
            c = here[f][h]
            total = 0.0
            for w, v in zip(sides, around[f]):
                total = total + w * (v[h] - c)
            return m * total

        u, v, e = here["U"][h], here["V"][h], here["E"][h]
        if "T" in names:
            rho = 0.8 * here["S"][h] - 0.2 * here["T"][h]
            near = [0.8 * s[h] - 0.2 * t[h] for s, t in zip(around["S"], around["T"])]
        else:
            rho = here["rho"][h]
            near = [r[h] for r in around["rho"]]
        grad_x = 0.5 * (sides[0] * (near[0] - rho) + sides[1] * (rho - near[1]))
        grad_y = 0.5 * (sides[2] * (near[2] - rho) + sides[3] * (rho - near[3]))
        out["U"].append(m * (u + DT * (0.5 * v - 0.5 * grad_x + 0.15 * lap("U") - 0.1 * u)))
        out["V"].append(m * (v + DT * (-0.5 * u - 0.5 * grad_y + 0.15 * lap("V") - 0.1 * v)))
        inner = jnp.where(levels() < NZ - 1.0, 1.0, 0.0)
        open_below = m * level_down(m) * inner
        du, dv = level_down(u) - u, level_down(v) - v
        shear = (du * du + dv * dv) * open_below
        out["E"].append(m * (e + DT * (0.5 * shear - 0.5 * e)))
        if "T" in names:
            out["T"].append(here["T"][h] * m + m * (DT * (0.15 * lap("T"))))
            out["S"].append(m * (here["S"][h] + DT * (0.15 * lap("S"))))
    return out


def put(ref, index, pair):
    ref[index + (slice(None), slice(0, 128))] = pair[0]
    ref[index + (slice(None), slice(128, 256))] = pair[1]


def column_edges(right_in, left_in):
    slot = {"U": 0, "V": 1, "T": 2, "S": 3, "E": 4}

    def edge(name, y, side, third):
        if name == "rho":
            return 0.8 * edge("S", y, side, third) - 0.2 * edge("T", y, side, third)
        ref = (right_in, left_in)[side]
        spot = 32 * lax.rem(y, 4) + 3 * slot[name] + third
        target = 0 if side == 0 else 127
        return pltpu.roll(ref[lax.div(y, 4)], lax.rem(target - spot + 256, 128), 1)

    return edge


def step_kernel(first_step, *refs):
    if first_step:
        (state_ref, racc, recv_ref, zu_ref, zd_ref, right_ref, left_ref, rim1, rim2, rim3, nb_ref, own_r, own_l,
         out_ref, up_ref, down_ref, right_out, left_out, heat_ref, sun_out, flow_out,
         lowq, highq, fx, wx, dx, wy, dy, dz, mm, cin, sun2, heat2, green) = refs
    else:
        (state_ref, racc, zu_ref, zd_ref, right_ref, left_ref, heat1, heat2_in, heat3, nb_ref, own_r, own_l, flow_ref,
         out_hbm,
         fx, wx, dx, wy, dy, dz, mm, cin, out_ref, sems) = refs
        lowq, highq = zu_ref, zd_ref
    section, even, third = place()
    lane = lanes()
    first, last = lane == 0, lane == 127

    def leave(c, h):
        return pltpu.make_async_copy(out_ref.at[h, c], out_hbm.at[c, :, pl.ds(128 * h, 128)], sems.at[h])

    def copy_rows(n, target, source):
        def body(i, carry):
            target(i)[...] = source(i)[...]
            return carry

        lax.fori_loop(0, n, body, 0)

    for g in range(2):
        cin[0, g] = right_ref[:, g * 128 : g * 128 + 128]
        cin[1, g] = left_ref[:, g * 128 : g * 128 + 128]
    edges = column_edges(cin.at[0], cin.at[1])

    @pl.when(section == 0)
    def _():
        for f in range(5):
            fx[f, 0] = zu_ref[f, 0]
            fx[f, 25] = zd_ref[f, 0]
            for t in range(3):
                copy_rows(TY, lambda i: fx.at[f, 1 + TY * t + i], lambda i: state_ref.at[3 * f + t, i])
        names = ("U", "V", "T", "S", "E")

        def get(f, y):
            return halves(fx[names.index(f), y + 1])

        for t in range(3):
            def body(y, carry):
                r = TY * t + y
                out = flow_update(get, lambda f, row, side: edges(f, y, side, t), nb_ref, r, names)
                source = jnp.where(even, t + 1, 3 - t)
                if first_step:
                    heat = recv_ref[source, lax.div(y, 2), lax.rem(y, 2)]
                else:
                    ends = jnp.where(even, heat1[y], heat3[y]) if t == 0 else jnp.where(even, heat3[y], heat1[y])
                    heat = heat2_in[y] if t == 1 else ends
                m = wet(nb_ref, 0, r)
                warm = halves(heat)
                out["T"] = [out["T"][h] + m[h] * (DT * 3.0 * warm[h]) for h in range(2)]
                for f, name in enumerate(names):
                    if first_step:
                        put(out_ref, (3 * f + t, y), out[name])
                    else:
                        for h in range(2):
                            out_ref[h, 3 * f + t, pl.ds(y, NZ, stride=TY), :] = out[name][h]
                return carry

            lax.fori_loop(0, TY, body, 0)
            if not first_step:
                for f in range(5):
                    for h in range(2):
                        leave(3 * f + t, h).start()
        if first_step:
            for f in range(5):
                up_ref[f, 0] = out_ref[3 * f + 2, TY - 1]
                down_ref[f, 0] = out_ref[3 * f, 0]

    @pl.when(section > 0)
    def _():
        if first_step:
            for f in range(4):
                copy_rows(TY, lambda i: fx.at[f, 1 + i], lambda i: recv_ref.at[0, 4 * f + lax.div(i, 2), lax.rem(i, 2)])
            below = jnp.where(even, section - 1, section + 1)
            above = jnp.where(even, section + 1, section - 1)
            bottom_end, top_end = (below < 1) | (below > 3), (above < 1) | (above > 3)
            for end, z, index, dest in ((bottom_end, zu_ref, below, lowq), (top_end, zd_ref, above, highq)):
                @pl.when(end)
                def _():
                    copy_rows(NC, lambda i: dest.at[i], lambda i: z.at[i])

                @pl.when(jnp.logical_not(end))
                def _():
                    copy_rows(NC, lambda i: dest.at[i], lambda i: recv_ref.at[jnp.clip(index, 0, 3), i])

            for s, rim in ((1, rim1), (2, rim2), (3, rim3)):
                @pl.when(section == s)
                def _():
                    for f in range(4):
                        fx[f, 0] = rim[f]
                        fx[f, TY + 1] = rim[4 + f]
                    for g in range(2):
                        ends = rim[8, :, g * 128 : g * 128 + 128]
                        cin[2, g] = ends
                        cin[3, g] = pltpu.roll(ends, 112, 1)
            for y in range(TY + 2):
                fx[4, y] = 0.05 + 0.15 * fx[3, y]
        else:
            for f, place_of in enumerate((0, 1, 4)):
                copy_rows(TY, lambda i: fx.at[place_of, 1 + i], lambda i: flow_ref.at[f, i])
            fx[1, 0] = zu_ref[NC, 0]
            fx[4, 0] = zu_ref[NC, 1]
            fx[4, TY + 1] = zd_ref[NC, 1]
        flow_edges = column_edges(cin.at[2], cin.at[3])
        fields = {"U": 0, "V": 1, "rho": 2, "E": 3, "K": 4}

        def get(f, y):
            return halves(fx[fields[f], y + 1])

        def spread_lane(ref, side, y, spot):
            v = ref[side, y // 4]
            return jnp.broadcast_to(v[:, spot : spot + 1], (NZ, 128))

        edge_w = [jnp.zeros((NZ, 128), F32)] * 2
        edge_d = [jnp.zeros((NZ, 128), F32)] * 2
        k_index = levels()
        east_k = []
        if first_step:
            turned = [[pltpu.roll(cin[2 + side, g], lax.rem(128 - third, 128), 1) for g in range(2)] for side in range(2)]
        for y in range(TY):
            g, base = y // 4, 32 * (y % 4)
            if first_step:
                def column(side, slot):
                    v = turned[side][g]
                    return jnp.broadcast_to(v[:, base + 3 * slot : base + 3 * slot + 1], (NZ, 128))

                u_west = column(0, 0)
                k_west = 0.05 + 0.15 * column(0, 4)
                k_east = 0.05 + 0.15 * column(1, 4)
            else:
                u_west = spread_lane(cin, 0, y, base + 30)
                k_west = spread_lane(cin, 0, y, base + 31)
                k_east = spread_lane(cin, 1, y, base + 31)
            east_k.append(k_east)
            k_here = jnp.broadcast_to(fx[4, y + 1, :, 0:1], (NZ, 128))
            m_here = jnp.where(k_index < nb_ref[0, y + 8 : y + 9, 0:1], 1.0, 0.0)
            m_west = jnp.where(k_index < nb_ref[2, y + 8 : y + 9, 0:1], 1.0, 0.0)
            both = m_here * m_west
            group = (lane >= base) & (lane < base + 32)
            edge_w[g] = jnp.where(group, DT * both * u_west, edge_w[g])
            edge_d[g] = jnp.where(group, DT * both * (k_west + k_here), edge_d[g])
        packed = []
        for g in range(2):
            half = slice(g * 128, g * 128 + 128)
            q_1 = cin[0, g]
            q_2 = pltpu.roll(q_1, 1, 1)
            q1 = own_l[:, half]
            q0 = pltpu.roll(q1, 1, 1)
            d_2, d_1, d0 = 0.5 * (q_1 - q_2), 0.5 * (q0 - q_1), 0.5 * (q1 - q0)
            h_1, h0 = minmod(d_1, d_2), minmod(d0, d_1)
            w = edge_w[g]
            flux = w * jnp.where(w > 0, q_1 + h_1, q0 - h0) - edge_d[g] * d_1
            q255 = own_r[:, half]
            q257 = cin[1, g]
            q256 = pltpu.roll(q257, 1, 1)
            high_east = q256 - minmod(0.5 * (q257 - q256), 0.5 * (q256 - q255))
            packed.append((d_1, flux, 0.5 * q256, high_east))
        for g in range(2):
            for n in range(4):
                cin[4 + n, g] = packed[g][n]

        for y in range(-1, TY):
            m, m_n = wet(nb_ref, 0, y), wet(nb_ref, 0, y + 1)
            v, k, k_n = get("V", y), get("K", y), get("K", y + 1)
            both = [m[h] * m_n[h] for h in range(2)]
            put(wy, (y + 1,), [DT * both[h] * v[h] for h in range(2)])
            put(dy, (y + 1,), [DT * both[h] * (k[h] + k_n[h]) for h in range(2)])
            if y < 0:
                continue
            m_e = wet(nb_ref, 1, y)
            both = [m[h] * m_e[h] for h in range(2)]
            u = get("U", y)
            k_e = east_of(k, east_k[y], last)
            put(wx, (y,), [DT * both[h] * u[h] for h in range(2)])
            put(dx, (y,), [DT * both[h] * (k[h] + k_e[h]) for h in range(2)])
            inner = jnp.where(k_index < NZ - 1.0, 0.5 * DT, 0.0)
            put(dz, (y,), [inner * (m[h] * level_down(m[h])) * (k[h] + level_down(k[h])) for h in range(2)])
            put(mm, (y,), m)

        def tracer(c, carry):
            q = {y: halves(state_ref[c, y]) for y in range(TY)}
            q.update({y - 2: halves(lowq[c, y]) for y in range(2)})
            q.update({y + TY: halves(highq[c, y]) for y in range(2)})
            p = {y: [0.5 * v for v in q[y]] for y in q}
            d = {y: [p[y + 1][h] - p[y][h] for h in range(2)] for y in range(-2, TY + 1)}
            s = {y: [minmod(d[y][h], d[y - 1][h]) for h in range(2)] for y in range(-1, TY + 1)}
            north = {}
            for y in range(-1, TY):
                w, f = halves(wy[y + 1]), halves(dy[y + 1])
                north[y] = [
                    w[h] * jnp.where(w[h] > 0, q[y][h] + s[y][h], q[y + 1][h] - s[y + 1][h]) - f[h] * d[y][h]
                    for h in range(2)
                ]
            for y in range(TY):
                g, spot = y // 4, 32 * (y % 4) + 2 * c
                to_first, to_last = 127 - spot, 126 - spot
                p_e = east_of(p[y], pltpu.roll(cin[6, g], to_last, 1), last)
                dxx = [p_e[h] - p[y][h] for h in range(2)]
                d_w = west_of(dxx, pltpu.roll(cin[4, g], to_first, 1), first)
                slope = [minmod(dxx[h], d_w[h]) for h in range(2)]
                low = [q[y][h] + slope[h] for h in range(2)]
                high = [q[y][h] - slope[h] for h in range(2)]
                high_e = east_of(high, pltpu.roll(cin[7, g], to_last, 1), last)
                w, f = halves(wx[y]), halves(dx[y])
                flux = [w[h] * jnp.where(w[h] > 0, low[h], high_e[h]) - f[h] * dxx[h] for h in range(2)]
                flux_w = west_of(flux, pltpu.roll(cin[5, g], to_first, 1), first)
                base, z, m = halves(racc[c, y]), halves(dz[y]), halves(mm[y])
                new = []
                for h in range(2):
                    down = z[h] * (level_down(q[y][h]) - q[y][h])
                    vert = down - pltpu.roll(down, 1, 0)
                    new.append(m[h] * (base[h] + (flux_w[h] - flux[h]) + (north[y - 1][h] - north[y][h]) + vert))
                if first_step:
                    put(out_ref, (c, y), new)
                else:
                    for h in range(2):
                        out_ref[h, c, pl.ds(y, NZ, stride=TY), :] = new[h]
            if not first_step:
                for h in range(2):
                    leave(c, h).start()
            return carry

        lax.fori_loop(0, NC, tracer, 0)

        if first_step:
            def flow(y, carry):
                out = flow_update(get, lambda f, row, side: flow_edges(f, y, side, third), nb_ref, y, ("U", "V", "rho", "E")[:2] + ("rho", "E"))
                put(flow_out, (0, y), out["U"])
                put(flow_out, (1, y), out["V"])
                put(flow_out, (2, y), [0.05 + 0.15 * e for e in out["E"]])
                return carry

            lax.fori_loop(0, TY, flow, 0)

            def edge_rows(c, carry):
                for j in range(2):
                    up_ref[c, j] = out_ref[c, TY - 2 + j]
                    down_ref[c, j] = out_ref[c, j]
                return carry

            lax.fori_loop(0, NC, edge_rows, 0)
            up_ref[NC, 0] = flow_out[1, TY - 1]
            up_ref[NC, 1] = flow_out[2, TY - 1]
            down_ref[NC, 1] = flow_out[2, 0]
            for y in range(TY):
                for h in range(2):
                    green[h, NZ * y : NZ * y + NZ, :] = out_ref[2, y, :, h * 128 : h * 128 + 128]
            shade(lambda h, k: green[h, pl.ds(k, TY, stride=NZ), :], sun2, heat2)
            for y in range(TY):
                rows = slice(NZ * y, NZ * y + NZ)
                put(sun_out, (y,), [sun2[h, rows] for h in range(2)])
                put(heat_ref, (y,), [heat2[h, rows] for h in range(2)])

    if not first_step:
        for h in range(2):
            leave(slice(None), h).wait()
    if first_step:
        per = jnp.where(section == 0, 1, 2)
        packs = list(pack_columns(lambda c, y: halves(out_ref[c, y]), per))

        @pl.when(section == 0)
        def _():
            for g in range(2):
                left_out[:, g * 128 : g * 128 + 128] = packs[g]
                right_out[:, g * 128 : g * 128 + 128] = packs[2 + g]

        @pl.when(section > 0)
        def _():
            tiles = list(packs)
            for y in range(TY):
                g, base = y // 4, 32 * (y % 4)
                k0 = jnp.broadcast_to(flow_out[2, y, :, 0:1], (NZ, 128))
                u255 = jnp.broadcast_to(flow_out[0, y, :, 255:256], (NZ, 128))
                k255 = jnp.broadcast_to(flow_out[2, y, :, 255:256], (NZ, 128))
                tiles[g] = jnp.where(lane == base + 31, k0, tiles[g])
                tiles[2 + g] = jnp.where(lane == base + 30, u255, tiles[2 + g])
                tiles[2 + g] = jnp.where(lane == base + 31, k255, tiles[2 + g])
            for g in range(2):
                left_out[:, g * 128 : g * 128 + 128] = tiles[g]
                right_out[:, g * 128 : g * 128 + 128] = tiles[2 + g]


def sds(*shape):
    return jax.ShapeDtypeStruct(shape, F32)


def vmem(n):
    return [pl.BlockSpec(memory_space=pltpu.VMEM)] * n


def step_scratch(first_step):
    row = (NZ, NX)
    scratch = [pltpu.VMEM((NC, 2) + row, F32)] * 2 if first_step else []
    scratch += [
        pltpu.VMEM((5, 26) + row, F32),
        pltpu.VMEM((TY,) + row, F32),
        pltpu.VMEM((TY,) + row, F32),
        pltpu.VMEM((TY + 1,) + row, F32),
        pltpu.VMEM((TY + 1,) + row, F32),
        pltpu.VMEM((TY,) + row, F32),
        pltpu.VMEM((TY,) + row, F32),
        pltpu.VMEM((8, 2, NZ, 128), F32),
    ]
    if first_step:
        return scratch + [pltpu.VMEM((2, TY * NZ, 128), F32)] * 3
    return scratch + [pltpu.VMEM((2, NC, NZ * TY, 128), F32), pltpu.SemaphoreType.DMA((2,))]


def pairs_of(mesh):
    ns, ngy, ngx = (mesh.shape[a] for a in AXES)

    def at(s, g, x):
        return (s * ngy + g) * ngx + x

    cross, inside, right, heat = [], [], [], {1: [], 2: [], 3: []}
    for x in range(ngx):
        for g in range(ngy):
            order = (1, 2, 3) if g % 2 == 0 else (3, 2, 1)
            inside += [(at(a, g, x), at(b, g, x)) for a, b in zip(order, order[1:])]
            if g + 1 < ngy:
                cross += [(at(0, g, x), at(0, g + 1, x)), (at(order[2], g, x), at(order[2], g + 1, x))]
            for s in heat:
                heat[s].append((at(s, g, x), at(0, g, x)))
            if x + 1 < ngx:
                right += [(at(s, g, x), at(s, g, x + 1)) for s in range(ns)]
    return cross, inside + cross, right, heat


def turn(pairs):
    return [(b, a) for a, b in pairs]


def solution(mesh):
    cross, chain, right, heat_pairs = pairs_of(mesh)

    def send(value, pairs):
        return lax.ppermute(value, AXES, pairs)

    def program(fields, sea_mask, bottom, reaction, growth):
        x = fields.reshape(NC, NZ * TY, NX)
        row = (NZ, NX)
        block = sds(NC, TY, *row)
        halo = sds(16, 2, *row)
        anywhere = pl.BlockSpec(memory_space=pl.ANY)
        weights = jax.ShapeDtypeStruct((NC * NZ, NC * NZ), BF16)

        def call(body, out_shape, in_specs, out_specs, scratch=(), cost=None):
            return pl.pallas_call(
                body,
                out_shape=out_shape,
                in_specs=in_specs,
                out_specs=out_specs,
                scratch_shapes=list(scratch),
                compiler_params=pltpu.CompilerParams(vmem_limit_bytes=VMEM_LIMIT),
                cost_estimate=cost,
            )

        x_scratch = pltpu.VMEM((2, NC, NZ * TY, 128), F32)
        rows = pltpu.VMEM((2, TY * NZ, 128), F32)
        a_out, zu, zd, sun = call(
            send_kernel, (sds(4, 16, 2, *row), halo, halo, sds(TY, *row)), [anywhere],
            (anywhere, anywhere, anywhere) + tuple(vmem(1)),
            [x_scratch, pltpu.VMEM((16, 2) + row, F32), pltpu.VMEM((16, 2) + row, F32), pltpu.VMEM((3, 16, 2) + row, F32),
             rows, rows, pltpu.SemaphoreType.DMA((5,))],
        )(x)
        recv = lax.all_to_all(a_out, "section", split_axis=0, concat_axis=0, tiled=True)
        zu_in, zd_in = send(zu, cross), send(zd, turn(cross))
        state, east, west, nb = call(
            turn_kernel, (block, sds(*row), sds(*row), sds(3, 40, NX)), [anywhere] * 3, tuple(vmem(4)),
            [x_scratch, pltpu.VMEM((5, TY, 512), jnp.int32), pltpu.VMEM((5, TY, 512), jnp.int32),
             pltpu.SemaphoreType.DMA((2,)), pltpu.SemaphoreType.DMA((2, 5, 3))],
        )(x, sea_mask, bottom)
        east_in, west_in = send(east, right), send(west, turn(right))
        rims = call(rim_kernel, tuple([sds(9, *row)] * 3), vmem(5), tuple(vmem(3)))(state, zu_in, zd_in, east_in, west_in)
        rims = [send(r, turn(heat_pairs[s])) for s, r in zip((1, 2, 3), rims)]
        react_cost = pl.CostEstimate(flops=6 * 240 * 240 * 2048, bytes_accessed=2 * NC * TY * NZ * NX * 4, transcendentals=0)
        grown, w_high, w_low = call(
            functools.partial(react_kernel, True), (block, weights, weights), vmem(4), tuple(vmem(3)), cost=react_cost,
        )(state, sun, reaction, growth.reshape(1, NC))
        state1, up, down, east1, west1, heat1, sun1, flow1 = call(
            functools.partial(step_kernel, True),
            (block, halo, halo, sds(*row), sds(*row), sds(TY, *row), sds(TY, *row), sds(3, TY, *row)),
            vmem(13), tuple(vmem(8)), step_scratch(True),
        )(state, grown, recv, zu_in, zd_in, east_in, west_in, *rims, nb, east, west)
        up_in, down_in = send(up, chain), send(down, turn(chain))
        east1_in, west1_in = send(east1, right), send(west1, turn(right))
        heats = [send(heat1, heat_pairs[s]) for s in (1, 2, 3)]
        grown1 = call(
            functools.partial(react_kernel, False), block, vmem(4), vmem(1)[0], cost=react_cost,
        )(state1, sun1, w_high, w_low)
        out = call(
            functools.partial(step_kernel, False), sds(NC, NZ * TY, NX), vmem(13), anywhere, step_scratch(False),
        )(state1, grown1, up_in, down_in, east1_in, west1_in, *heats, nb, east1, west1, flow1)
        return out.reshape(1, NC, NZ, TY, NX)

    return jax.shard_map(
        program,
        mesh=mesh,
        in_specs=(P("section", None, None, "gy", "gx"), P(), P(), P(), P()),
        out_specs=P("section", None, None, "gy", "gx"),
        check_vma=False,
    )
```

```python
import functools

import jax
import jax.numpy as jnp
from jax import lax
from jax.experimental import pallas as pl
from jax.experimental.pallas import tpu as pltpu
from jax.sharding import PartitionSpec as P


AXES = ("section", "gy", "gx")
NC, NZ, TY, NX = 15, 16, 8, 256
DT = 0.2
F32 = jnp.float32
BF16 = jnp.bfloat16
VMEM_LIMIT = 24 * 1024 * 1024


def minmod(a, b):
    return jnp.maximum(jnp.minimum(a, b), jnp.minimum(jnp.maximum(a, b), 0.0))


def lanes():
    return lax.broadcasted_iota(jnp.int32, (NZ, 128), 1)


def levels():
    return lax.broadcasted_iota(jnp.int32, (NZ, 128), 0).astype(F32)


def halves(row):
    return row[:, :128], row[:, 128:]


def place():
    section = lax.axis_index("section")
    tile = lax.axis_index("gy")
    even = tile % 2 == 0
    third = jnp.where(even, section - 1, 3 - section)
    return section, even, third


def shade(read, sun_ref, heat_ref):
    for h in range(2):
        depth = jnp.zeros((TY, 128), F32)
        for k in range(NZ):
            chlorophyll = jnp.maximum(read(h, k), 0.0)
            sunlight = jnp.exp(-depth)
            depth = depth + (0.05 + 0.1 * chlorophyll)
            sun_ref[h, pl.ds(k, TY, stride=NZ), :] = sunlight
            heat_ref[h, pl.ds(k, TY, stride=NZ), :] = 0.1 * chlorophyll * sunlight


def pack_columns(read, per):
    lane = lanes()

    def body(c, packs):
        packs = list(packs)
        for y in range(TY):
            left, right = read(c, y)
            spot = 32 * (y % 4) + per * c
            here = (lane >= spot) & (lane < spot + per)
            g = y // 4
            packs[g] = jnp.where(here, pltpu.roll(left, spot, 1), packs[g])
            packs[2 + g] = jnp.where(here, pltpu.roll(right, lax.rem(spot + per, 128), 1), packs[2 + g])
        return tuple(packs)

    zero = jnp.zeros((NZ, 128), F32)
    return lax.fori_loop(0, NC, body, (zero,) * 4)


def load_block(x_hbm, x_ref, sems):
    loads = [
        pltpu.make_async_copy(x_hbm.at[:, :, pl.ds(128 * h, 128)], x_ref.at[h], sems.at[h]) for h in range(2)
    ]
    for load in loads:
        load.start()
    for load in loads:
        load.wait()


def send_kernel(x_hbm, a_hbm, zu_hbm, zd_hbm, x_ref, top_ref, base_ref, flow_ref, sun2, heat2, sems):
    section, even, _ = place()
    is_ocean = section == 0
    load_block(x_hbm, x_ref, sems)

    def turned(c, y):
        return [x_ref[h, c, pl.ds(y, NZ, stride=TY), :] for h in range(2)]

    @pl.when(is_ocean)
    def _():
        for f in range(5):
            put(top_ref, (f, 0), turned(3 * f + 2, TY - 1))
            put(base_ref, (f, 0), turned(3 * f, 0))
        for t in range(3):
            def body(y, carry):
                i, j = lax.div(y, 2), lax.rem(y, 2)
                salt, warm = turned(9 + t, y), turned(6 + t, y)
                put(flow_ref, (t, i, j), turned(t, y))
                put(flow_ref, (t, 4 + i, j), turned(3 + t, y))
                put(flow_ref, (t, 8 + i, j), [0.8 * salt[h] - 0.2 * warm[h] for h in range(2)])
                put(flow_ref, (t, 12 + i, j), turned(12 + t, y))
                return carry

            lax.fori_loop(0, TY, body, 0)
        outs = [pltpu.make_async_copy(top_ref, zu_hbm, sems.at[0]), pltpu.make_async_copy(base_ref, zd_hbm, sems.at[1])]
        for t in range(3):
            target = jnp.where(even, t + 1, 3 - t)
            outs.append(pltpu.make_async_copy(flow_ref.at[t], a_hbm.at[target], sems.at[2 + t]))
        for out in outs:
            out.start()
        for out in outs:
            out.wait()

    @pl.when(jnp.logical_not(is_ocean))
    def _():
        above = jnp.where(even, section + 1, section - 1)
        below = jnp.where(even, section - 1, section + 1)
        above = jnp.where((above < 1) | (above > 3), section, above)
        below = jnp.where((below < 1) | (below > 3), section, below)

        def body(c, carry):
            for j in range(2):
                put(top_ref, (c, j), turned(c, TY - 2 + j))
                put(base_ref, (c, j), turned(c, j))
            return carry

        lax.fori_loop(0, NC, body, 0)
        outs = [
            pltpu.make_async_copy(top_ref, a_hbm.at[above], sems.at[0]),
            pltpu.make_async_copy(base_ref, a_hbm.at[below], sems.at[1]),
            pltpu.make_async_copy(top_ref, zu_hbm, sems.at[2]),
            pltpu.make_async_copy(base_ref, zd_hbm, sems.at[3]),
        ]
        for out in outs:
            out.start()
        shade(lambda h, k: x_ref[h, 2, TY * k : TY * k + TY, :], sun2, heat2)
        for y in range(TY):
            rows = slice(NZ * y, NZ * y + NZ)
            put(flow_ref, (0, y // 2, y % 2), [heat2[h, rows] for h in range(2)])
        warmth = pltpu.make_async_copy(flow_ref.at[0, pl.ds(0, 4)], a_hbm.at[0, pl.ds(0, 4)], sems.at[4])
        warmth.start()
        for out in outs:
            out.wait()
        warmth.wait()


def turn_kernel(x_hbm, sea_hbm, bottom_hbm, state_ref, right_ref, left_ref, nb_ref, sun_ref, ends_ref, x_ref, sea_buf, bottom_buf, sun2, heat2, sems, wins):
    section, _, third = place()
    tile, column = lax.axis_index("gy"), lax.axis_index("gx")
    is_ocean = section == 0
    per = jnp.where(is_ocean, 1, 2)
    group = jnp.where(is_ocean, 3 * tile, 3 * tile + third)
    n_groups, n_cols = sea_hbm.shape[0] // TY, sea_hbm.shape[1]
    pieces = ((-128, 128), (0, 256), (256, 128))
    copies = []
    for n, (hbm, buf) in enumerate(((sea_hbm, sea_buf), (bottom_hbm, bottom_buf))):
        for g in range(5):
            row = pl.multiple_of(jnp.clip(group + g - 1, 0, n_groups - 1) * TY, TY)
            for i, (offset, width) in enumerate(pieces):
                col = pl.multiple_of(jnp.clip(column * NX + offset, 0, n_cols - width), 128)
                copies.append(
                    pltpu.make_async_copy(
                        hbm.at[pl.ds(row, TY), pl.ds(col, width)],
                        buf.at[g, :, pl.ds(offset + 128, width)],
                        wins.at[n, g, i],
                    )
                )
    for copy in copies:
        copy.start()
    load_block(x_hbm, x_ref, sems)

    def read(c, y):
        pair = [x_ref[h, c, pl.ds(y, NZ, stride=TY), :] for h in range(2)]
        put(state_ref, (c, y), pair)
        if y in (0, TY - 1):
            put(ends_ref, (y // (TY - 1), c), pair)
        return pair

    packs = pack_columns(read, per)
    for g in range(2):
        left_ref[:, g * 128 : g * 128 + 128] = packs[g]
        right_ref[:, g * 128 : g * 128 + 128] = packs[2 + g]

    @pl.when(jnp.logical_not(is_ocean))
    def _():
        shade(lambda h, k: x_ref[h, 2, TY * k : TY * k + TY, :], sun2, heat2)
        for y in range(TY):
            put(sun_ref, (y,), [sun2[h, NZ * y : NZ * y + NZ] for h in range(2)])

    for copy in copies:
        copy.wait()
    lane = lax.broadcasted_iota(jnp.int32, (TY, 128), 1)
    for g in range(5):
        inside = (group + g - 1 >= 0) & (group + g - 1 < n_groups)
        valid = (column > 0, True, True, column * NX + NX < n_cols)
        depth = []
        for i in range(4):
            part = slice(128 * i, 128 * i + 128)
            value = (sea_buf[g, :, part] * bottom_buf[g, :, part]).astype(F32)
            depth.append(jnp.where(inside & valid[i], value, 0.0))
        rows = slice(TY * g, TY * g + TY)
        for h in range(2):
            cols = slice(128 * h, 128 * h + 128)
            nb_ref[0, rows, cols] = depth[1 + h]
            nb_ref[1, rows, cols] = jnp.where(lane == 127, pltpu.roll(depth[2 + h], 127, 1), pltpu.roll(depth[1 + h], 127, 1))
            nb_ref[2, rows, cols] = jnp.where(lane == 0, pltpu.roll(depth[h], 1, 1), pltpu.roll(depth[1 + h], 1, 1))


def build_weights(reaction_ref, growth_ref, wh_ref, wl_ref):
    size = NC * NZ
    matrix = reaction_ref[...] * growth_ref[...]
    level_of = lax.rem(lax.broadcasted_iota(jnp.int32, (size, size), 0), NZ)
    same = level_of == lax.rem(lax.broadcasted_iota(jnp.int32, (size, size), 1), NZ)
    up = lax.div(lax.broadcasted_iota(jnp.int32, (size, NC), 0), NZ) == lax.broadcasted_iota(jnp.int32, (size, NC), 1)
    across = lax.broadcasted_iota(jnp.int32, (NC, size), 0) == lax.div(lax.broadcasted_iota(jnp.int32, (NC, size), 1), NZ)
    up = jnp.where(up, 1.0, 0.0).astype(BF16)
    across = jnp.where(across, 1.0, 0.0).astype(BF16)
    high = matrix.astype(BF16)
    low = (matrix - high.astype(F32)).astype(BF16)
    for part, out in ((high, wh_ref), (low, wl_ref)):
        wide = jnp.dot(part, across, preferred_element_type=F32).astype(BF16)
        full = jnp.dot(up, wide, preferred_element_type=F32)
        out[...] = jnp.where(same, full, 0.0).astype(BF16)


def react_kernel(build, *refs):
    if build:
        state_ref, sun_ref, reaction_ref, growth_ref, out_hbm, wh_hbm, wl_hbm, out_ref, wh_ref, wl_ref, sems = refs
    else:
        state_ref, sun_ref, wh_ref, wl_ref, out_ref = refs

    @pl.when(lax.axis_index("section") > 0)
    def _():
        if build:
            build_weights(reaction_ref, growth_ref, wh_ref, wl_ref)

        def react(y, carry):
            q = state_ref[:, y]
            x = jnp.maximum(q, 0.0).reshape(NC * NZ, NX)
            x_high = x.astype(BF16)
            x_low = (x - x_high.astype(F32)).astype(BF16)
            total = jnp.dot(wh_ref[...], x_high, preferred_element_type=F32)
            total = total + jnp.dot(wh_ref[...], x_low, preferred_element_type=F32)
            total = total + jnp.dot(wl_ref[...], x_high, preferred_element_type=F32)
            nutrient = jnp.maximum(q[0], 0.0)
            uptake = DT * (nutrient / (nutrient + 0.5) * sun_ref[y])
            out_ref[:, y] = q + total.reshape(NC, NZ, NX) * uptake[None]
            if build:
                pltpu.make_async_copy(out_ref.at[:, y], out_hbm.at[:, y], sems.at[0]).start()
            return carry

        if build:
            kept = [pltpu.make_async_copy(w, out, sems.at[i]) for i, (w, out) in enumerate(((wh_ref, wh_hbm), (wl_ref, wl_hbm)), 1)]
            for copy in kept:
                copy.start()
        lax.fori_loop(0, TY, react, 0)
        if build:
            for copy in kept:
                copy.wait()
            pltpu.make_async_copy(out_ref, out_hbm, sems.at[0]).wait()


def rim_kernel(ends_ref, zu_ref, zd_ref, right_ref, left_ref, r1_ref, r2_ref, r3_ref):
    section, even, _ = place()

    @pl.when(section == 0)
    def _():
        def row(t, f, y):
            if y < 0:
                return zu_ref[f, 0] if t == 0 else ends_ref[1, 3 * f + t - 1]
            return zd_ref[f, 0] if t == 2 else ends_ref[0, 3 * f + t + 1]

        def fill(out, t):
            for n, y in ((0, -1), (4, TY)):
                out[n] = row(t, 0, y)
                out[n + 1] = row(t, 1, y)
                out[n + 2] = 0.8 * row(t, 3, y) - 0.2 * row(t, 2, y)
                out[n + 3] = row(t, 4, y)
            for g in range(2):
                half = slice(g * 128, g * 128 + 128)
                out[8, :, half] = right_ref[:, half] + pltpu.roll(left_ref[:, half], 16, 1)

        fill(r2_ref, 1)

        @pl.when(even)
        def _():
            fill(r1_ref, 0)
            fill(r3_ref, 2)

        @pl.when(jnp.logical_not(even))
        def _():
            fill(r1_ref, 2)
            fill(r3_ref, 0)


def wet(nb_ref, shift, y):
    k = levels()
    row = nb_ref[shift, pl.ds(y + 8, 1), :]
    return tuple(jnp.where(k < row[:, h * 128 : h * 128 + 128], 1.0, 0.0) for h in range(2))


def east_of(pair, edge, last):
    a, b = (pltpu.roll(v, 127, 1) for v in pair)
    return jnp.where(last, b, a), jnp.where(last, edge, b)


def west_of(pair, edge, first):
    a, b = (pltpu.roll(v, 1, 1) for v in pair)
    return jnp.where(first, edge, a), jnp.where(first, a, b)


def level_down(v):
    return pltpu.roll(v, NZ - 1, 0)


def flow_update(get, edge, nb_ref, y, names):
    lane = lanes()
    first, last = lane == 0, lane == 127
    centre, east, west = (wet(nb_ref, s, y) for s in range(3))
    north, south = wet(nb_ref, 0, y + 1), wet(nb_ref, 0, y - 1)
    here = {f: get(f, y) for f in names}
    around = {}
    for f in names:
        if f == "E":
            continue
        around[f] = (
            east_of(here[f], edge(f, y, 1), last),
            west_of(here[f], edge(f, y, 0), first),
            get(f, y + 1),
            get(f, y - 1),
        )
    out = {f: [] for f in names}
    for h in range(2):
        m = centre[h]
        sides = (east[h], west[h], north[h], south[h])

        def lap(f):
            c = here[f][h]
            total = 0.0
            for w, v in zip(sides, around[f]):
                total = total + w * (v[h] - c)
            return m * total

        u, v, e = here["U"][h], here["V"][h], here["E"][h]
        if "T" in names:
            rho = 0.8 * here["S"][h] - 0.2 * here["T"][h]
            near = [0.8 * s[h] - 0.2 * t[h] for s, t in zip(around["S"], around["T"])]
        else:
            rho = here["rho"][h]
            near = [r[h] for r in around["rho"]]
        grad_x = 0.5 * (sides[0] * (near[0] - rho) + sides[1] * (rho - near[1]))
        grad_y = 0.5 * (sides[2] * (near[2] - rho) + sides[3] * (rho - near[3]))
        out["U"].append(m * (u + DT * (0.5 * v - 0.5 * grad_x + 0.15 * lap("U") - 0.1 * u)))
        out["V"].append(m * (v + DT * (-0.5 * u - 0.5 * grad_y + 0.15 * lap("V") - 0.1 * v)))
        inner = jnp.where(levels() < NZ - 1.0, 1.0, 0.0)
        open_below = m * level_down(m) * inner
        du, dv = level_down(u) - u, level_down(v) - v
        shear = (du * du + dv * dv) * open_below
        out["E"].append(m * (e + DT * (0.5 * shear - 0.5 * e)))
        if "T" in names:
            out["T"].append(here["T"][h] * m + m * (DT * (0.15 * lap("T"))))
            out["S"].append(m * (here["S"][h] + DT * (0.15 * lap("S"))))
    return out


def put(ref, index, pair):
    ref[index + (slice(None), slice(0, 128))] = pair[0]
    ref[index + (slice(None), slice(128, 256))] = pair[1]


def column_edges(right_in, left_in):
    slot = {"U": 0, "V": 1, "T": 2, "S": 3, "E": 4}

    def edge(name, y, side, third):
        if name == "rho":
            return 0.8 * edge("S", y, side, third) - 0.2 * edge("T", y, side, third)
        ref = (right_in, left_in)[side]
        spot = 32 * lax.rem(y, 4) + 3 * slot[name] + third
        target = 0 if side == 0 else 127
        return pltpu.roll(ref[lax.div(y, 4)], lax.rem(target - spot + 256, 128), 1)

    return edge


def step_kernel(first_step, *refs):
    if first_step:
        (state_hbm, racc_hbm, recv_hbm, zu_hbm, zd_hbm, right_hbm, left_hbm, rim1, rim2, rim3, nb_hbm, own_r_hbm, own_l_hbm,
         out_ref, up_ref, down_ref, right_out, left_out, heat_ref, sun_out, flow_out,
         state_ref, racc, inflow, lowq, highq, rim, nb_ref, right_ref, left_ref, own_r, own_l,
         fx, wx, dx, wy, dy, dz, mm, cin, sun2, heat2, green, sems, bands) = refs
    else:
        (state_ref, racc, zu_ref, zd_ref, right_ref, left_ref, heat1, heat2_in, heat3, nb_ref, own_r, own_l, flow_ref,
         out_hbm,
         fx, wx, dx, wy, dy, dz, mm, cin, out_ref, sems) = refs
        lowq, highq = zu_ref, zd_ref
    section, even, third = place()
    lane = lanes()
    first, last = lane == 0, lane == 127

    def leave(c, h):
        return pltpu.make_async_copy(out_ref.at[h, c], out_hbm.at[c, :, pl.ds(128 * h, 128)], sems.at[h])

    def copy_rows(n, target, source):
        def body(i, carry):
            target(i)[...] = source(i)[...]
            return carry

        lax.fori_loop(0, n, body, 0)

    if first_step:
        def fetch(source, target, sem):
            copy = pltpu.make_async_copy(source, target, sem)
            copy.start()
            return copy

        small = [
            fetch(source, target, sems.at[i])
            for i, (source, target) in enumerate(
                ((nb_hbm, nb_ref), (right_hbm, right_ref), (left_hbm, left_ref), (own_r_hbm, own_r), (own_l_hbm, own_l))
            )
        ]

        @pl.when(section == 0)
        def _():
            for t in range(3):
                fetch(recv_hbm.at[jnp.where(even, t + 1, 3 - t), pl.ds(0, 4)], inflow.at[pl.ds(4 * t, 4)], sems.at[5])
            fetch(zu_hbm.at[pl.ds(0, NC)], lowq, sems.at[6])
            fetch(zd_hbm.at[pl.ds(0, NC)], highq, sems.at[7])

        @pl.when(section > 0)
        def _():
            fetch(recv_hbm.at[0], inflow, sems.at[5])
            for s, source in ((1, rim1), (2, rim2), (3, rim3)):
                @pl.when(section == s)
                def _():
                    fetch(source, rim, sems.at[8])
            below = jnp.where(even, section - 1, section + 1)
            above = jnp.where(even, section + 1, section - 1)
            for z, index, dest, sem in ((zu_hbm, below, lowq, 6), (zd_hbm, above, highq, 7)):
                end = (index < 1) | (index > 3)

                @pl.when(end)
                def _():
                    fetch(z.at[pl.ds(0, NC)], dest, sems.at[sem])

                @pl.when(jnp.logical_not(end))
                def _():
                    fetch(recv_hbm.at[jnp.clip(index, 0, 3), pl.ds(0, NC)], dest, sems.at[sem])

        def band(c):
            return (
                lambda: pltpu.make_async_copy(state_hbm.at[c], state_ref.at[c], bands.at[0, c]),
                lambda: pltpu.make_async_copy(racc_hbm.at[c], racc.at[c], bands.at[1, c]),
            )

        for c in range(NC):
            band(c)[0]().start()

            @pl.when(section > 0)
            def _():
                band(c)[1]().start()

        for copy in small:
            copy.wait()

    for g in range(2):
        cin[0, g] = right_ref[:, g * 128 : g * 128 + 128]
        cin[1, g] = left_ref[:, g * 128 : g * 128 + 128]
    edges = column_edges(cin.at[0], cin.at[1])

    @pl.when(section == 0)
    def _():
        if first_step:
            pltpu.make_async_copy(recv_hbm.at[0, pl.ds(0, 12)], inflow.at[pl.ds(0, 12)], sems.at[5]).wait()
            pltpu.make_async_copy(zu_hbm.at[pl.ds(0, NC)], lowq, sems.at[6]).wait()
            pltpu.make_async_copy(zd_hbm.at[pl.ds(0, NC)], highq, sems.at[7]).wait()
            for c in range(NC):
                band(c)[0]().wait()
        south_in, north_in = (lowq, highq) if first_step else (zu_ref, zd_ref)
        for f in range(5):
            fx[f, 0] = south_in[f, 0]
            fx[f, 25] = north_in[f, 0]
            for t in range(3):
                copy_rows(TY, lambda i: fx.at[f, 1 + TY * t + i], lambda i: state_ref.at[3 * f + t, i])
        names = ("U", "V", "T", "S", "E")

        def get(f, y):
            return halves(fx[names.index(f), y + 1])

        for t in range(3):
            def body(y, carry):
                r = TY * t + y
                out = flow_update(get, lambda f, row, side: edges(f, y, side, t), nb_ref, r, names)
                if first_step:
                    heat = inflow[4 * t + lax.div(y, 2), lax.rem(y, 2)]
                else:
                    ends = jnp.where(even, heat1[y], heat3[y]) if t == 0 else jnp.where(even, heat3[y], heat1[y])
                    heat = heat2_in[y] if t == 1 else ends
                m = wet(nb_ref, 0, r)
                warm = halves(heat)
                out["T"] = [out["T"][h] + m[h] * (DT * 3.0 * warm[h]) for h in range(2)]
                for f, name in enumerate(names):
                    if first_step:
                        put(out_ref, (3 * f + t, y), out[name])
                    else:
                        for h in range(2):
                            out_ref[h, 3 * f + t, pl.ds(y, NZ, stride=TY), :] = out[name][h]
                return carry

            lax.fori_loop(0, TY, body, 0)
            if not first_step:
                for f in range(5):
                    for h in range(2):
                        leave(3 * f + t, h).start()
        if first_step:
            for f in range(5):
                up_ref[f, 0] = out_ref[3 * f + 2, TY - 1]
                down_ref[f, 0] = out_ref[3 * f, 0]

    @pl.when(section > 0)
    def _():
        if first_step:
            pltpu.make_async_copy(recv_hbm.at[0], inflow, sems.at[5]).wait()
            pltpu.make_async_copy(rim1, rim, sems.at[8]).wait()
            for f in range(4):
                copy_rows(TY, lambda i: fx.at[f, 1 + i], lambda i: inflow.at[4 * f + lax.div(i, 2), lax.rem(i, 2)])
                fx[f, 0] = rim[f]
                fx[f, TY + 1] = rim[4 + f]
            for g in range(2):
                ends = rim[8, :, g * 128 : g * 128 + 128]
                cin[2, g] = ends
                cin[3, g] = pltpu.roll(ends, 112, 1)
            for y in range(TY + 2):
                fx[4, y] = 0.05 + 0.15 * fx[3, y]
        else:
            for f, place_of in enumerate((0, 1, 4)):
                copy_rows(TY, lambda i: fx.at[place_of, 1 + i], lambda i: flow_ref.at[f, i])
            fx[1, 0] = zu_ref[NC, 0]
            fx[4, 0] = zu_ref[NC, 1]
            fx[4, TY + 1] = zd_ref[NC, 1]
        flow_edges = column_edges(cin.at[2], cin.at[3])
        fields = {"U": 0, "V": 1, "rho": 2, "E": 3, "K": 4}

        def get(f, y):
            return halves(fx[fields[f], y + 1])

        def spread_lane(ref, side, y, spot):
            v = ref[side, y // 4]
            return jnp.broadcast_to(v[:, spot : spot + 1], (NZ, 128))

        edge_w = [jnp.zeros((NZ, 128), F32)] * 2
        edge_d = [jnp.zeros((NZ, 128), F32)] * 2
        k_index = levels()
        east_k = []
        if first_step:
            turned = [[pltpu.roll(cin[2 + side, g], lax.rem(128 - third, 128), 1) for g in range(2)] for side in range(2)]
        for y in range(TY):
            g, base = y // 4, 32 * (y % 4)
            if first_step:
                def column(side, slot):
                    v = turned[side][g]
                    return jnp.broadcast_to(v[:, base + 3 * slot : base + 3 * slot + 1], (NZ, 128))

                u_west = column(0, 0)
                k_west = 0.05 + 0.15 * column(0, 4)
                k_east = 0.05 + 0.15 * column(1, 4)
            else:
                u_west = spread_lane(cin, 0, y, base + 30)
                k_west = spread_lane(cin, 0, y, base + 31)
                k_east = spread_lane(cin, 1, y, base + 31)
            east_k.append(k_east)
            k_here = jnp.broadcast_to(fx[4, y + 1, :, 0:1], (NZ, 128))
            m_here = jnp.where(k_index < nb_ref[0, y + 8 : y + 9, 0:1], 1.0, 0.0)
            m_west = jnp.where(k_index < nb_ref[2, y + 8 : y + 9, 0:1], 1.0, 0.0)
            both = m_here * m_west
            group = (lane >= base) & (lane < base + 32)
            edge_w[g] = jnp.where(group, DT * both * u_west, edge_w[g])
            edge_d[g] = jnp.where(group, DT * both * (k_west + k_here), edge_d[g])
        packed = []
        for g in range(2):
            half = slice(g * 128, g * 128 + 128)
            q_1 = cin[0, g]
            q_2 = pltpu.roll(q_1, 1, 1)
            q1 = own_l[:, half]
            q0 = pltpu.roll(q1, 1, 1)
            d_2, d_1, d0 = 0.5 * (q_1 - q_2), 0.5 * (q0 - q_1), 0.5 * (q1 - q0)
            h_1, h0 = minmod(d_1, d_2), minmod(d0, d_1)
            w = edge_w[g]
            flux = w * jnp.where(w > 0, q_1 + h_1, q0 - h0) - edge_d[g] * d_1
            q255 = own_r[:, half]
            q257 = cin[1, g]
            q256 = pltpu.roll(q257, 1, 1)
            high_east = q256 - minmod(0.5 * (q257 - q256), 0.5 * (q256 - q255))
            packed.append((d_1, flux, 0.5 * q256, high_east))
        for g in range(2):
            for n in range(4):
                cin[4 + n, g] = packed[g][n]

        for y in range(-1, TY):
            m, m_n = wet(nb_ref, 0, y), wet(nb_ref, 0, y + 1)
            v, k, k_n = get("V", y), get("K", y), get("K", y + 1)
            both = [m[h] * m_n[h] for h in range(2)]
            put(wy, (y + 1,), [DT * both[h] * v[h] for h in range(2)])
            put(dy, (y + 1,), [DT * both[h] * (k[h] + k_n[h]) for h in range(2)])
            if y < 0:
                continue
            m_e = wet(nb_ref, 1, y)
            both = [m[h] * m_e[h] for h in range(2)]
            u = get("U", y)
            k_e = east_of(k, east_k[y], last)
            put(wx, (y,), [DT * both[h] * u[h] for h in range(2)])
            put(dx, (y,), [DT * both[h] * (k[h] + k_e[h]) for h in range(2)])
            inner = jnp.where(k_index < NZ - 1.0, 0.5 * DT, 0.0)
            put(dz, (y,), [inner * (m[h] * level_down(m[h])) * (k[h] + level_down(k[h])) for h in range(2)])
            put(mm, (y,), m)

        if first_step:
            pltpu.make_async_copy(zu_hbm.at[pl.ds(0, NC)], lowq, sems.at[6]).wait()
            pltpu.make_async_copy(zd_hbm.at[pl.ds(0, NC)], highq, sems.at[7]).wait()

        def tracer(c, carry):
            if first_step:
                for copy in band(c):
                    copy().wait()
            q = {y: halves(state_ref[c, y]) for y in range(TY)}
            q.update({y - 2: halves(lowq[c, y]) for y in range(2)})
            q.update({y + TY: halves(highq[c, y]) for y in range(2)})
            p = {y: [0.5 * v for v in q[y]] for y in q}
            d = {y: [p[y + 1][h] - p[y][h] for h in range(2)] for y in range(-2, TY + 1)}
            s = {y: [minmod(d[y][h], d[y - 1][h]) for h in range(2)] for y in range(-1, TY + 1)}
            north = {}
            for y in range(-1, TY):
                w, f = halves(wy[y + 1]), halves(dy[y + 1])
                north[y] = [
                    w[h] * jnp.where(w[h] > 0, q[y][h] + s[y][h], q[y + 1][h] - s[y + 1][h]) - f[h] * d[y][h]
                    for h in range(2)
                ]
            for y in range(TY):
                g, spot = y // 4, 32 * (y % 4) + 2 * c
                to_first, to_last = 127 - spot, 126 - spot
                p_e = east_of(p[y], pltpu.roll(cin[6, g], to_last, 1), last)
                dxx = [p_e[h] - p[y][h] for h in range(2)]
                d_w = west_of(dxx, pltpu.roll(cin[4, g], to_first, 1), first)
                slope = [minmod(dxx[h], d_w[h]) for h in range(2)]
                low = [q[y][h] + slope[h] for h in range(2)]
                high = [q[y][h] - slope[h] for h in range(2)]
                high_e = east_of(high, pltpu.roll(cin[7, g], to_last, 1), last)
                w, f = halves(wx[y]), halves(dx[y])
                flux = [w[h] * jnp.where(w[h] > 0, low[h], high_e[h]) - f[h] * dxx[h] for h in range(2)]
                flux_w = west_of(flux, pltpu.roll(cin[5, g], to_first, 1), first)
                base, z, m = halves(racc[c, y]), halves(dz[y]), halves(mm[y])
                new = []
                for h in range(2):
                    down = z[h] * (level_down(q[y][h]) - q[y][h])
                    vert = down - pltpu.roll(down, 1, 0)
                    new.append(m[h] * (base[h] + (flux_w[h] - flux[h]) + (north[y - 1][h] - north[y][h]) + vert))
                if first_step:
                    put(out_ref, (c, y), new)
                else:
                    for h in range(2):
                        out_ref[h, c, pl.ds(y, NZ, stride=TY), :] = new[h]
            if not first_step:
                for h in range(2):
                    leave(c, h).start()
            return carry

        lax.fori_loop(0, NC, tracer, 0)

        if first_step:
            def flow(y, carry):
                out = flow_update(get, lambda f, row, side: flow_edges(f, y, side, third), nb_ref, y, ("U", "V", "rho", "E")[:2] + ("rho", "E"))
                put(flow_out, (0, y), out["U"])
                put(flow_out, (1, y), out["V"])
                put(flow_out, (2, y), [0.05 + 0.15 * e for e in out["E"]])
                return carry

            lax.fori_loop(0, TY, flow, 0)

            def edge_rows(c, carry):
                for j in range(2):
                    up_ref[c, j] = out_ref[c, TY - 2 + j]
                    down_ref[c, j] = out_ref[c, j]
                return carry

            lax.fori_loop(0, NC, edge_rows, 0)
            up_ref[NC, 0] = flow_out[1, TY - 1]
            up_ref[NC, 1] = flow_out[2, TY - 1]
            down_ref[NC, 1] = flow_out[2, 0]
            for y in range(TY):
                for h in range(2):
                    green[h, NZ * y : NZ * y + NZ, :] = out_ref[2, y, :, h * 128 : h * 128 + 128]
            shade(lambda h, k: green[h, pl.ds(k, TY, stride=NZ), :], sun2, heat2)
            for y in range(TY):
                rows = slice(NZ * y, NZ * y + NZ)
                put(sun_out, (y,), [sun2[h, rows] for h in range(2)])
                put(heat_ref, (y,), [heat2[h, rows] for h in range(2)])

    if not first_step:
        for h in range(2):
            leave(slice(None), h).wait()
    if first_step:
        per = jnp.where(section == 0, 1, 2)
        packs = list(pack_columns(lambda c, y: halves(out_ref[c, y]), per))

        @pl.when(section == 0)
        def _():
            for g in range(2):
                left_out[:, g * 128 : g * 128 + 128] = packs[g]
                right_out[:, g * 128 : g * 128 + 128] = packs[2 + g]

        @pl.when(section > 0)
        def _():
            tiles = list(packs)
            for y in range(TY):
                g, base = y // 4, 32 * (y % 4)
                k0 = jnp.broadcast_to(flow_out[2, y, :, 0:1], (NZ, 128))
                u255 = jnp.broadcast_to(flow_out[0, y, :, 255:256], (NZ, 128))
                k255 = jnp.broadcast_to(flow_out[2, y, :, 255:256], (NZ, 128))
                tiles[g] = jnp.where(lane == base + 31, k0, tiles[g])
                tiles[2 + g] = jnp.where(lane == base + 30, u255, tiles[2 + g])
                tiles[2 + g] = jnp.where(lane == base + 31, k255, tiles[2 + g])
            for g in range(2):
                left_out[:, g * 128 : g * 128 + 128] = tiles[g]
                right_out[:, g * 128 : g * 128 + 128] = tiles[2 + g]


def sds(*shape):
    return jax.ShapeDtypeStruct(shape, F32)


def vmem(n):
    return [pl.BlockSpec(memory_space=pltpu.VMEM)] * n


def step_scratch(first_step):
    row = (NZ, NX)
    scratch = []
    if first_step:
        scratch = [pltpu.VMEM((NC, TY) + row, F32)] * 2 + [pltpu.VMEM((16, 2) + row, F32)]
        scratch += [pltpu.VMEM((NC, 2) + row, F32)] * 2
        scratch += [pltpu.VMEM((9,) + row, F32), pltpu.VMEM((3, 40, NX), F32)] + [pltpu.VMEM(row, F32)] * 4
    scratch += [
        pltpu.VMEM((5, 26) + row, F32),
        pltpu.VMEM((TY,) + row, F32),
        pltpu.VMEM((TY,) + row, F32),
        pltpu.VMEM((TY + 1,) + row, F32),
        pltpu.VMEM((TY + 1,) + row, F32),
        pltpu.VMEM((TY,) + row, F32),
        pltpu.VMEM((TY,) + row, F32),
        pltpu.VMEM((8, 2, NZ, 128), F32),
    ]
    if first_step:
        scratch += [pltpu.VMEM((2, TY * NZ, 128), F32)] * 3
        return scratch + [pltpu.SemaphoreType.DMA((9,)), pltpu.SemaphoreType.DMA((2, NC))]
    return scratch + [pltpu.VMEM((2, NC, NZ * TY, 128), F32), pltpu.SemaphoreType.DMA((2,))]


def pairs_of(mesh):
    ns, ngy, ngx = (mesh.shape[a] for a in AXES)

    def at(s, g, x):
        return (s * ngy + g) * ngx + x

    cross, inside, right, heat = [], [], [], {1: [], 2: [], 3: []}
    for x in range(ngx):
        for g in range(ngy):
            order = (1, 2, 3) if g % 2 == 0 else (3, 2, 1)
            inside += [(at(a, g, x), at(b, g, x)) for a, b in zip(order, order[1:])]
            if g + 1 < ngy:
                cross += [(at(0, g, x), at(0, g + 1, x)), (at(order[2], g, x), at(order[2], g + 1, x))]
            for s in heat:
                heat[s].append((at(s, g, x), at(0, g, x)))
            if x + 1 < ngx:
                right += [(at(s, g, x), at(s, g, x + 1)) for s in range(ns)]
    return cross, inside + cross, right, heat


def turn(pairs):
    return [(b, a) for a, b in pairs]


def solution(mesh):
    cross, chain, right, heat_pairs = pairs_of(mesh)

    def send(value, pairs):
        return lax.ppermute(value, AXES, pairs)

    def program(fields, sea_mask, bottom, reaction, growth):
        x = fields.reshape(NC, NZ * TY, NX)
        row = (NZ, NX)
        block = sds(NC, TY, *row)
        halo = sds(16, 2, *row)
        anywhere = pl.BlockSpec(memory_space=pltpu.HBM)
        weights = jax.ShapeDtypeStruct((NC * NZ, NC * NZ), BF16)

        def call(body, out_shape, in_specs, out_specs, scratch=(), cost=None):
            def placed(shape, spec):
                return pltpu.HBM(shape.shape, shape.dtype) if spec is anywhere else shape

            if isinstance(out_specs, tuple):
                out_shape = tuple(placed(*pair) for pair in zip(out_shape, out_specs))
            kernel = pl.pallas_call(
                body,
                out_shape=out_shape,
                in_specs=in_specs,
                out_specs=out_specs,
                scratch_shapes=list(scratch),
                compiler_params=pltpu.CompilerParams(vmem_limit_bytes=VMEM_LIMIT),
                cost_estimate=cost,
            )

            def run(*operands):
                return kernel(*[
                    pltpu.with_memory_space_constraint(v, pltpu.HBM) if spec is anywhere else v
                    for v, spec in zip(operands, in_specs)
                ])

            return run

        x_scratch = pltpu.VMEM((2, NC, NZ * TY, 128), F32)
        rows = pltpu.VMEM((2, TY * NZ, 128), F32)
        a_out, zu, zd = call(
            send_kernel, (sds(4, 16, 2, *row), halo, halo), [anywhere], (anywhere,) * 3,
            [x_scratch, pltpu.VMEM((16, 2) + row, F32), pltpu.VMEM((16, 2) + row, F32), pltpu.VMEM((3, 16, 2) + row, F32),
             rows, rows, pltpu.SemaphoreType.DMA((5,))],
        )(x)
        recv = lax.all_to_all(a_out, "section", split_axis=0, concat_axis=0, tiled=True)
        zu_in, zd_in = send(zu, cross), send(zd, turn(cross))
        state, east, west, nb, sun, ends = call(
            turn_kernel, (block, sds(*row), sds(*row), sds(3, 40, NX), sds(TY, *row), sds(2, NC, *row)),
            [anywhere] * 3, tuple(vmem(6)),
            [x_scratch, pltpu.VMEM((5, TY, 512), jnp.int32), pltpu.VMEM((5, TY, 512), jnp.int32), rows, rows,
             pltpu.SemaphoreType.DMA((2,)), pltpu.SemaphoreType.DMA((2, 5, 3))],
        )(x, sea_mask, bottom)
        east_in, west_in = send(east, right), send(west, turn(right))
        rims = call(rim_kernel, tuple([sds(9, *row)] * 3), vmem(5), tuple(vmem(3)))(ends, zu_in, zd_in, east_in, west_in)
        rims = [send(r, turn(heat_pairs[s])) for s, r in zip((1, 2, 3), rims)]
        react_cost = pl.CostEstimate(flops=6 * 240 * 240 * 2048, bytes_accessed=2 * NC * TY * NZ * NX * 4, transcendentals=0)
        grown, w_high, w_low = call(
            functools.partial(react_kernel, True), (block, weights, weights), vmem(4), (anywhere,) * 3,
            [pltpu.VMEM((NC, TY) + row, F32)] + [pltpu.VMEM((NC * NZ, NC * NZ), BF16)] * 2 + [pltpu.SemaphoreType.DMA((3,))],
            cost=react_cost,
        )(state, sun, reaction, growth.reshape(1, NC))
        state1, up, down, east1, west1, heat1, sun1, flow1 = call(
            functools.partial(step_kernel, True),
            (block, halo, halo, sds(*row), sds(*row), sds(TY, *row), sds(TY, *row), sds(3, TY, *row)),
            [anywhere] * 13, tuple(vmem(8)), step_scratch(True),
        )(state, grown, recv, zu_in, zd_in, east_in, west_in, *rims, nb, east, west)
        up_in, down_in = send(up, chain), send(down, turn(chain))
        east1_in, west1_in = send(east1, right), send(west1, turn(right))
        heats = [send(heat1, heat_pairs[s]) for s in (1, 2, 3)]
        grown1 = call(
            functools.partial(react_kernel, False), block, vmem(4), vmem(1)[0], cost=react_cost,
        )(state1, sun1, w_high, w_low)
        out = call(
            functools.partial(step_kernel, False), sds(NC, NZ * TY, NX), vmem(13), anywhere, step_scratch(False),
        )(state1, grown1, up_in, down_in, east1_in, west1_in, *heats, nb, east1, west1, flow1)
        return out.reshape(1, NC, NZ, TY, NX)

    return jax.shard_map(
        program,
        mesh=mesh,
        in_specs=(P("section", None, None, "gy", "gx"), P(), P(), P(), P()),
        out_specs=P("section", None, None, "gy", "gx"),
        check_vma=False,
    )
```

```python
import functools

import jax
import jax.numpy as jnp
from jax import lax
from jax.experimental import pallas as pl
from jax.experimental.pallas import tpu as pltpu
from jax.sharding import PartitionSpec as P


AXES = ("section", "gy", "gx")
NC, NZ, TY, NX = 15, 16, 8, 256
DT = 0.2
F32 = jnp.float32
BF16 = jnp.bfloat16
VMEM_LIMIT = 24 * 1024 * 1024


def minmod(a, b):
    return jnp.maximum(jnp.minimum(a, b), jnp.minimum(jnp.maximum(a, b), 0.0))


def lanes():
    return lax.broadcasted_iota(jnp.int32, (NZ, 128), 1)


def levels():
    return lax.broadcasted_iota(jnp.int32, (NZ, 128), 0).astype(F32)


def halves(row):
    return row[:, :128], row[:, 128:]


def place():
    section = lax.axis_index("section")
    tile = lax.axis_index("gy")
    even = tile % 2 == 0
    third = jnp.where(even, section - 1, 3 - section)
    return section, even, third


def shade(read, sun_ref, heat_ref):
    for h in range(2):
        depth = jnp.zeros((TY, 128), F32)
        for k in range(NZ):
            chlorophyll = jnp.maximum(read(h, k), 0.0)
            sunlight = jnp.exp(-depth)
            depth = depth + (0.05 + 0.1 * chlorophyll)
            sun_ref[h, pl.ds(k, TY, stride=NZ), :] = sunlight
            heat_ref[h, pl.ds(k, TY, stride=NZ), :] = 0.1 * chlorophyll * sunlight


def pack_columns(read, per):
    lane = lanes()

    def body(c, packs):
        packs = list(packs)
        for y in range(TY):
            left, right = read(c, y)
            spot = 32 * (y % 4) + per * c
            here = (lane >= spot) & (lane < spot + per)
            g = y // 4
            packs[g] = jnp.where(here, pltpu.roll(left, spot, 1), packs[g])
            packs[2 + g] = jnp.where(here, pltpu.roll(right, lax.rem(spot + per, 128), 1), packs[2 + g])
        return tuple(packs)

    zero = jnp.zeros((NZ, 128), F32)
    return lax.fori_loop(0, NC, body, (zero,) * 4)


def load_block(x_hbm, x_ref, sems):
    loads = [
        pltpu.make_async_copy(x_hbm.at[:, :, pl.ds(128 * h, 128)], x_ref.at[h], sems.at[h]) for h in range(2)
    ]
    for load in loads:
        load.start()
    for load in loads:
        load.wait()


def send_kernel(x_hbm, a_hbm, zu_hbm, zd_hbm, ou_ref, od_ref, x_ref, top_ref, base_ref, flow_ref, sun2, heat2, sems):
    section, even, _ = place()
    is_ocean = section == 0
    load_block(x_hbm, x_ref, sems)

    def turned(c, y):
        return [x_ref[h, c, pl.ds(y, NZ, stride=TY), :] for h in range(2)]

    @pl.when(is_ocean)
    def _():
        for f in range(5):
            put(ou_ref, (f,), turned(3 * f + 2, TY - 1))
            put(od_ref, (f,), turned(3 * f, 0))
        for t in range(3):
            def body(y, carry):
                i, j = lax.div(y, 2), lax.rem(y, 2)
                salt, warm = turned(9 + t, y), turned(6 + t, y)
                put(flow_ref, (t, i, j), turned(t, y))
                put(flow_ref, (t, 4 + i, j), turned(3 + t, y))
                put(flow_ref, (t, 8 + i, j), [0.8 * salt[h] - 0.2 * warm[h] for h in range(2)])
                put(flow_ref, (t, 12 + i, j), turned(12 + t, y))
                return carry

            lax.fori_loop(0, TY, body, 0)
        outs = []
        for t in range(3):
            target = jnp.where(even, t + 1, 3 - t)
            outs.append(pltpu.make_async_copy(flow_ref.at[t], a_hbm.at[target], sems.at[2 + t]))
        for out in outs:
            out.start()
        for out in outs:
            out.wait()

    @pl.when(jnp.logical_not(is_ocean))
    def _():
        above = jnp.where(even, section + 1, section - 1)
        below = jnp.where(even, section - 1, section + 1)
        above = jnp.where((above < 1) | (above > 3), section, above)
        below = jnp.where((below < 1) | (below > 3), section, below)

        def body(c, carry):
            for j in range(2):
                put(top_ref, (c, j), turned(c, TY - 2 + j))
                put(base_ref, (c, j), turned(c, j))
            return carry

        lax.fori_loop(0, NC, body, 0)
        outs = [
            pltpu.make_async_copy(top_ref, a_hbm.at[above], sems.at[0]),
            pltpu.make_async_copy(base_ref, a_hbm.at[below], sems.at[1]),
            pltpu.make_async_copy(top_ref, zu_hbm, sems.at[2]),
            pltpu.make_async_copy(base_ref, zd_hbm, sems.at[3]),
        ]
        for out in outs:
            out.start()
        shade(lambda h, k: x_ref[h, 2, TY * k : TY * k + TY, :], sun2, heat2)
        for y in range(TY):
            rows = slice(NZ * y, NZ * y + NZ)
            put(flow_ref, (0, y // 2, y % 2), [heat2[h, rows] for h in range(2)])
        warmth = pltpu.make_async_copy(flow_ref.at[0, pl.ds(0, 4)], a_hbm.at[0, pl.ds(0, 4)], sems.at[4])
        warmth.start()
        for out in outs:
            out.wait()
        warmth.wait()


def by_parity(first_in, second_in):
    odd = lax.rem(lax.axis_index("gx"), 2) == 1
    return jnp.where(odd, first_in, second_in), jnp.where(odd, second_in, first_in)


def give_columns(packs, first_ref, second_ref):
    odd = lax.rem(lax.axis_index("gx"), 2) == 1
    for g in range(2):
        half = slice(g * 128, g * 128 + 128)
        first_ref[:, half] = jnp.where(odd, packs[g], packs[2 + g])
        second_ref[:, half] = jnp.where(odd, packs[2 + g], packs[g])


def column_kernel(x_hbm, first_ref, second_ref, ends_ref, x_ref, sems):
    is_ocean = lax.axis_index("section") == 0
    load_block(x_hbm, x_ref, sems)

    def read(c, y):
        return [x_ref[h, c, pl.ds(y, NZ, stride=TY), :] for h in range(2)]

    give_columns(pack_columns(read, jnp.where(is_ocean, 1, 2)), first_ref, second_ref)

    @pl.when(is_ocean)
    def _():
        def body(c, carry):
            put(ends_ref, (0, c), read(c, 0))
            put(ends_ref, (1, c), read(c, TY - 1))
            return carry

        lax.fori_loop(0, NC, body, 0)


def cut_depths(sea_hbm, bottom_hbm, nb_ref, sea_buf, bottom_buf, wins):
    section, _, third = place()
    tile, column = lax.axis_index("gy"), lax.axis_index("gx")
    is_ocean = section == 0
    group = jnp.where(is_ocean, 3 * tile, 3 * tile + third)
    n_groups, n_cols = sea_hbm.shape[0] // TY, sea_hbm.shape[1]
    pieces = ((-128, 128), (0, 256), (256, 128))
    copies = []
    for n, (hbm, buf) in enumerate(((sea_hbm, sea_buf), (bottom_hbm, bottom_buf))):
        for g in range(5):
            row = pl.multiple_of(jnp.clip(group + g - 1, 0, n_groups - 1) * TY, TY)
            for i, (offset, width) in enumerate(pieces):
                col = pl.multiple_of(jnp.clip(column * NX + offset, 0, n_cols - width), 128)
                copies.append(
                    pltpu.make_async_copy(
                        hbm.at[pl.ds(row, TY), pl.ds(col, width)],
                        buf.at[g, :, pl.ds(offset + 128, width)],
                        wins.at[n, g, i],
                    )
                )
    for copy in copies:
        copy.start()

    def finish():
        for copy in copies:
            copy.wait()
        lane = lax.broadcasted_iota(jnp.int32, (TY, 128), 1)
        for g in range(5):
            inside = (group + g - 1 >= 0) & (group + g - 1 < n_groups)
            valid = (column > 0, True, True, column * NX + NX < n_cols)
            depth = []
            for i in range(4):
                part = slice(128 * i, 128 * i + 128)
                value = (sea_buf[g, :, part] * bottom_buf[g, :, part]).astype(F32)
                depth.append(jnp.where(inside & valid[i], value, 0.0))
            rows = slice(TY * g, TY * g + TY)
            for h in range(2):
                cols = slice(128 * h, 128 * h + 128)
                nb_ref[0, rows, cols] = depth[1 + h]
                nb_ref[1, rows, cols] = jnp.where(lane == 127, pltpu.roll(depth[2 + h], 127, 1), pltpu.roll(depth[1 + h], 127, 1))
                nb_ref[2, rows, cols] = jnp.where(lane == 0, pltpu.roll(depth[h], 1, 1), pltpu.roll(depth[1 + h], 1, 1))

    return finish


def build_weights(reaction_ref, growth_ref, wh_ref, wl_ref):
    size = NC * NZ
    matrix = reaction_ref[...] * growth_ref[...]
    level_of = lax.rem(lax.broadcasted_iota(jnp.int32, (size, size), 0), NZ)
    same = level_of == lax.rem(lax.broadcasted_iota(jnp.int32, (size, size), 1), NZ)
    up = lax.div(lax.broadcasted_iota(jnp.int32, (size, NC), 0), NZ) == lax.broadcasted_iota(jnp.int32, (size, NC), 1)
    across = lax.broadcasted_iota(jnp.int32, (NC, size), 0) == lax.div(lax.broadcasted_iota(jnp.int32, (NC, size), 1), NZ)
    up = jnp.where(up, 1.0, 0.0).astype(BF16)
    across = jnp.where(across, 1.0, 0.0).astype(BF16)
    high = matrix.astype(BF16)
    low = (matrix - high.astype(F32)).astype(BF16)
    for part, out in ((high, wh_ref), (low, wl_ref)):
        wide = jnp.dot(part, across, preferred_element_type=F32).astype(BF16)
        full = jnp.dot(up, wide, preferred_element_type=F32)
        out[...] = jnp.where(same, full, 0.0).astype(BF16)


def react_kernel(build, *refs):
    if build:
        (x_hbm, sea_hbm, bottom_hbm, reaction_ref, growth_ref, state_hbm, out_hbm, wh_hbm, wl_hbm, nb_hbm,
         x_ref, state_ref, out_ref, wh_ref, wl_ref, nb_ref, sun_ref, sea_buf, bottom_buf, sun2, heat2, sems, wins, kept) = refs
        finish = cut_depths(sea_hbm, bottom_hbm, nb_ref, sea_buf, bottom_buf, wins)
        load_block(x_hbm, x_ref, sems)

        def turn(c, carry):
            for y in range(TY):
                put(state_ref, (c, y), [x_ref[h, c, pl.ds(y, NZ, stride=TY), :] for h in range(2)])
            pltpu.make_async_copy(state_ref.at[c], state_hbm.at[c], kept.at[0]).start()
            return carry

        lax.fori_loop(0, NC, turn, 0)
        finish()
        pltpu.make_async_copy(nb_ref, nb_hbm, kept.at[4]).start()
    else:
        state_ref, sun_ref, wh_ref, wl_ref, out_ref = refs

    @pl.when(lax.axis_index("section") > 0)
    def _():
        if build:
            shade(lambda h, k: x_ref[h, 2, TY * k : TY * k + TY, :], sun2, heat2)
            for y in range(TY):
                put(sun_ref, (y,), [sun2[h, NZ * y : NZ * y + NZ] for h in range(2)])
            build_weights(reaction_ref, growth_ref, wh_ref, wl_ref)

        def react(y, carry):
            q = state_ref[:, y]
            x = jnp.maximum(q, 0.0).reshape(NC * NZ, NX)
            x_high = x.astype(BF16)
            x_low = (x - x_high.astype(F32)).astype(BF16)
            total = jnp.dot(wh_ref[...], x_high, preferred_element_type=F32)
            total = total + jnp.dot(wh_ref[...], x_low, preferred_element_type=F32)
            total = total + jnp.dot(wl_ref[...], x_high, preferred_element_type=F32)
            nutrient = jnp.maximum(q[0], 0.0)
            uptake = DT * (nutrient / (nutrient + 0.5) * sun_ref[y])
            out_ref[:, y] = q + total.reshape(NC, NZ, NX) * uptake[None]
            if build:
                pltpu.make_async_copy(out_ref.at[:, y], out_hbm.at[:, y], kept.at[1]).start()
            return carry

        if build:
            weights = [pltpu.make_async_copy(wh_ref, wh_hbm, kept.at[2]), pltpu.make_async_copy(wl_ref, wl_hbm, kept.at[3])]
            for copy in weights:
                copy.start()
        lax.fori_loop(0, TY, react, 0)
        if build:
            for copy in weights:
                copy.wait()
            pltpu.make_async_copy(out_ref, out_hbm, kept.at[1]).wait()

    if build:
        pltpu.make_async_copy(state_ref, state_hbm, kept.at[0]).wait()
        pltpu.make_async_copy(nb_ref, nb_hbm, kept.at[4]).wait()


def rim_kernel(ends_ref, zu_ref, zd_ref, first_ref, second_ref, r1_ref, r2_ref, r3_ref):
    section, even, _ = place()

    @pl.when(section == 0)
    def _():
        def row(t, f, y):
            if y < 0:
                return zu_ref[f] if t == 0 else ends_ref[1, 3 * f + t - 1]
            return zd_ref[f] if t == 2 else ends_ref[0, 3 * f + t + 1]

        def fill(out, t):
            for n, y in ((0, -1), (4, TY)):
                out[n] = row(t, 0, y)
                out[n + 1] = row(t, 1, y)
                out[n + 2] = 0.8 * row(t, 3, y) - 0.2 * row(t, 2, y)
                out[n + 3] = row(t, 4, y)
            for g in range(2):
                half = slice(g * 128, g * 128 + 128)
                west, east = by_parity(first_ref[:, half], second_ref[:, half])
                out[8, :, half] = west + pltpu.roll(east, 16, 1)

        fill(r2_ref, 1)

        @pl.when(even)
        def _():
            fill(r1_ref, 0)
            fill(r3_ref, 2)

        @pl.when(jnp.logical_not(even))
        def _():
            fill(r1_ref, 2)
            fill(r3_ref, 0)


def wet(nb_ref, shift, y):
    k = levels()
    row = nb_ref[shift, pl.ds(y + 8, 1), :]
    return tuple(jnp.where(k < row[:, h * 128 : h * 128 + 128], 1.0, 0.0) for h in range(2))


def east_of(pair, edge, last):
    a, b = (pltpu.roll(v, 127, 1) for v in pair)
    return jnp.where(last, b, a), jnp.where(last, edge, b)


def west_of(pair, edge, first):
    a, b = (pltpu.roll(v, 1, 1) for v in pair)
    return jnp.where(first, edge, a), jnp.where(first, a, b)


def level_down(v):
    return pltpu.roll(v, NZ - 1, 0)


def flow_update(get, edge, nb_ref, y, names):
    lane = lanes()
    first, last = lane == 0, lane == 127
    centre, east, west = (wet(nb_ref, s, y) for s in range(3))
    north, south = wet(nb_ref, 0, y + 1), wet(nb_ref, 0, y - 1)
    here = {f: get(f, y) for f in names}
    around = {}
    for f in names:
        if f == "E":
            continue
        around[f] = (
            east_of(here[f], edge(f, y, 1), last),
            west_of(here[f], edge(f, y, 0), first),
            get(f, y + 1),
            get(f, y - 1),
        )
    out = {f: [] for f in names}
    for h in range(2):
        m = centre[h]
        sides = (east[h], west[h], north[h], south[h])

        def lap(f):
            c = here[f][h]
            total = 0.0
            for w, v in zip(sides, around[f]):
                total = total + w * (v[h] - c)
            return m * total

        u, v, e = here["U"][h], here["V"][h], here["E"][h]
        if "T" in names:
            rho = 0.8 * here["S"][h] - 0.2 * here["T"][h]
            near = [0.8 * s[h] - 0.2 * t[h] for s, t in zip(around["S"], around["T"])]
        else:
            rho = here["rho"][h]
            near = [r[h] for r in around["rho"]]
        grad_x = 0.5 * (sides[0] * (near[0] - rho) + sides[1] * (rho - near[1]))
        grad_y = 0.5 * (sides[2] * (near[2] - rho) + sides[3] * (rho - near[3]))
        out["U"].append(m * (u + DT * (0.5 * v - 0.5 * grad_x + 0.15 * lap("U") - 0.1 * u)))
        out["V"].append(m * (v + DT * (-0.5 * u - 0.5 * grad_y + 0.15 * lap("V") - 0.1 * v)))
        inner = jnp.where(levels() < NZ - 1.0, 1.0, 0.0)
        open_below = m * level_down(m) * inner
        du, dv = level_down(u) - u, level_down(v) - v
        shear = (du * du + dv * dv) * open_below
        out["E"].append(m * (e + DT * (0.5 * shear - 0.5 * e)))
        if "T" in names:
            out["T"].append(here["T"][h] * m + m * (DT * (0.15 * lap("T"))))
            out["S"].append(m * (here["S"][h] + DT * (0.15 * lap("S"))))
    return out


def put(ref, index, pair):
    ref[index + (slice(None), slice(0, 128))] = pair[0]
    ref[index + (slice(None), slice(128, 256))] = pair[1]


def column_edges(right_in, left_in):
    slot = {"U": 0, "V": 1, "T": 2, "S": 3, "E": 4}

    def edge(name, y, side, third):
        if name == "rho":
            return 0.8 * edge("S", y, side, third) - 0.2 * edge("T", y, side, third)
        ref = (right_in, left_in)[side]
        spot = 32 * lax.rem(y, 4) + 3 * slot[name] + third
        target = 0 if side == 0 else 127
        return pltpu.roll(ref[lax.div(y, 4)], lax.rem(target - spot + 256, 128), 1)

    return edge


def step_kernel(first_step, *refs):
    if first_step:
        (state_hbm, racc_hbm, recv_hbm, zu_hbm, zd_hbm, ou_hbm, od_hbm, first_hbm, second_hbm, rim1, rim2, rim3, nb_hbm, mine_a_hbm, mine_b_hbm,
         out_ref, up_ref, down_ref, first_out, second_out, heat_ref, sun_out, flow_out,
         state_ref, racc, inflow, lowq, highq, rim, nb_ref, first_in, second_in, mine_a, mine_b,
         fx, wx, dx, wy, dy, dz, mm, cin, sun2, heat2, green, sems, bands) = refs
    else:
        (state_ref, racc, zu_ref, zd_ref, first_in, second_in, heat1, heat2_in, heat3, nb_ref, mine_a, mine_b, flow_ref,
         out_hbm,
         fx, wx, dx, wy, dy, dz, mm, cin, out_ref, sems) = refs
        lowq, highq = zu_ref, zd_ref
    section, even, third = place()
    lane = lanes()
    first, last = lane == 0, lane == 127

    def leave(c, h):
        return pltpu.make_async_copy(out_ref.at[h, c], out_hbm.at[c, :, pl.ds(128 * h, 128)], sems.at[h])

    def copy_rows(n, target, source):
        def body(i, carry):
            target(i)[...] = source(i)[...]
            return carry

        lax.fori_loop(0, n, body, 0)

    if first_step:
        def fetch(source, target, sem):
            copy = pltpu.make_async_copy(source, target, sem)
            copy.start()
            return copy

        small = [
            fetch(source, target, sems.at[i])
            for i, (source, target) in enumerate(
                ((nb_hbm, nb_ref), (first_hbm, first_in), (second_hbm, second_in), (mine_a_hbm, mine_a), (mine_b_hbm, mine_b))
            )
        ]

        @pl.when(section == 0)
        def _():
            for t in range(3):
                fetch(recv_hbm.at[jnp.where(even, t + 1, 3 - t), pl.ds(0, 4)], inflow.at[pl.ds(4 * t, 4)], sems.at[5])
            fetch(ou_hbm, rim.at[pl.ds(0, 5)], sems.at[6])
            fetch(od_hbm, lowq.at[pl.ds(0, 5), 0], sems.at[7])

        @pl.when(section > 0)
        def _():
            fetch(recv_hbm.at[0], inflow, sems.at[5])
            for s, source in ((1, rim1), (2, rim2), (3, rim3)):
                @pl.when(section == s)
                def _():
                    fetch(source, rim, sems.at[8])
            below = jnp.where(even, section - 1, section + 1)
            above = jnp.where(even, section + 1, section - 1)
            for z, index, dest, sem in ((zu_hbm, below, lowq, 6), (zd_hbm, above, highq, 7)):
                end = (index < 1) | (index > 3)

                @pl.when(end)
                def _():
                    fetch(z.at[pl.ds(0, NC)], dest, sems.at[sem])

                @pl.when(jnp.logical_not(end))
                def _():
                    fetch(recv_hbm.at[jnp.clip(index, 0, 3), pl.ds(0, NC)], dest, sems.at[sem])

        def band(c):
            return (
                lambda: pltpu.make_async_copy(state_hbm.at[c], state_ref.at[c], bands.at[0, c]),
                lambda: pltpu.make_async_copy(racc_hbm.at[c], racc.at[c], bands.at[1, c]),
            )

        for c in range(NC):
            band(c)[0]().start()

            @pl.when(section > 0)
            def _():
                band(c)[1]().start()

        for copy in small:
            copy.wait()

    for g in range(2):
        half = slice(g * 128, g * 128 + 128)
        cin[0, g], cin[1, g] = by_parity(first_in[:, half], second_in[:, half])
    edges = column_edges(cin.at[0], cin.at[1])

    @pl.when(section == 0)
    def _():
        if first_step:
            pltpu.make_async_copy(recv_hbm.at[0, pl.ds(0, 12)], inflow.at[pl.ds(0, 12)], sems.at[5]).wait()
            pltpu.make_async_copy(ou_hbm, rim.at[pl.ds(0, 5)], sems.at[6]).wait()
            pltpu.make_async_copy(od_hbm, lowq.at[pl.ds(0, 5), 0], sems.at[7]).wait()
            for c in range(NC):
                band(c)[0]().wait()
        for f in range(5):
            fx[f, 0] = rim[f] if first_step else zu_ref[f, 0]
            fx[f, 25] = lowq[f, 0] if first_step else zd_ref[f, 0]
            for t in range(3):
                copy_rows(TY, lambda i: fx.at[f, 1 + TY * t + i], lambda i: state_ref.at[3 * f + t, i])
        names = ("U", "V", "T", "S", "E")

        def get(f, y):
            return halves(fx[names.index(f), y + 1])

        for t in range(3):
            def body(y, carry):
                r = TY * t + y
                out = flow_update(get, lambda f, row, side: edges(f, y, side, t), nb_ref, r, names)
                if first_step:
                    heat = inflow[4 * t + lax.div(y, 2), lax.rem(y, 2)]
                else:
                    ends = jnp.where(even, heat1[y], heat3[y]) if t == 0 else jnp.where(even, heat3[y], heat1[y])
                    heat = heat2_in[y] if t == 1 else ends
                m = wet(nb_ref, 0, r)
                warm = halves(heat)
                out["T"] = [out["T"][h] + m[h] * (DT * 3.0 * warm[h]) for h in range(2)]
                for f, name in enumerate(names):
                    if first_step:
                        put(out_ref, (3 * f + t, y), out[name])
                    else:
                        for h in range(2):
                            out_ref[h, 3 * f + t, pl.ds(y, NZ, stride=TY), :] = out[name][h]
                return carry

            lax.fori_loop(0, TY, body, 0)
            if not first_step:
                for f in range(5):
                    for h in range(2):
                        leave(3 * f + t, h).start()
        if first_step:
            for f in range(5):
                up_ref[f, 0] = out_ref[3 * f + 2, TY - 1]
                down_ref[f, 0] = out_ref[3 * f, 0]

    @pl.when(section > 0)
    def _():
        if first_step:
            pltpu.make_async_copy(recv_hbm.at[0], inflow, sems.at[5]).wait()
            pltpu.make_async_copy(rim1, rim, sems.at[8]).wait()
            for f in range(4):
                copy_rows(TY, lambda i: fx.at[f, 1 + i], lambda i: inflow.at[4 * f + lax.div(i, 2), lax.rem(i, 2)])
                fx[f, 0] = rim[f]
                fx[f, TY + 1] = rim[4 + f]
            for g in range(2):
                ends = rim[8, :, g * 128 : g * 128 + 128]
                cin[2, g] = ends
                cin[3, g] = pltpu.roll(ends, 112, 1)
            for y in range(TY + 2):
                fx[4, y] = 0.05 + 0.15 * fx[3, y]
        else:
            for f, place_of in enumerate((0, 1, 4)):
                copy_rows(TY, lambda i: fx.at[place_of, 1 + i], lambda i: flow_ref.at[f, i])
            fx[1, 0] = zu_ref[NC, 0]
            fx[4, 0] = zu_ref[NC, 1]
            fx[4, TY + 1] = zd_ref[NC, 1]
        flow_edges = column_edges(cin.at[2], cin.at[3])
        fields = {"U": 0, "V": 1, "rho": 2, "E": 3, "K": 4}

        def get(f, y):
            return halves(fx[fields[f], y + 1])

        def spread_lane(ref, side, y, spot):
            v = ref[side, y // 4]
            return jnp.broadcast_to(v[:, spot : spot + 1], (NZ, 128))

        edge_w = [jnp.zeros((NZ, 128), F32)] * 2
        edge_d = [jnp.zeros((NZ, 128), F32)] * 2
        k_index = levels()
        east_k = []
        if first_step:
            turned = [[pltpu.roll(cin[2 + side, g], lax.rem(128 - third, 128), 1) for g in range(2)] for side in range(2)]
        for y in range(TY):
            g, base = y // 4, 32 * (y % 4)
            if first_step:
                def column(side, slot):
                    v = turned[side][g]
                    return jnp.broadcast_to(v[:, base + 3 * slot : base + 3 * slot + 1], (NZ, 128))

                u_west = column(0, 0)
                k_west = 0.05 + 0.15 * column(0, 4)
                k_east = 0.05 + 0.15 * column(1, 4)
            else:
                u_west = spread_lane(cin, 0, y, base + 30)
                k_west = spread_lane(cin, 0, y, base + 31)
                k_east = spread_lane(cin, 1, y, base + 31)
            east_k.append(k_east)
            k_here = jnp.broadcast_to(fx[4, y + 1, :, 0:1], (NZ, 128))
            m_here = jnp.where(k_index < nb_ref[0, y + 8 : y + 9, 0:1], 1.0, 0.0)
            m_west = jnp.where(k_index < nb_ref[2, y + 8 : y + 9, 0:1], 1.0, 0.0)
            both = m_here * m_west
            group = (lane >= base) & (lane < base + 32)
            edge_w[g] = jnp.where(group, DT * both * u_west, edge_w[g])
            edge_d[g] = jnp.where(group, DT * both * (k_west + k_here), edge_d[g])
        packed = []
        for g in range(2):
            half = slice(g * 128, g * 128 + 128)
            q_1 = cin[0, g]
            q_2 = pltpu.roll(q_1, 1, 1)
            q255, q1 = by_parity(mine_b[:, half], mine_a[:, half])
            q0 = pltpu.roll(q1, 1, 1)
            d_2, d_1, d0 = 0.5 * (q_1 - q_2), 0.5 * (q0 - q_1), 0.5 * (q1 - q0)
            h_1, h0 = minmod(d_1, d_2), minmod(d0, d_1)
            w = edge_w[g]
            flux = w * jnp.where(w > 0, q_1 + h_1, q0 - h0) - edge_d[g] * d_1
            q257 = cin[1, g]
            q256 = pltpu.roll(q257, 1, 1)
            high_east = q256 - minmod(0.5 * (q257 - q256), 0.5 * (q256 - q255))
            packed.append((d_1, flux, 0.5 * q256, high_east))
        for g in range(2):
            for n in range(4):
                cin[4 + n, g] = packed[g][n]

        for y in range(-1, TY):
            m, m_n = wet(nb_ref, 0, y), wet(nb_ref, 0, y + 1)
            v, k, k_n = get("V", y), get("K", y), get("K", y + 1)
            both = [m[h] * m_n[h] for h in range(2)]
            put(wy, (y + 1,), [DT * both[h] * v[h] for h in range(2)])
            put(dy, (y + 1,), [DT * both[h] * (k[h] + k_n[h]) for h in range(2)])
            if y < 0:
                continue
            m_e = wet(nb_ref, 1, y)
            both = [m[h] * m_e[h] for h in range(2)]
            u = get("U", y)
            k_e = east_of(k, east_k[y], last)
            put(wx, (y,), [DT * both[h] * u[h] for h in range(2)])
            put(dx, (y,), [DT * both[h] * (k[h] + k_e[h]) for h in range(2)])
            inner = jnp.where(k_index < NZ - 1.0, 0.5 * DT, 0.0)
            put(dz, (y,), [inner * (m[h] * level_down(m[h])) * (k[h] + level_down(k[h])) for h in range(2)])
            put(mm, (y,), m)

        if first_step:
            pltpu.make_async_copy(zu_hbm.at[pl.ds(0, NC)], lowq, sems.at[6]).wait()
            pltpu.make_async_copy(zd_hbm.at[pl.ds(0, NC)], highq, sems.at[7]).wait()

        def tracer(c, carry):
            if first_step:
                for copy in band(c):
                    copy().wait()
            q = {y: halves(state_ref[c, y]) for y in range(TY)}
            q.update({y - 2: halves(lowq[c, y]) for y in range(2)})
            q.update({y + TY: halves(highq[c, y]) for y in range(2)})
            p = {y: [0.5 * v for v in q[y]] for y in q}
            d = {y: [p[y + 1][h] - p[y][h] for h in range(2)] for y in range(-2, TY + 1)}
            s = {y: [minmod(d[y][h], d[y - 1][h]) for h in range(2)] for y in range(-1, TY + 1)}
            north = {}
            for y in range(-1, TY):
                w, f = halves(wy[y + 1]), halves(dy[y + 1])
                north[y] = [
                    w[h] * jnp.where(w[h] > 0, q[y][h] + s[y][h], q[y + 1][h] - s[y + 1][h]) - f[h] * d[y][h]
                    for h in range(2)
                ]
            for y in range(TY):
                g, spot = y // 4, 32 * (y % 4) + 2 * c
                to_first, to_last = 127 - spot, 126 - spot
                p_e = east_of(p[y], pltpu.roll(cin[6, g], to_last, 1), last)
                dxx = [p_e[h] - p[y][h] for h in range(2)]
                d_w = west_of(dxx, pltpu.roll(cin[4, g], to_first, 1), first)
                slope = [minmod(dxx[h], d_w[h]) for h in range(2)]
                low = [q[y][h] + slope[h] for h in range(2)]
                high = [q[y][h] - slope[h] for h in range(2)]
                high_e = east_of(high, pltpu.roll(cin[7, g], to_last, 1), last)
                w, f = halves(wx[y]), halves(dx[y])
                flux = [w[h] * jnp.where(w[h] > 0, low[h], high_e[h]) - f[h] * dxx[h] for h in range(2)]
                flux_w = west_of(flux, pltpu.roll(cin[5, g], to_first, 1), first)
                base, z, m = halves(racc[c, y]), halves(dz[y]), halves(mm[y])
                new = []
                for h in range(2):
                    down = z[h] * (level_down(q[y][h]) - q[y][h])
                    vert = down - pltpu.roll(down, 1, 0)
                    new.append(m[h] * (base[h] + (flux_w[h] - flux[h]) + (north[y - 1][h] - north[y][h]) + vert))
                if first_step:
                    put(out_ref, (c, y), new)
                else:
                    for h in range(2):
                        out_ref[h, c, pl.ds(y, NZ, stride=TY), :] = new[h]
            if not first_step:
                for h in range(2):
                    leave(c, h).start()
            return carry

        lax.fori_loop(0, NC, tracer, 0)

        if first_step:
            def flow(y, carry):
                out = flow_update(get, lambda f, row, side: flow_edges(f, y, side, third), nb_ref, y, ("U", "V", "rho", "E")[:2] + ("rho", "E"))
                put(flow_out, (0, y), out["U"])
                put(flow_out, (1, y), out["V"])
                put(flow_out, (2, y), [0.05 + 0.15 * e for e in out["E"]])
                return carry

            lax.fori_loop(0, TY, flow, 0)

            def edge_rows(c, carry):
                for j in range(2):
                    up_ref[c, j] = out_ref[c, TY - 2 + j]
                    down_ref[c, j] = out_ref[c, j]
                return carry

            lax.fori_loop(0, NC, edge_rows, 0)
            up_ref[NC, 0] = flow_out[1, TY - 1]
            up_ref[NC, 1] = flow_out[2, TY - 1]
            down_ref[NC, 1] = flow_out[2, 0]
            for y in range(TY):
                for h in range(2):
                    green[h, NZ * y : NZ * y + NZ, :] = out_ref[2, y, :, h * 128 : h * 128 + 128]
            shade(lambda h, k: green[h, pl.ds(k, TY, stride=NZ), :], sun2, heat2)
            for y in range(TY):
                rows = slice(NZ * y, NZ * y + NZ)
                put(sun_out, (y,), [sun2[h, rows] for h in range(2)])
                put(heat_ref, (y,), [heat2[h, rows] for h in range(2)])

    if not first_step:
        for h in range(2):
            leave(slice(None), h).wait()
    if first_step:
        per = jnp.where(section == 0, 1, 2)
        packs = list(pack_columns(lambda c, y: halves(out_ref[c, y]), per))

        @pl.when(section == 0)
        def _():
            give_columns(packs, first_out, second_out)

        @pl.when(section > 0)
        def _():
            tiles = list(packs)
            for y in range(TY):
                g, base = y // 4, 32 * (y % 4)
                k0 = jnp.broadcast_to(flow_out[2, y, :, 0:1], (NZ, 128))
                u255 = jnp.broadcast_to(flow_out[0, y, :, 255:256], (NZ, 128))
                k255 = jnp.broadcast_to(flow_out[2, y, :, 255:256], (NZ, 128))
                tiles[g] = jnp.where(lane == base + 31, k0, tiles[g])
                tiles[2 + g] = jnp.where(lane == base + 30, u255, tiles[2 + g])
                tiles[2 + g] = jnp.where(lane == base + 31, k255, tiles[2 + g])
            give_columns(tiles, first_out, second_out)


def sds(*shape):
    return jax.ShapeDtypeStruct(shape, F32)


def vmem(n):
    return [pl.BlockSpec(memory_space=pltpu.VMEM)] * n


def step_scratch(first_step):
    row = (NZ, NX)
    scratch = []
    if first_step:
        scratch = [pltpu.VMEM((NC, TY) + row, F32)] * 2 + [pltpu.VMEM((16, 2) + row, F32)]
        scratch += [pltpu.VMEM((NC, 2) + row, F32)] * 2
        scratch += [pltpu.VMEM((9,) + row, F32), pltpu.VMEM((3, 40, NX), F32)] + [pltpu.VMEM(row, F32)] * 4
    scratch += [
        pltpu.VMEM((5, 26) + row, F32),
        pltpu.VMEM((TY,) + row, F32),
        pltpu.VMEM((TY,) + row, F32),
        pltpu.VMEM((TY + 1,) + row, F32),
        pltpu.VMEM((TY + 1,) + row, F32),
        pltpu.VMEM((TY,) + row, F32),
        pltpu.VMEM((TY,) + row, F32),
        pltpu.VMEM((8, 2, NZ, 128), F32),
    ]
    if first_step:
        scratch += [pltpu.VMEM((2, TY * NZ, 128), F32)] * 3
        return scratch + [pltpu.SemaphoreType.DMA((9,)), pltpu.SemaphoreType.DMA((2, NC))]
    return scratch + [pltpu.VMEM((2, NC, NZ * TY, 128), F32), pltpu.SemaphoreType.DMA((2,))]


def pairs_of(mesh):
    ns, ngy, ngx = (mesh.shape[a] for a in AXES)

    def at(s, g, x):
        return (s * ngy + g) * ngx + x

    cross, ocean, inside, swaps, heat = [], [], [], ([], []), {1: [], 2: [], 3: []}
    for x in range(ngx):
        for g in range(ngy):
            order = (1, 2, 3) if g % 2 == 0 else (3, 2, 1)
            inside += [(at(a, g, x), at(b, g, x)) for a, b in zip(order, order[1:])]
            if g + 1 < ngy:
                cross.append((at(order[2], g, x), at(order[2], g + 1, x)))
                ocean.append((at(0, g, x), at(0, g + 1, x)))
            for s in heat:
                heat[s].append((at(s, g, x), at(0, g, x)))
            if x + 1 < ngx:
                swaps[x % 2].extend((at(s, g, x), at(s, g, x + 1)) for s in range(ns))
    return cross, ocean, inside + cross + ocean, [p + turn(p) for p in swaps], heat


def turn(pairs):
    return [(b, a) for a, b in pairs]


def solution(mesh):
    cross, ocean, chain, swaps, heat_pairs = pairs_of(mesh)

    def send(value, pairs):
        return lax.ppermute(value, AXES, pairs)

    def program(fields, sea_mask, bottom, reaction, growth):
        x = fields.reshape(NC, NZ * TY, NX)
        row = (NZ, NX)
        block = sds(NC, TY, *row)
        halo = sds(16, 2, *row)
        anywhere = pl.BlockSpec(memory_space=pltpu.HBM)
        weights = jax.ShapeDtypeStruct((NC * NZ, NC * NZ), BF16)

        def call(body, out_shape, in_specs, out_specs, scratch=(), cost=None):
            def placed(shape, spec):
                return pltpu.HBM(shape.shape, shape.dtype) if spec is anywhere else shape

            if isinstance(out_specs, tuple):
                out_shape = tuple(placed(*pair) for pair in zip(out_shape, out_specs))
            kernel = pl.pallas_call(
                body,
                out_shape=out_shape,
                in_specs=in_specs,
                out_specs=out_specs,
                scratch_shapes=list(scratch),
                compiler_params=pltpu.CompilerParams(vmem_limit_bytes=VMEM_LIMIT),
                cost_estimate=cost,
            )

            def run(*operands):
                return kernel(*[
                    pltpu.with_memory_space_constraint(v, pltpu.HBM) if spec is anywhere else v
                    for v, spec in zip(operands, in_specs)
                ])

            return run

        x_scratch = pltpu.VMEM((2, NC, NZ * TY, 128), F32)
        rows = pltpu.VMEM((2, TY * NZ, 128), F32)
        a_out, zu, zd, ou, od = call(
            send_kernel, (sds(4, 16, 2, *row), halo, halo, sds(5, *row), sds(5, *row)), [anywhere],
            (anywhere,) * 3 + tuple(vmem(2)),
            [x_scratch, pltpu.VMEM((16, 2) + row, F32), pltpu.VMEM((16, 2) + row, F32), pltpu.VMEM((3, 16, 2) + row, F32),
             rows, rows, pltpu.SemaphoreType.DMA((5,))],
        )(x)
        recv = lax.all_to_all(a_out, "section", split_axis=0, concat_axis=0, tiled=True)
        ou_in, od_in = send(ou, ocean), send(od, turn(ocean))
        mine_a, mine_b, ends = call(
            column_kernel, (sds(*row), sds(*row), sds(2, NC, *row)), [anywhere], tuple(vmem(3)),
            [x_scratch, pltpu.SemaphoreType.DMA((2,))],
        )(x)
        first_in, second_in = send(mine_a, swaps[0]), send(mine_b, swaps[1])
        zu_in, zd_in = send(zu, cross), send(zd, turn(cross))
        rims = call(rim_kernel, tuple([sds(9, *row)] * 3), vmem(5), tuple(vmem(3)))(ends, ou_in, od_in, first_in, second_in)
        rims = [send(r, turn(heat_pairs[s])) for s, r in zip((1, 2, 3), rims)]
        react_cost = pl.CostEstimate(flops=6 * 240 * 240 * 2048, bytes_accessed=2 * NC * TY * NZ * NX * 4, transcendentals=0)
        window = pltpu.VMEM((5, TY, 512), jnp.int32)
        whole = pltpu.VMEM((NC, TY) + row, F32)
        square = pltpu.VMEM((NC * NZ, NC * NZ), BF16)
        state, grown, w_high, w_low, nb = call(
            functools.partial(react_kernel, True), (block, block, weights, weights, sds(3, 40, NX)),
            [anywhere] * 3 + vmem(2), (anywhere,) * 5,
            [x_scratch, whole, whole, square, square, pltpu.VMEM((3, 40, NX), F32), pltpu.VMEM((TY,) + row, F32), window, window,
             rows, rows, pltpu.SemaphoreType.DMA((2,)), pltpu.SemaphoreType.DMA((2, 5, 3)), pltpu.SemaphoreType.DMA((5,))],
            cost=react_cost,
        )(x, sea_mask, bottom, reaction, growth.reshape(1, NC))
        state1, up, down, next_a, next_b, heat1, sun1, flow1 = call(
            functools.partial(step_kernel, True),
            (block, halo, halo, sds(*row), sds(*row), sds(TY, *row), sds(TY, *row), sds(3, TY, *row)),
            [anywhere] * 15, tuple(vmem(8)), step_scratch(True),
        )(state, grown, recv, zu_in, zd_in, ou_in, od_in, first_in, second_in, *rims, nb, mine_a, mine_b)
        up_in, down_in = send(up, chain), send(down, turn(chain))
        first1_in, second1_in = send(next_a, swaps[0]), send(next_b, swaps[1])
        heats = [send(heat1, heat_pairs[s]) for s in (1, 2, 3)]
        grown1 = call(
            functools.partial(react_kernel, False), block, vmem(4), vmem(1)[0], cost=react_cost,
        )(state1, sun1, w_high, w_low)
        out = call(
            functools.partial(step_kernel, False), sds(NC, NZ * TY, NX), vmem(13), anywhere, step_scratch(False),
        )(state1, grown1, up_in, down_in, first1_in, second1_in, *heats, nb, next_a, next_b, flow1)
        return out.reshape(1, NC, NZ, TY, NX)

    return jax.shard_map(
        program,
        mesh=mesh,
        in_specs=(P("section", None, None, "gy", "gx"), P(), P(), P(), P()),
        out_specs=P("section", None, None, "gy", "gx"),
        check_vma=False,
    )
```

```python
import functools

import jax
import jax.numpy as jnp
from jax import lax
from jax.experimental import pallas as pl
from jax.experimental.pallas import tpu as pltpu
from jax.sharding import PartitionSpec as P


AXES = ("section", "gy", "gx")
NC, NZ, TY, NX = 15, 16, 8, 256
DT = 0.2
F32 = jnp.float32
BF16 = jnp.bfloat16
VMEM_LIMIT = 24 * 1024 * 1024


def minmod(a, b):
    return jnp.maximum(jnp.minimum(a, b), jnp.minimum(jnp.maximum(a, b), 0.0))


def lanes():
    return lax.broadcasted_iota(jnp.int32, (NZ, 128), 1)


def levels():
    return lax.broadcasted_iota(jnp.int32, (NZ, 128), 0).astype(F32)


def halves(row):
    return row[:, :128], row[:, 128:]


def place():
    section = lax.axis_index("section")
    tile = lax.axis_index("gy")
    even = tile % 2 == 0
    third = jnp.where(even, section - 1, 3 - section)
    return section, even, third


def shade(read, sun_ref, heat_ref):
    for h in range(2):
        depth = jnp.zeros((TY, 128), F32)
        for k in range(NZ):
            chlorophyll = jnp.maximum(read(h, k), 0.0)
            sunlight = jnp.exp(-depth)
            depth = depth + (0.05 + 0.1 * chlorophyll)
            sun_ref[h, pl.ds(k, TY, stride=NZ), :] = sunlight
            heat_ref[h, pl.ds(k, TY, stride=NZ), :] = 0.1 * chlorophyll * sunlight


def pack_columns(read, per):
    lane = lanes()

    def body(c, packs):
        packs = list(packs)
        for y in range(TY):
            left, right = read(c, y)
            spot = 32 * (y % 4) + per * c
            here = (lane >= spot) & (lane < spot + per)
            g = y // 4
            packs[g] = jnp.where(here, pltpu.roll(left, spot, 1), packs[g])
            packs[2 + g] = jnp.where(here, pltpu.roll(right, lax.rem(spot + per, 128), 1), packs[2 + g])
        return tuple(packs)

    zero = jnp.zeros((NZ, 128), F32)
    return lax.fori_loop(0, NC, body, (zero,) * 4)


def load_block(x_hbm, x_ref, sems):
    loads = [
        pltpu.make_async_copy(x_hbm.at[:, :, pl.ds(128 * h, 128)], x_ref.at[h], sems.at[h]) for h in range(2)
    ]
    for load in loads:
        load.start()
    for load in loads:
        load.wait()


def send_kernel(x_hbm, a_hbm, z_hbm, oa_ref, ob_ref, x_ref, top_ref, base_ref, flow_ref, sun2, heat2, sems):
    section, even, third = place()
    is_ocean = section == 0
    odd = chain_odd()
    load_block(x_hbm, x_ref, sems)

    def turned(c, y):
        return [x_ref[h, c, pl.ds(y, NZ, stride=TY), :] for h in range(2)]

    @pl.when(is_ocean)
    def _():
        for f in range(5):
            top, base = turned(3 * f + 2, TY - 1), turned(3 * f, 0)
            put(oa_ref, (f,), [jnp.where(odd, b, a) for a, b in zip(top, base)])
            put(ob_ref, (f,), [jnp.where(odd, a, b) for a, b in zip(top, base)])
        for t in range(3):
            def body(y, carry):
                i, j = lax.div(y, 2), lax.rem(y, 2)
                salt, warm = turned(9 + t, y), turned(6 + t, y)
                put(flow_ref, (t, i, j), turned(t, y))
                put(flow_ref, (t, 4 + i, j), turned(3 + t, y))
                put(flow_ref, (t, 8 + i, j), [0.8 * salt[h] - 0.2 * warm[h] for h in range(2)])
                put(flow_ref, (t, 12 + i, j), turned(12 + t, y))
                return carry

            lax.fori_loop(0, TY, body, 0)
        outs = []
        for t in range(3):
            target = jnp.where(even, t + 1, 3 - t)
            outs.append(pltpu.make_async_copy(flow_ref.at[t], a_hbm.at[target], sems.at[2 + t]))
        for out in outs:
            out.start()
        for out in outs:
            out.wait()

    @pl.when(jnp.logical_not(is_ocean))
    def _():
        above = jnp.where(even, section + 1, section - 1)
        below = jnp.where(even, section - 1, section + 1)
        above = jnp.where((above < 1) | (above > 3), section, above)
        below = jnp.where((below < 1) | (below > 3), section, below)

        def body(c, carry):
            for j in range(2):
                put(top_ref, (c, j), turned(c, TY - 2 + j))
                put(base_ref, (c, j), turned(c, j))
            return carry

        lax.fori_loop(0, NC, body, 0)
        outs = [
            pltpu.make_async_copy(top_ref, a_hbm.at[above], sems.at[0]),
            pltpu.make_async_copy(base_ref, a_hbm.at[below], sems.at[1]),
        ]
        for out in outs:
            out.start()

        @pl.when(third == 2)
        def _():
            pltpu.make_async_copy(top_ref, z_hbm, sems.at[2]).start()

        @pl.when(third == 0)
        def _():
            pltpu.make_async_copy(base_ref, z_hbm, sems.at[2]).start()

        shade(lambda h, k: x_ref[h, 2, TY * k : TY * k + TY, :], sun2, heat2)
        for y in range(TY):
            rows = slice(NZ * y, NZ * y + NZ)
            put(flow_ref, (0, y // 2, y % 2), [heat2[h, rows] for h in range(2)])
        warmth = pltpu.make_async_copy(flow_ref.at[0, pl.ds(0, 4)], a_hbm.at[0, pl.ds(0, 4)], sems.at[4])
        warmth.start()
        for out in outs:
            out.wait()
        warmth.wait()

        @pl.when(third != 1)
        def _():
            pltpu.make_async_copy(top_ref, z_hbm, sems.at[2]).wait()


def chain_odd():
    section, _, third = place()
    tile = lax.axis_index("gy")
    return lax.rem(jnp.where(section == 0, tile, 3 * tile + third), 2) == 1


def by_parity(first_in, second_in):
    odd = lax.rem(lax.axis_index("gx"), 2) == 1
    return jnp.where(odd, first_in, second_in), jnp.where(odd, second_in, first_in)


def give_columns(packs, first_ref, second_ref):
    odd = lax.rem(lax.axis_index("gx"), 2) == 1
    for g in range(2):
        half = slice(g * 128, g * 128 + 128)
        first_ref[:, half] = jnp.where(odd, packs[g], packs[2 + g])
        second_ref[:, half] = jnp.where(odd, packs[2 + g], packs[g])


def column_kernel(x_hbm, first_ref, second_ref, ends_ref, x_ref, sems):
    is_ocean = lax.axis_index("section") == 0
    load_block(x_hbm, x_ref, sems)

    def read(c, y):
        return [x_ref[h, c, pl.ds(y, NZ, stride=TY), :] for h in range(2)]

    give_columns(pack_columns(read, jnp.where(is_ocean, 1, 2)), first_ref, second_ref)

    @pl.when(is_ocean)
    def _():
        def body(c, carry):
            put(ends_ref, (0, c), read(c, 0))
            put(ends_ref, (1, c), read(c, TY - 1))
            return carry

        lax.fori_loop(0, NC, body, 0)


def cut_depths(sea_hbm, bottom_hbm, nb_ref, sea_buf, bottom_buf, wins):
    section, _, third = place()
    tile, column = lax.axis_index("gy"), lax.axis_index("gx")
    is_ocean = section == 0
    group = jnp.where(is_ocean, 3 * tile, 3 * tile + third)
    n_groups, n_cols = sea_hbm.shape[0] // TY, sea_hbm.shape[1]
    pieces = ((-128, 128), (0, 256), (256, 128))
    copies = []
    for n, (hbm, buf) in enumerate(((sea_hbm, sea_buf), (bottom_hbm, bottom_buf))):
        for g in range(5):
            row = pl.multiple_of(jnp.clip(group + g - 1, 0, n_groups - 1) * TY, TY)
            for i, (offset, width) in enumerate(pieces):
                col = pl.multiple_of(jnp.clip(column * NX + offset, 0, n_cols - width), 128)
                copies.append(
                    pltpu.make_async_copy(
                        hbm.at[pl.ds(row, TY), pl.ds(col, width)],
                        buf.at[g, :, pl.ds(offset + 128, width)],
                        wins.at[n, g, i],
                    )
                )
    for copy in copies:
        copy.start()

    def finish():
        for copy in copies:
            copy.wait()
        lane = lax.broadcasted_iota(jnp.int32, (TY, 128), 1)
        for g in range(5):
            inside = (group + g - 1 >= 0) & (group + g - 1 < n_groups)
            valid = (column > 0, True, True, column * NX + NX < n_cols)
            depth = []
            for i in range(4):
                part = slice(128 * i, 128 * i + 128)
                value = (sea_buf[g, :, part] * bottom_buf[g, :, part]).astype(F32)
                depth.append(jnp.where(inside & valid[i], value, 0.0))
            rows = slice(TY * g, TY * g + TY)
            for h in range(2):
                cols = slice(128 * h, 128 * h + 128)
                nb_ref[0, rows, cols] = depth[1 + h]
                nb_ref[1, rows, cols] = jnp.where(lane == 127, pltpu.roll(depth[2 + h], 127, 1), pltpu.roll(depth[1 + h], 127, 1))
                nb_ref[2, rows, cols] = jnp.where(lane == 0, pltpu.roll(depth[h], 1, 1), pltpu.roll(depth[1 + h], 1, 1))

    return finish


def build_weights(reaction_ref, growth_ref, wh_ref, wl_ref):
    size = NC * NZ
    matrix = reaction_ref[...] * growth_ref[...]
    level_of = lax.rem(lax.broadcasted_iota(jnp.int32, (size, size), 0), NZ)
    same = level_of == lax.rem(lax.broadcasted_iota(jnp.int32, (size, size), 1), NZ)
    up = lax.div(lax.broadcasted_iota(jnp.int32, (size, NC), 0), NZ) == lax.broadcasted_iota(jnp.int32, (size, NC), 1)
    across = lax.broadcasted_iota(jnp.int32, (NC, size), 0) == lax.div(lax.broadcasted_iota(jnp.int32, (NC, size), 1), NZ)
    up = jnp.where(up, 1.0, 0.0).astype(BF16)
    across = jnp.where(across, 1.0, 0.0).astype(BF16)
    high = matrix.astype(BF16)
    low = (matrix - high.astype(F32)).astype(BF16)
    for part, out in ((high, wh_ref), (low, wl_ref)):
        wide = jnp.dot(part, across, preferred_element_type=F32).astype(BF16)
        full = jnp.dot(up, wide, preferred_element_type=F32)
        out[...] = jnp.where(same, full, 0.0).astype(BF16)


def react_kernel(build, *refs):
    if build:
        (x_hbm, sea_hbm, bottom_hbm, reaction_ref, growth_ref, state_hbm, out_hbm, wh_hbm, wl_hbm, nb_hbm,
         x_ref, state_ref, out_ref, wh_ref, wl_ref, nb_ref, sun_ref, sea_buf, bottom_buf, sun2, heat2, sems, wins, kept) = refs
        finish = cut_depths(sea_hbm, bottom_hbm, nb_ref, sea_buf, bottom_buf, wins)
        load_block(x_hbm, x_ref, sems)

        def turn(c, carry):
            for y in range(TY):
                put(state_ref, (c, y), [x_ref[h, c, pl.ds(y, NZ, stride=TY), :] for h in range(2)])
            pltpu.make_async_copy(state_ref.at[c], state_hbm.at[c], kept.at[0]).start()
            return carry

        lax.fori_loop(0, NC, turn, 0)
        finish()
        pltpu.make_async_copy(nb_ref, nb_hbm, kept.at[4]).start()
    else:
        state_ref, sun_ref, wh_ref, wl_ref, out_ref = refs

    @pl.when(lax.axis_index("section") > 0)
    def _():
        if build:
            shade(lambda h, k: x_ref[h, 2, TY * k : TY * k + TY, :], sun2, heat2)
            for y in range(TY):
                put(sun_ref, (y,), [sun2[h, NZ * y : NZ * y + NZ] for h in range(2)])
            build_weights(reaction_ref, growth_ref, wh_ref, wl_ref)

        def react(y, carry):
            q = state_ref[:, y]
            x = jnp.maximum(q, 0.0).reshape(NC * NZ, NX)
            x_high = x.astype(BF16)
            x_low = (x - x_high.astype(F32)).astype(BF16)
            total = jnp.dot(wh_ref[...], x_high, preferred_element_type=F32)
            total = total + jnp.dot(wh_ref[...], x_low, preferred_element_type=F32)
            total = total + jnp.dot(wl_ref[...], x_high, preferred_element_type=F32)
            nutrient = jnp.maximum(q[0], 0.0)
            uptake = DT * (nutrient / (nutrient + 0.5) * sun_ref[y])
            out_ref[:, y] = q + total.reshape(NC, NZ, NX) * uptake[None]
            if build:
                pltpu.make_async_copy(out_ref.at[:, y], out_hbm.at[:, y], kept.at[1]).start()
            return carry

        if build:
            weights = [pltpu.make_async_copy(wh_ref, wh_hbm, kept.at[2]), pltpu.make_async_copy(wl_ref, wl_hbm, kept.at[3])]
            for copy in weights:
                copy.start()
        lax.fori_loop(0, TY, react, 0)
        if build:
            for copy in weights:
                copy.wait()
            pltpu.make_async_copy(out_ref, out_hbm, kept.at[1]).wait()

    if build:
        pltpu.make_async_copy(state_ref, state_hbm, kept.at[0]).wait()
        pltpu.make_async_copy(nb_ref, nb_hbm, kept.at[4]).wait()


def rim_kernel(ends_ref, oa_ref, ob_ref, first_ref, second_ref, r1_ref, r2_ref, r3_ref):
    section, even, _ = place()
    odd = chain_odd()

    @pl.when(section == 0)
    def _():
        def row(t, f, y):
            if y < 0:
                return jnp.where(odd, oa_ref[f], ob_ref[f]) if t == 0 else ends_ref[1, 3 * f + t - 1]
            return jnp.where(odd, ob_ref[f], oa_ref[f]) if t == 2 else ends_ref[0, 3 * f + t + 1]

        def fill(out, t):
            for n, y in ((0, -1), (4, TY)):
                out[n] = row(t, 0, y)
                out[n + 1] = row(t, 1, y)
                out[n + 2] = 0.8 * row(t, 3, y) - 0.2 * row(t, 2, y)
                out[n + 3] = row(t, 4, y)
            for g in range(2):
                half = slice(g * 128, g * 128 + 128)
                west, east = by_parity(first_ref[:, half], second_ref[:, half])
                out[8, :, half] = west + pltpu.roll(east, 16, 1)

        fill(r2_ref, 1)

        @pl.when(even)
        def _():
            fill(r1_ref, 0)
            fill(r3_ref, 2)

        @pl.when(jnp.logical_not(even))
        def _():
            fill(r1_ref, 2)
            fill(r3_ref, 0)


def wet(nb_ref, shift, y):
    k = levels()
    row = nb_ref[shift, pl.ds(y + 8, 1), :]
    return tuple(jnp.where(k < row[:, h * 128 : h * 128 + 128], 1.0, 0.0) for h in range(2))


def east_of(pair, edge, last):
    a, b = (pltpu.roll(v, 127, 1) for v in pair)
    return jnp.where(last, b, a), jnp.where(last, edge, b)


def west_of(pair, edge, first):
    a, b = (pltpu.roll(v, 1, 1) for v in pair)
    return jnp.where(first, edge, a), jnp.where(first, a, b)


def level_down(v):
    return pltpu.roll(v, NZ - 1, 0)


def flow_update(get, edge, nb_ref, y, names):
    lane = lanes()
    first, last = lane == 0, lane == 127
    centre, east, west = (wet(nb_ref, s, y) for s in range(3))
    north, south = wet(nb_ref, 0, y + 1), wet(nb_ref, 0, y - 1)
    here = {f: get(f, y) for f in names}
    around = {}
    for f in names:
        if f == "E":
            continue
        around[f] = (
            east_of(here[f], edge(f, y, 1), last),
            west_of(here[f], edge(f, y, 0), first),
            get(f, y + 1),
            get(f, y - 1),
        )
    out = {f: [] for f in names}
    for h in range(2):
        m = centre[h]
        sides = (east[h], west[h], north[h], south[h])

        def lap(f):
            c = here[f][h]
            total = 0.0
            for w, v in zip(sides, around[f]):
                total = total + w * (v[h] - c)
            return m * total

        u, v, e = here["U"][h], here["V"][h], here["E"][h]
        if "T" in names:
            rho = 0.8 * here["S"][h] - 0.2 * here["T"][h]
            near = [0.8 * s[h] - 0.2 * t[h] for s, t in zip(around["S"], around["T"])]
        else:
            rho = here["rho"][h]
            near = [r[h] for r in around["rho"]]
        grad_x = 0.5 * (sides[0] * (near[0] - rho) + sides[1] * (rho - near[1]))
        grad_y = 0.5 * (sides[2] * (near[2] - rho) + sides[3] * (rho - near[3]))
        out["U"].append(m * (u + DT * (0.5 * v - 0.5 * grad_x + 0.15 * lap("U") - 0.1 * u)))
        out["V"].append(m * (v + DT * (-0.5 * u - 0.5 * grad_y + 0.15 * lap("V") - 0.1 * v)))
        inner = jnp.where(levels() < NZ - 1.0, 1.0, 0.0)
        open_below = m * level_down(m) * inner
        du, dv = level_down(u) - u, level_down(v) - v
        shear = (du * du + dv * dv) * open_below
        out["E"].append(m * (e + DT * (0.5 * shear - 0.5 * e)))
        if "T" in names:
            out["T"].append(here["T"][h] * m + m * (DT * (0.15 * lap("T"))))
            out["S"].append(m * (here["S"][h] + DT * (0.15 * lap("S"))))
    return out


def put(ref, index, pair):
    ref[index + (slice(None), slice(0, 128))] = pair[0]
    ref[index + (slice(None), slice(128, 256))] = pair[1]


def column_edges(right_in, left_in):
    slot = {"U": 0, "V": 1, "T": 2, "S": 3, "E": 4}

    def edge(name, y, side, third):
        if name == "rho":
            return 0.8 * edge("S", y, side, third) - 0.2 * edge("T", y, side, third)
        ref = (right_in, left_in)[side]
        spot = 32 * lax.rem(y, 4) + 3 * slot[name] + third
        target = 0 if side == 0 else 127
        return pltpu.roll(ref[lax.div(y, 4)], lax.rem(target - spot + 256, 128), 1)

    return edge


def step_kernel(first_step, *refs):
    if first_step:
        (state_hbm, racc_hbm, recv_hbm, z_hbm, oa_hbm, ob_hbm, first_hbm, second_hbm, rim1, rim2, rim3, nb_hbm, mine_a_hbm, mine_b_hbm,
         out_ref, pair_a, pair_b, first_out, second_out, heat_ref, sun_out, flow_out,
         state_ref, racc, inflow, lowq, highq, rim, nb_ref, first_in, second_in, mine_a, mine_b,
         fx, wx, dx, wy, dy, dz, mm, cin, sun2, heat2, green, sems, bands) = refs
    else:
        (state_ref, racc, pair_a, pair_b, first_in, second_in, nb_ref, mine_a, mine_b, flow_ref,
         out_hbm,
         fx, wx, dx, wy, dy, dz, mm, cin, out_ref, sems) = refs
    section, even, third = place()
    odd = chain_odd()
    lane = lanes()
    first, last = lane == 0, lane == 127

    def leave(c, h):
        return pltpu.make_async_copy(out_ref.at[h, c], out_hbm.at[c, :, pl.ds(128 * h, 128)], sems.at[h])

    def copy_rows(n, target, source):
        def body(i, carry):
            target(i)[...] = source(i)[...]
            return carry

        lax.fori_loop(0, n, body, 0)

    if first_step:
        def fetch(source, target, sem):
            copy = pltpu.make_async_copy(source, target, sem)
            copy.start()
            return copy

        small = [
            fetch(source, target, sems.at[i])
            for i, (source, target) in enumerate(
                ((nb_hbm, nb_ref), (first_hbm, first_in), (second_hbm, second_in), (mine_a_hbm, mine_a), (mine_b_hbm, mine_b))
            )
        ]

        @pl.when(section == 0)
        def _():
            for t in range(3):
                fetch(recv_hbm.at[jnp.where(even, t + 1, 3 - t), pl.ds(0, 4)], inflow.at[pl.ds(4 * t, 4)], sems.at[5])
            fetch(oa_hbm, highq.at[pl.ds(0, 5), 0], sems.at[6])
            fetch(ob_hbm, lowq.at[pl.ds(0, 5), 0], sems.at[7])

        @pl.when(section > 0)
        def _():
            fetch(recv_hbm.at[0], inflow, sems.at[5])
            for s, source in ((1, rim1), (2, rim2), (3, rim3)):
                @pl.when(section == s)
                def _():
                    fetch(source, rim, sems.at[8])
            below = jnp.where(even, section - 1, section + 1)
            above = jnp.where(even, section + 1, section - 1)
            for index, dest, sem in ((below, lowq, 6), (above, highq, 7)):
                end = (index < 1) | (index > 3)

                @pl.when(end)
                def _():
                    fetch(z_hbm.at[pl.ds(0, NC)], dest, sems.at[sem])

                @pl.when(jnp.logical_not(end))
                def _():
                    fetch(recv_hbm.at[jnp.clip(index, 0, 3), pl.ds(0, NC)], dest, sems.at[sem])

        def band(c):
            return (
                lambda: pltpu.make_async_copy(state_hbm.at[c], state_ref.at[c], bands.at[0, c]),
                lambda: pltpu.make_async_copy(racc_hbm.at[c], racc.at[c], bands.at[1, c]),
            )

        for c in range(NC):
            band(c)[0]().start()

            @pl.when(section > 0)
            def _():
                band(c)[1]().start()

        for copy in small:
            copy.wait()

    for g in range(2):
        half = slice(g * 128, g * 128 + 128)
        cin[0, g], cin[1, g] = by_parity(first_in[:, half], second_in[:, half])
    edges = column_edges(cin.at[0], cin.at[1])

    @pl.when(section == 0)
    def _():
        if first_step:
            pltpu.make_async_copy(recv_hbm.at[0, pl.ds(0, 12)], inflow.at[pl.ds(0, 12)], sems.at[5]).wait()
            pltpu.make_async_copy(oa_hbm, highq.at[pl.ds(0, 5), 0], sems.at[6]).wait()
            pltpu.make_async_copy(ob_hbm, lowq.at[pl.ds(0, 5), 0], sems.at[7]).wait()
            for c in range(NC):
                band(c)[0]().wait()
        for f in range(5):
            from_a, from_b = (highq[f, 0], lowq[f, 0]) if first_step else (pair_a[f, 0], pair_b[f, 0])
            fx[f, 0] = jnp.where(odd, from_a, from_b)
            fx[f, 25] = jnp.where(odd, from_b, from_a)
            for t in range(3):
                copy_rows(TY, lambda i: fx.at[f, 1 + TY * t + i], lambda i: state_ref.at[3 * f + t, i])
        names = ("U", "V", "T", "S", "E")

        def get(f, y):
            return halves(fx[names.index(f), y + 1])

        for t in range(3):
            def body(y, carry):
                r = TY * t + y
                out = flow_update(get, lambda f, row, side: edges(f, y, side, t), nb_ref, r, names)
                if first_step:
                    m = wet(nb_ref, 0, r)
                    warm = halves(inflow[4 * t + lax.div(y, 2), lax.rem(y, 2)])
                    out["T"] = [out["T"][h] + m[h] * (DT * 3.0 * warm[h]) for h in range(2)]
                for f, name in enumerate(names):
                    if first_step:
                        put(out_ref, (3 * f + t, y), out[name])
                    else:
                        for h in range(2):
                            out_ref[h, 3 * f + t, pl.ds(y, NZ, stride=TY), :] = out[name][h]
                return carry

            lax.fori_loop(0, TY, body, 0)
            if not first_step:
                for f in range(5):
                    for h in range(2):
                        leave(3 * f + t, h).start()
        if first_step:
            for f in range(5):
                top, base = out_ref[3 * f + 2, TY - 1], out_ref[3 * f, 0]
                pair_a[f, 0] = jnp.where(odd, base, top)
                pair_b[f, 0] = jnp.where(odd, top, base)

    @pl.when(section > 0)
    def _():
        if first_step:
            pltpu.make_async_copy(recv_hbm.at[0], inflow, sems.at[5]).wait()
            pltpu.make_async_copy(rim1, rim, sems.at[8]).wait()
            for f in range(4):
                copy_rows(TY, lambda i: fx.at[f, 1 + i], lambda i: inflow.at[4 * f + lax.div(i, 2), lax.rem(i, 2)])
                fx[f, 0] = rim[f]
                fx[f, TY + 1] = rim[4 + f]
            for g in range(2):
                ends = rim[8, :, g * 128 : g * 128 + 128]
                cin[2, g] = ends
                cin[3, g] = pltpu.roll(ends, 112, 1)
            for y in range(TY + 2):
                fx[4, y] = 0.05 + 0.15 * fx[3, y]
        else:
            for f, place_of in enumerate((0, 1, 4)):
                copy_rows(TY, lambda i: fx.at[place_of, 1 + i], lambda i: flow_ref.at[f, i])
            fx[1, 0] = jnp.where(odd, pair_a[NC, 0], pair_b[NC, 0])
            fx[4, 0] = jnp.where(odd, pair_a[NC, 1], pair_b[NC, 1])
            fx[4, TY + 1] = jnp.where(odd, pair_b[NC, 1], pair_a[NC, 1])
        flow_edges = column_edges(cin.at[2], cin.at[3])
        fields = {"U": 0, "V": 1, "rho": 2, "E": 3, "K": 4}

        def get(f, y):
            return halves(fx[fields[f], y + 1])

        def spread_lane(ref, side, y, spot):
            v = ref[side, y // 4]
            return jnp.broadcast_to(v[:, spot : spot + 1], (NZ, 128))

        edge_w = [jnp.zeros((NZ, 128), F32)] * 2
        edge_d = [jnp.zeros((NZ, 128), F32)] * 2
        k_index = levels()
        east_k = []
        if first_step:
            turned = [[pltpu.roll(cin[2 + side, g], lax.rem(128 - third, 128), 1) for g in range(2)] for side in range(2)]
        for y in range(TY):
            g, base = y // 4, 32 * (y % 4)
            if first_step:
                def column(side, slot):
                    v = turned[side][g]
                    return jnp.broadcast_to(v[:, base + 3 * slot : base + 3 * slot + 1], (NZ, 128))

                u_west = column(0, 0)
                k_west = 0.05 + 0.15 * column(0, 4)
                k_east = 0.05 + 0.15 * column(1, 4)
            else:
                u_west = spread_lane(cin, 0, y, base + 30)
                k_west = spread_lane(cin, 0, y, base + 31)
                k_east = spread_lane(cin, 1, y, base + 31)
            east_k.append(k_east)
            k_here = jnp.broadcast_to(fx[4, y + 1, :, 0:1], (NZ, 128))
            m_here = jnp.where(k_index < nb_ref[0, y + 8 : y + 9, 0:1], 1.0, 0.0)
            m_west = jnp.where(k_index < nb_ref[2, y + 8 : y + 9, 0:1], 1.0, 0.0)
            both = m_here * m_west
            group = (lane >= base) & (lane < base + 32)
            edge_w[g] = jnp.where(group, DT * both * u_west, edge_w[g])
            edge_d[g] = jnp.where(group, DT * both * (k_west + k_here), edge_d[g])
        packed = []
        for g in range(2):
            half = slice(g * 128, g * 128 + 128)
            q_1 = cin[0, g]
            q_2 = pltpu.roll(q_1, 1, 1)
            q255, q1 = by_parity(mine_b[:, half], mine_a[:, half])
            q0 = pltpu.roll(q1, 1, 1)
            d_2, d_1, d0 = 0.5 * (q_1 - q_2), 0.5 * (q0 - q_1), 0.5 * (q1 - q0)
            h_1, h0 = minmod(d_1, d_2), minmod(d0, d_1)
            w = edge_w[g]
            flux = w * jnp.where(w > 0, q_1 + h_1, q0 - h0) - edge_d[g] * d_1
            q257 = cin[1, g]
            q256 = pltpu.roll(q257, 1, 1)
            high_east = q256 - minmod(0.5 * (q257 - q256), 0.5 * (q256 - q255))
            packed.append((d_1, flux, 0.5 * q256, high_east))
        for g in range(2):
            for n in range(4):
                cin[4 + n, g] = packed[g][n]

        for y in range(-1, TY):
            m, m_n = wet(nb_ref, 0, y), wet(nb_ref, 0, y + 1)
            v, k, k_n = get("V", y), get("K", y), get("K", y + 1)
            both = [m[h] * m_n[h] for h in range(2)]
            put(wy, (y + 1,), [DT * both[h] * v[h] for h in range(2)])
            put(dy, (y + 1,), [DT * both[h] * (k[h] + k_n[h]) for h in range(2)])
            if y < 0:
                continue
            m_e = wet(nb_ref, 1, y)
            both = [m[h] * m_e[h] for h in range(2)]
            u = get("U", y)
            k_e = east_of(k, east_k[y], last)
            put(wx, (y,), [DT * both[h] * u[h] for h in range(2)])
            put(dx, (y,), [DT * both[h] * (k[h] + k_e[h]) for h in range(2)])
            inner = jnp.where(k_index < NZ - 1.0, 0.5 * DT, 0.0)
            put(dz, (y,), [inner * (m[h] * level_down(m[h])) * (k[h] + level_down(k[h])) for h in range(2)])
            put(mm, (y,), m)

        if first_step:
            pltpu.make_async_copy(z_hbm.at[pl.ds(0, NC)], lowq, sems.at[6]).wait()
            pltpu.make_async_copy(z_hbm.at[pl.ds(0, NC)], highq, sems.at[7]).wait()

        def tracer(c, carry):
            if first_step:
                for copy in band(c):
                    copy().wait()
            q = {y: halves(state_ref[c, y]) for y in range(TY)}
            for y in range(2):
                if first_step:
                    low, high = lowq[c, y], highq[c, y]
                else:
                    low = jnp.where(odd, pair_a[c, y], pair_b[c, y])
                    high = jnp.where(odd, pair_b[c, y], pair_a[c, y])
                q[y - 2], q[y + TY] = halves(low), halves(high)
            p = {y: [0.5 * v for v in q[y]] for y in q}
            d = {y: [p[y + 1][h] - p[y][h] for h in range(2)] for y in range(-2, TY + 1)}
            s = {y: [minmod(d[y][h], d[y - 1][h]) for h in range(2)] for y in range(-1, TY + 1)}
            north = {}
            for y in range(-1, TY):
                w, f = halves(wy[y + 1]), halves(dy[y + 1])
                north[y] = [
                    w[h] * jnp.where(w[h] > 0, q[y][h] + s[y][h], q[y + 1][h] - s[y + 1][h]) - f[h] * d[y][h]
                    for h in range(2)
                ]
            for y in range(TY):
                g, spot = y // 4, 32 * (y % 4) + 2 * c
                to_first, to_last = 127 - spot, 126 - spot
                p_e = east_of(p[y], pltpu.roll(cin[6, g], to_last, 1), last)
                dxx = [p_e[h] - p[y][h] for h in range(2)]
                d_w = west_of(dxx, pltpu.roll(cin[4, g], to_first, 1), first)
                slope = [minmod(dxx[h], d_w[h]) for h in range(2)]
                low = [q[y][h] + slope[h] for h in range(2)]
                high = [q[y][h] - slope[h] for h in range(2)]
                high_e = east_of(high, pltpu.roll(cin[7, g], to_last, 1), last)
                w, f = halves(wx[y]), halves(dx[y])
                flux = [w[h] * jnp.where(w[h] > 0, low[h], high_e[h]) - f[h] * dxx[h] for h in range(2)]
                flux_w = west_of(flux, pltpu.roll(cin[5, g], to_first, 1), first)
                base, z, m = halves(racc[c, y]), halves(dz[y]), halves(mm[y])
                new = []
                for h in range(2):
                    down = z[h] * (level_down(q[y][h]) - q[y][h])
                    vert = down - pltpu.roll(down, 1, 0)
                    new.append(m[h] * (base[h] + (flux_w[h] - flux[h]) + (north[y - 1][h] - north[y][h]) + vert))
                if first_step:
                    put(out_ref, (c, y), new)
                else:
                    for h in range(2):
                        out_ref[h, c, pl.ds(y, NZ, stride=TY), :] = new[h]
            if not first_step:
                for h in range(2):
                    leave(c, h).start()
            return carry

        lax.fori_loop(0, NC, tracer, 0)

        if first_step:
            def flow(y, carry):
                out = flow_update(get, lambda f, row, side: flow_edges(f, y, side, third), nb_ref, y, ("U", "V", "rho", "E")[:2] + ("rho", "E"))
                put(flow_out, (0, y), out["U"])
                put(flow_out, (1, y), out["V"])
                put(flow_out, (2, y), [0.05 + 0.15 * e for e in out["E"]])
                return carry

            lax.fori_loop(0, TY, flow, 0)

            def edge_rows(c, carry):
                for j in range(2):
                    top, base = out_ref[c, TY - 2 + j], out_ref[c, j]
                    pair_a[c, j] = jnp.where(odd, base, top)
                    pair_b[c, j] = jnp.where(odd, top, base)
                return carry

            lax.fori_loop(0, NC, edge_rows, 0)
            for j, f in ((0, 1), (1, 2)):
                top, base = flow_out[f, TY - 1], flow_out[f, 0]
                pair_a[NC, j] = jnp.where(odd, base, top)
                pair_b[NC, j] = jnp.where(odd, top, base)
            for y in range(TY):
                for h in range(2):
                    green[h, NZ * y : NZ * y + NZ, :] = out_ref[2, y, :, h * 128 : h * 128 + 128]
            shade(lambda h, k: green[h, pl.ds(k, TY, stride=NZ), :], sun2, heat2)
            for y in range(TY):
                rows = slice(NZ * y, NZ * y + NZ)
                put(sun_out, (y,), [sun2[h, rows] for h in range(2)])
                put(heat_ref, (y,), [heat2[h, rows] for h in range(2)])

    if not first_step:
        for h in range(2):
            leave(slice(None), h).wait()
    if first_step:
        per = jnp.where(section == 0, 1, 2)
        packs = list(pack_columns(lambda c, y: halves(out_ref[c, y]), per))

        @pl.when(section == 0)
        def _():
            give_columns(packs, first_out, second_out)

        @pl.when(section > 0)
        def _():
            tiles = list(packs)
            for y in range(TY):
                g, base = y // 4, 32 * (y % 4)
                k0 = jnp.broadcast_to(flow_out[2, y, :, 0:1], (NZ, 128))
                u255 = jnp.broadcast_to(flow_out[0, y, :, 255:256], (NZ, 128))
                k255 = jnp.broadcast_to(flow_out[2, y, :, 255:256], (NZ, 128))
                tiles[g] = jnp.where(lane == base + 31, k0, tiles[g])
                tiles[2 + g] = jnp.where(lane == base + 30, u255, tiles[2 + g])
                tiles[2 + g] = jnp.where(lane == base + 31, k255, tiles[2 + g])
            give_columns(tiles, first_out, second_out)


def heat_kernel(out_any, heat1, heat2, heat3, nb_ref, out_hbm, warm_ref, sems):
    section, even, _ = place()

    @pl.when(section == 0)
    def _():
        def moves(back):
            pairs = [(out_hbm.at[pl.ds(6, 3), :, pl.ds(128 * h, 128)], warm_ref.at[h]) for h in range(2)]
            return [pltpu.make_async_copy(*(p[::-1] if back else p), sems.at[h]) for h, p in enumerate(pairs)]

        for move in moves(False):
            move.start()
        for move in moves(False):
            move.wait()

        def body(y, carry):
            ends = [jnp.where(even, heat1[y], heat3[y]), heat2[y], jnp.where(even, heat3[y], heat1[y])]
            for t in range(3):
                m = wet(nb_ref, 0, TY * t + y)
                warm = halves(ends[t])
                for h in range(2):
                    spot = (h, t, pl.ds(y, NZ, stride=TY), slice(None))
                    warm_ref[spot] = warm_ref[spot] + m[h] * (DT * 3.0 * warm[h])
            return carry

        lax.fori_loop(0, TY, body, 0)
        for move in moves(True):
            move.start()
        for move in moves(True):
            move.wait()


def sds(*shape):
    return jax.ShapeDtypeStruct(shape, F32)


def vmem(n):
    return [pl.BlockSpec(memory_space=pltpu.VMEM)] * n


def step_scratch(first_step):
    row = (NZ, NX)
    scratch = []
    if first_step:
        scratch = [pltpu.VMEM((NC, TY) + row, F32)] * 2 + [pltpu.VMEM((16, 2) + row, F32)]
        scratch += [pltpu.VMEM((NC, 2) + row, F32)] * 2
        scratch += [pltpu.VMEM((9,) + row, F32), pltpu.VMEM((3, 40, NX), F32)] + [pltpu.VMEM(row, F32)] * 4
    scratch += [
        pltpu.VMEM((5, 26) + row, F32),
        pltpu.VMEM((TY,) + row, F32),
        pltpu.VMEM((TY,) + row, F32),
        pltpu.VMEM((TY + 1,) + row, F32),
        pltpu.VMEM((TY + 1,) + row, F32),
        pltpu.VMEM((TY,) + row, F32),
        pltpu.VMEM((TY,) + row, F32),
        pltpu.VMEM((8, 2, NZ, 128), F32),
    ]
    if first_step:
        scratch += [pltpu.VMEM((2, TY * NZ, 128), F32)] * 3
        return scratch + [pltpu.SemaphoreType.DMA((9,)), pltpu.SemaphoreType.DMA((2, NC))]
    return scratch + [pltpu.VMEM((2, NC, NZ * TY, 128), F32), pltpu.SemaphoreType.DMA((2,))]


def pairs_of(mesh):
    ns, ngy, ngx = (mesh.shape[a] for a in AXES)

    def at(s, g, x):
        return (s * ngy + g) * ngx + x

    cross, ocean, chain, swaps, heat = [], ([], []), ([], []), ([], []), {1: [], 2: [], 3: []}
    for x in range(ngx):
        for g in range(ngy):
            order = (1, 2, 3) if g % 2 == 0 else (3, 2, 1)
            for t, (a, b) in enumerate(zip(order, order[1:])):
                chain[(3 * g + t) % 2].append((at(a, g, x), at(b, g, x)))
            if g + 1 < ngy:
                cross.append((at(order[2], g, x), at(order[2], g + 1, x)))
                chain[(3 * g + 2) % 2].append(cross[-1])
                ocean[g % 2].append((at(0, g, x), at(0, g + 1, x)))
            for s in heat:
                heat[s].append((at(s, g, x), at(0, g, x)))
            if x + 1 < ngx:
                swaps[x % 2].extend((at(s, g, x), at(s, g, x + 1)) for s in range(ns))
    chain = [a + b for a, b in zip(chain, ocean)]
    return cross + turn(cross), *[[p + turn(p) for p in pairs] for pairs in (ocean, chain, swaps)], heat


def turn(pairs):
    return [(b, a) for a, b in pairs]


def solution(mesh):
    cross, ocean, chain, swaps, heat_pairs = pairs_of(mesh)

    def send(value, pairs):
        return lax.ppermute(value, AXES, pairs)

    def program(fields, sea_mask, bottom, reaction, growth):
        x = fields.reshape(NC, NZ * TY, NX)
        row = (NZ, NX)
        block = sds(NC, TY, *row)
        halo = sds(16, 2, *row)
        anywhere = pl.BlockSpec(memory_space=pltpu.HBM)
        loose = pl.BlockSpec(memory_space=pl.ANY)
        weights = jax.ShapeDtypeStruct((NC * NZ, NC * NZ), BF16)

        def call(body, out_shape, in_specs, out_specs, scratch=(), cost=None, limit=VMEM_LIMIT):
            def placed(shape, spec):
                return pltpu.HBM(shape.shape, shape.dtype) if spec is anywhere else shape

            if isinstance(out_specs, tuple):
                out_shape = tuple(placed(*pair) for pair in zip(out_shape, out_specs))
            kernel = pl.pallas_call(
                body,
                out_shape=out_shape,
                in_specs=in_specs,
                out_specs=out_specs,
                scratch_shapes=list(scratch),
                compiler_params=pltpu.CompilerParams(vmem_limit_bytes=limit),
                cost_estimate=cost,
            )

            def run(*operands):
                return kernel(*[
                    pltpu.with_memory_space_constraint(v, pltpu.HBM) if spec is anywhere else v
                    for v, spec in zip(operands, in_specs)
                ])

            return run

        x_scratch = pltpu.VMEM((2, NC, NZ * TY, 128), F32)
        rows = pltpu.VMEM((2, TY * NZ, 128), F32)
        a_out, z, oa, ob = call(
            send_kernel, (sds(4, 16, 2, *row), halo, sds(5, *row), sds(5, *row)), [anywhere],
            (anywhere,) * 2 + tuple(vmem(2)),
            [x_scratch, pltpu.VMEM((16, 2) + row, F32), pltpu.VMEM((16, 2) + row, F32), pltpu.VMEM((3, 16, 2) + row, F32),
             rows, rows, pltpu.SemaphoreType.DMA((5,))],
        )(x)
        recv = lax.all_to_all(a_out, "section", split_axis=0, concat_axis=0, tiled=True)
        oa_in, ob_in = send(oa, ocean[0]), send(ob, ocean[1])
        mine_a, mine_b, ends = call(
            column_kernel, (sds(*row), sds(*row), sds(2, NC, *row)), [anywhere], tuple(vmem(3)),
            [x_scratch, pltpu.SemaphoreType.DMA((2,))],
        )(x)
        first_in, second_in = send(mine_a, swaps[0]), send(mine_b, swaps[1])
        z_in = send(z, cross)
        rims = call(rim_kernel, tuple([sds(9, *row)] * 3), vmem(5), tuple(vmem(3)))(ends, oa_in, ob_in, first_in, second_in)
        rims = [send(r, turn(heat_pairs[s])) for s, r in zip((1, 2, 3), rims)]
        react_cost = pl.CostEstimate(flops=6 * 240 * 240 * 2048, bytes_accessed=2 * NC * TY * NZ * NX * 4, transcendentals=0)
        window = pltpu.VMEM((5, TY, 512), jnp.int32)
        whole = pltpu.VMEM((NC, TY) + row, F32)
        square = pltpu.VMEM((NC * NZ, NC * NZ), BF16)
        state, grown, w_high, w_low, nb = call(
            functools.partial(react_kernel, True), (block, block, weights, weights, sds(3, 40, NX)),
            [anywhere] * 3 + vmem(2), (anywhere,) * 5,
            [x_scratch, whole, whole, square, square, pltpu.VMEM((3, 40, NX), F32), pltpu.VMEM((TY,) + row, F32), window, window,
             rows, rows, pltpu.SemaphoreType.DMA((2,)), pltpu.SemaphoreType.DMA((2, 5, 3)), pltpu.SemaphoreType.DMA((5,))],
            cost=react_cost, limit=60 * 1024 * 1024,
        )(x, sea_mask, bottom, reaction, growth.reshape(1, NC))
        state1, pair_a, pair_b, next_a, next_b, heat1, sun1, flow1 = call(
            functools.partial(step_kernel, True),
            (block, halo, halo, sds(*row), sds(*row), sds(TY, *row), sds(TY, *row), sds(3, TY, *row)),
            [anywhere] * 2 + [loose] * 9 + [anywhere] * 3, tuple(vmem(8)), step_scratch(True),
        )(state, grown, recv, z_in, oa_in, ob_in, first_in, second_in, *rims, nb, mine_a, mine_b)
        pair_a_in, pair_b_in = send(pair_a, chain[0]), send(pair_b, chain[1])
        first1_in, second1_in = send(next_a, swaps[0]), send(next_b, swaps[1])
        heats = [send(heat1, heat_pairs[s]) for s in (1, 2, 3)]
        grown1 = call(
            functools.partial(react_kernel, False), block, vmem(4), vmem(1)[0], cost=react_cost,
        )(state1, sun1, w_high, w_low)
        out = call(
            functools.partial(step_kernel, False), sds(NC, NZ * TY, NX), vmem(10), anywhere, step_scratch(False),
        )(state1, grown1, pair_a_in, pair_b_in, first1_in, second1_in, nb, next_a, next_b, flow1)
        out = pl.pallas_call(
            heat_kernel,
            out_shape=sds(NC, NZ * TY, NX),
            in_specs=[anywhere] + vmem(4),
            out_specs=anywhere,
            scratch_shapes=[pltpu.VMEM((2, 3, NZ * TY, 128), F32), pltpu.SemaphoreType.DMA((2,))],
            input_output_aliases={0: 0},
            compiler_params=pltpu.CompilerParams(vmem_limit_bytes=VMEM_LIMIT),
            name="heating",
        )(out, *heats, nb)
        return out.reshape(1, NC, NZ, TY, NX)

    return jax.shard_map(
        program,
        mesh=mesh,
        in_specs=(P("section", None, None, "gy", "gx"), P(), P(), P(), P()),
        out_specs=P("section", None, None, "gy", "gx"),
        check_vma=False,
    )
```

```python
import functools

import jax
import jax.numpy as jnp
from jax import lax
from jax.experimental import pallas as pl
from jax.experimental.pallas import tpu as pltpu
from jax.sharding import PartitionSpec as P


AXES = ("section", "gy", "gx")
NC, NZ, TY, NX = 15, 16, 8, 256
DT = 0.2
F32 = jnp.float32
BF16 = jnp.bfloat16
VMEM_LIMIT = 24 * 1024 * 1024


def minmod(a, b):
    return jnp.maximum(jnp.minimum(a, b), jnp.minimum(jnp.maximum(a, b), 0.0))


def lanes():
    return lax.broadcasted_iota(jnp.int32, (NZ, 128), 1)


def levels():
    return lax.broadcasted_iota(jnp.int32, (NZ, 128), 0).astype(F32)


def halves(row):
    return row[:, :128], row[:, 128:]


def place():
    section = lax.axis_index("section")
    tile = lax.axis_index("gy")
    even = tile % 2 == 0
    third = jnp.where(even, section - 1, 3 - section)
    return section, even, third


def shade(read, sun_ref, heat_ref):
    for h in range(2):
        depth = jnp.zeros((TY, 128), F32)
        for k in range(NZ):
            chlorophyll = jnp.maximum(read(h, k), 0.0)
            sunlight = jnp.exp(-depth)
            depth = depth + (0.05 + 0.1 * chlorophyll)
            sun_ref[h, pl.ds(k, TY, stride=NZ), :] = sunlight
            heat_ref[h, pl.ds(k, TY, stride=NZ), :] = 0.1 * chlorophyll * sunlight


def pack_columns(read, per, loop=functools.partial(lax.fori_loop, 0, NC)):
    lane = lanes()

    def body(c, packs):
        packs = list(packs)
        for y in range(TY):
            left, right = read(c, y)
            spot = 32 * (y % 4) + per * c
            here = (lane >= spot) & (lane < spot + per)
            g = y // 4
            packs[g] = jnp.where(here, pltpu.roll(left, spot, 1), packs[g])
            packs[2 + g] = jnp.where(here, pltpu.roll(right, lax.rem(spot + per, 128), 1), packs[2 + g])
        return tuple(packs)

    zero = jnp.zeros((NZ, 128), F32)
    return loop(body, (zero,) * 4)


PARTS = 3


def load_block(x_hbm, x_ref, sems):
    size = NC // PARTS
    loads = [
        [
            pltpu.make_async_copy(
                x_hbm.at[pl.ds(size * i, size), :, pl.ds(128 * h, 128)], x_ref.at[h, pl.ds(size * i, size)], sems.at[h, i]
            )
            for h in range(2)
        ]
        for i in range(PARTS)
    ]
    for part in loads:
        for load in part:
            load.start()

    def wait(i):
        for load in loads[i]:
            load.wait()

    return wait


def over_parts(wait, body, carry):
    size = NC // PARTS
    for i in range(PARTS):
        wait(i)
        carry = lax.fori_loop(size * i, size * (i + 1), body, carry)
    return carry


def send_kernel(x_hbm, a_hbm, z_hbm, oa_ref, ob_ref, x_ref, top_ref, base_ref, flow_ref, sun2, heat2, sems, loads):
    section, even, third = place()
    is_ocean = section == 0
    odd = chain_odd()
    wait = load_block(x_hbm, x_ref, loads)

    def turned(c, y):
        return [x_ref[h, c, pl.ds(y, NZ, stride=TY), :] for h in range(2)]

    @pl.when(is_ocean)
    def _():
        for i in range(PARTS):
            wait(i)
        for f in range(5):
            top, base = turned(3 * f + 2, TY - 1), turned(3 * f, 0)
            put(oa_ref, (f,), [jnp.where(odd, b, a) for a, b in zip(top, base)])
            put(ob_ref, (f,), [jnp.where(odd, a, b) for a, b in zip(top, base)])
        for t in range(3):
            def body(y, carry):
                i, j = lax.div(y, 2), lax.rem(y, 2)
                salt, warm = turned(9 + t, y), turned(6 + t, y)
                put(flow_ref, (t, i, j), turned(t, y))
                put(flow_ref, (t, 4 + i, j), turned(3 + t, y))
                put(flow_ref, (t, 8 + i, j), [0.8 * salt[h] - 0.2 * warm[h] for h in range(2)])
                put(flow_ref, (t, 12 + i, j), turned(12 + t, y))
                return carry

            lax.fori_loop(0, TY, body, 0)
        outs = []
        for t in range(3):
            target = jnp.where(even, t + 1, 3 - t)
            outs.append(pltpu.make_async_copy(flow_ref.at[t], a_hbm.at[target], sems.at[2 + t]))
        for out in outs:
            out.start()
        for out in outs:
            out.wait()

    @pl.when(jnp.logical_not(is_ocean))
    def _():
        above = jnp.where(even, section + 1, section - 1)
        below = jnp.where(even, section - 1, section + 1)
        above = jnp.where((above < 1) | (above > 3), section, above)
        below = jnp.where((below < 1) | (below > 3), section, below)

        def body(c, carry):
            for j in range(2):
                put(top_ref, (c, j), turned(c, TY - 2 + j))
                put(base_ref, (c, j), turned(c, j))
            return carry

        wait(0)
        shade(lambda h, k: x_ref[h, 2, TY * k : TY * k + TY, :], sun2, heat2)
        for y in range(TY):
            rows = slice(NZ * y, NZ * y + NZ)
            put(flow_ref, (0, y // 2, y % 2), [heat2[h, rows] for h in range(2)])
        warmth = pltpu.make_async_copy(flow_ref.at[0, pl.ds(0, 4)], a_hbm.at[0, pl.ds(0, 4)], sems.at[4])
        warmth.start()
        over_parts(lambda i: wait(i) if i else None, body, 0)
        outs = [
            pltpu.make_async_copy(top_ref, a_hbm.at[above], sems.at[0]),
            pltpu.make_async_copy(base_ref, a_hbm.at[below], sems.at[1]),
        ]
        for out in outs:
            out.start()

        @pl.when(third == 2)
        def _():
            pltpu.make_async_copy(top_ref, z_hbm, sems.at[2]).start()

        @pl.when(third == 0)
        def _():
            pltpu.make_async_copy(base_ref, z_hbm, sems.at[2]).start()

        for out in outs:
            out.wait()
        warmth.wait()

        @pl.when(third != 1)
        def _():
            pltpu.make_async_copy(top_ref, z_hbm, sems.at[2]).wait()


def chain_odd():
    section, _, third = place()
    tile = lax.axis_index("gy")
    return lax.rem(jnp.where(section == 0, tile, 3 * tile + third), 2) == 1


def by_parity(first_in, second_in):
    odd = lax.rem(lax.axis_index("gx"), 2) == 1
    return jnp.where(odd, first_in, second_in), jnp.where(odd, second_in, first_in)


def give_columns(packs, first_ref, second_ref):
    odd = lax.rem(lax.axis_index("gx"), 2) == 1
    for g in range(2):
        half = slice(g * 128, g * 128 + 128)
        first_ref[:, half] = jnp.where(odd, packs[g], packs[2 + g])
        second_ref[:, half] = jnp.where(odd, packs[2 + g], packs[g])


def column_kernel(x_hbm, first_ref, second_ref, ends_ref, x_ref, sems):
    is_ocean = lax.axis_index("section") == 0
    wait = load_block(x_hbm, x_ref, sems)

    def read(c, y):
        return [x_ref[h, c, pl.ds(y, NZ, stride=TY), :] for h in range(2)]

    loop = functools.partial(over_parts, wait)
    give_columns(pack_columns(read, jnp.where(is_ocean, 1, 2), loop), first_ref, second_ref)

    @pl.when(is_ocean)
    def _():
        def body(c, carry):
            put(ends_ref, (0, c), read(c, 0))
            put(ends_ref, (1, c), read(c, TY - 1))
            return carry

        lax.fori_loop(0, NC, body, 0)


def cut_depths(sea_hbm, bottom_hbm, nb_ref, sea_buf, bottom_buf, wins):
    section, _, third = place()
    tile, column = lax.axis_index("gy"), lax.axis_index("gx")
    is_ocean = section == 0
    group = jnp.where(is_ocean, 3 * tile, 3 * tile + third)
    n_groups, n_cols = sea_hbm.shape[0] // TY, sea_hbm.shape[1]
    pieces = ((-128, 128), (0, 256), (256, 128))
    copies = []
    for n, (hbm, buf) in enumerate(((sea_hbm, sea_buf), (bottom_hbm, bottom_buf))):
        for g in range(5):
            row = pl.multiple_of(jnp.clip(group + g - 1, 0, n_groups - 1) * TY, TY)
            for i, (offset, width) in enumerate(pieces):
                col = pl.multiple_of(jnp.clip(column * NX + offset, 0, n_cols - width), 128)
                copies.append(
                    pltpu.make_async_copy(
                        hbm.at[pl.ds(row, TY), pl.ds(col, width)],
                        buf.at[g, :, pl.ds(offset + 128, width)],
                        wins.at[n, g, i],
                    )
                )
    for copy in copies:
        copy.start()

    def finish():
        for copy in copies:
            copy.wait()
        lane = lax.broadcasted_iota(jnp.int32, (TY, 128), 1)
        for g in range(5):
            inside = (group + g - 1 >= 0) & (group + g - 1 < n_groups)
            valid = (column > 0, True, True, column * NX + NX < n_cols)
            depth = []
            for i in range(4):
                part = slice(128 * i, 128 * i + 128)
                value = (sea_buf[g, :, part] * bottom_buf[g, :, part]).astype(F32)
                depth.append(jnp.where(inside & valid[i], value, 0.0))
            rows = slice(TY * g, TY * g + TY)
            for h in range(2):
                cols = slice(128 * h, 128 * h + 128)
                nb_ref[0, rows, cols] = depth[1 + h]
                nb_ref[1, rows, cols] = jnp.where(lane == 127, pltpu.roll(depth[2 + h], 127, 1), pltpu.roll(depth[1 + h], 127, 1))
                nb_ref[2, rows, cols] = jnp.where(lane == 0, pltpu.roll(depth[h], 1, 1), pltpu.roll(depth[1 + h], 1, 1))

    return finish


def build_weights(reaction_ref, growth_ref, wh_ref, wl_ref):
    size = NC * NZ
    matrix = reaction_ref[...] * growth_ref[...]
    level_of = lax.rem(lax.broadcasted_iota(jnp.int32, (size, size), 0), NZ)
    same = level_of == lax.rem(lax.broadcasted_iota(jnp.int32, (size, size), 1), NZ)
    up = lax.div(lax.broadcasted_iota(jnp.int32, (size, NC), 0), NZ) == lax.broadcasted_iota(jnp.int32, (size, NC), 1)
    across = lax.broadcasted_iota(jnp.int32, (NC, size), 0) == lax.div(lax.broadcasted_iota(jnp.int32, (NC, size), 1), NZ)
    up = jnp.where(up, 1.0, 0.0).astype(BF16)
    across = jnp.where(across, 1.0, 0.0).astype(BF16)
    high = matrix.astype(BF16)
    low = (matrix - high.astype(F32)).astype(BF16)
    for part, out in ((high, wh_ref), (low, wl_ref)):
        wide = jnp.dot(part, across, preferred_element_type=F32).astype(BF16)
        full = jnp.dot(up, wide, preferred_element_type=F32)
        out[...] = jnp.where(same, full, 0.0).astype(BF16)


def react_kernel(build, *refs):
    if build:
        (x_hbm, sea_hbm, bottom_hbm, reaction_ref, growth_ref, first_in, second_in, mine_a, mine_b,
         state_hbm, out_hbm, slopes_hbm, wh_hbm, wl_hbm, nb_hbm,
         slopes, ends, x_ref, state_ref, out_ref, wh_ref, wl_ref, nb_ref, sun_ref, sea_buf, bottom_buf, sun2, heat2, sems, wins, kept) = refs
        finish = cut_depths(sea_hbm, bottom_hbm, nb_ref, sea_buf, bottom_buf, wins)
        wait = load_block(x_hbm, x_ref, sems)

        def turn(c, carry):
            for y in range(TY):
                put(state_ref, (c, y), [x_ref[h, c, pl.ds(y, NZ, stride=TY), :] for h in range(2)])
            pltpu.make_async_copy(state_ref.at[c], state_hbm.at[c], kept.at[0]).start()
            return carry

        over_parts(wait, turn, 0)
        finish()
        pltpu.make_async_copy(nb_ref, nb_hbm, kept.at[4]).start()
    else:
        state_ref, sun_ref, wh_ref, wl_ref, out_ref = refs

    @pl.when(lax.axis_index("section") > 0)
    def _():
        if build:
            shade(lambda h, k: x_ref[h, 2, TY * k : TY * k + TY, :], sun2, heat2)
            for y in range(TY):
                put(sun_ref, (y,), [sun2[h, NZ * y : NZ * y + NZ] for h in range(2)])
            build_weights(reaction_ref, growth_ref, wh_ref, wl_ref)

        def react(y, carry):
            q = state_ref[:, y]
            x = jnp.maximum(q, 0.0).reshape(NC * NZ, NX)
            x_high = x.astype(BF16)
            x_low = (x - x_high.astype(F32)).astype(BF16)
            total = jnp.dot(wh_ref[...], x_high, preferred_element_type=F32)
            total = total + jnp.dot(wh_ref[...], x_low, preferred_element_type=F32)
            total = total + jnp.dot(wl_ref[...], x_high, preferred_element_type=F32)
            nutrient = jnp.maximum(q[0], 0.0)
            uptake = DT * (nutrient / (nutrient + 0.5) * sun_ref[y])
            out_ref[:, y] = q + total.reshape(NC, NZ, NX) * uptake[None]
            if build:
                pltpu.make_async_copy(out_ref.at[:, y], out_hbm.at[:, y], kept.at[1]).start()
            return carry

        if build:
            weights = [pltpu.make_async_copy(wh_ref, wh_hbm, kept.at[2]), pltpu.make_async_copy(wl_ref, wl_hbm, kept.at[3])]
            for copy in weights:
                copy.start()
        lax.fori_loop(0, TY, react, 0)
        if build:
            lane = lanes()
            first, last = lane == 0, lane == 127
            for g in range(2):
                half = slice(g * 128, g * 128 + 128)
                west, east = by_parity(first_in[:, half], second_in[:, half])
                mine_east, mine_west = by_parity(mine_b[:, half], mine_a[:, half])
                d_1, _, _, half_east, high_east = column_ends(west, east, mine_west, mine_east)
                ends[0, g], ends[1, g], ends[2, g] = d_1, half_east, high_east

            def slope(c, carry):
                for y in range(TY):
                    g, spot = y // 4, 32 * (y % 4) + 2 * c
                    to_first, to_last = 127 - spot, 126 - spot
                    q = halves(state_ref[c, y])
                    parts = column_slopes(
                        q, [0.5 * v for v in q], pltpu.roll(ends[1, g], to_last, 1), pltpu.roll(ends[0, g], to_first, 1),
                        pltpu.roll(ends[2, g], to_last, 1), first, last,
                    )
                    for n, part in enumerate(parts):
                        put(slopes, (n, c, y), part)
                pltpu.make_async_copy(slopes.at[:, c], slopes_hbm.at[:, c], kept.at[5]).start()
                return carry

            lax.fori_loop(0, NC, slope, 0)
            for copy in weights:
                copy.wait()
            pltpu.make_async_copy(slopes, slopes_hbm, kept.at[5]).wait()
            pltpu.make_async_copy(out_ref, out_hbm, kept.at[1]).wait()

    if build:
        pltpu.make_async_copy(state_ref, state_hbm, kept.at[0]).wait()
        pltpu.make_async_copy(nb_ref, nb_hbm, kept.at[4]).wait()


def rim_kernel(ends_ref, oa_ref, ob_ref, first_ref, second_ref, r1_ref, r2_ref, r3_ref):
    section, even, _ = place()
    odd = chain_odd()

    @pl.when(section == 0)
    def _():
        def row(t, f, y):
            if y < 0:
                return jnp.where(odd, oa_ref[f], ob_ref[f]) if t == 0 else ends_ref[1, 3 * f + t - 1]
            return jnp.where(odd, ob_ref[f], oa_ref[f]) if t == 2 else ends_ref[0, 3 * f + t + 1]

        def fill(out, t):
            for n, y in ((0, -1), (4, TY)):
                out[n] = row(t, 0, y)
                out[n + 1] = row(t, 1, y)
                out[n + 2] = 0.8 * row(t, 3, y) - 0.2 * row(t, 2, y)
                out[n + 3] = row(t, 4, y)
            for g in range(2):
                half = slice(g * 128, g * 128 + 128)
                west, east = by_parity(first_ref[:, half], second_ref[:, half])
                out[8, :, half] = west + pltpu.roll(east, 16, 1)

        fill(r2_ref, 1)

        @pl.when(even)
        def _():
            fill(r1_ref, 0)
            fill(r3_ref, 2)

        @pl.when(jnp.logical_not(even))
        def _():
            fill(r1_ref, 2)
            fill(r3_ref, 0)


def wet(nb_ref, shift, y):
    k = levels()
    row = nb_ref[shift, pl.ds(y + 8, 1), :]
    return tuple(jnp.where(k < row[:, h * 128 : h * 128 + 128], 1.0, 0.0) for h in range(2))


def east_of(pair, edge, last):
    a, b = (pltpu.roll(v, 127, 1) for v in pair)
    return jnp.where(last, b, a), jnp.where(last, edge, b)


def west_of(pair, edge, first):
    a, b = (pltpu.roll(v, 1, 1) for v in pair)
    return jnp.where(first, edge, a), jnp.where(first, a, b)


def level_down(v):
    return pltpu.roll(v, NZ - 1, 0)


def flow_update(get, edge, nb_ref, y, names):
    lane = lanes()
    first, last = lane == 0, lane == 127
    centre, east, west = (wet(nb_ref, s, y) for s in range(3))
    north, south = wet(nb_ref, 0, y + 1), wet(nb_ref, 0, y - 1)
    here = {f: get(f, y) for f in names}
    around = {}
    for f in names:
        if f == "E":
            continue
        around[f] = (
            east_of(here[f], edge(f, y, 1), last),
            west_of(here[f], edge(f, y, 0), first),
            get(f, y + 1),
            get(f, y - 1),
        )
    out = {f: [] for f in names}
    for h in range(2):
        m = centre[h]
        sides = (east[h], west[h], north[h], south[h])

        def lap(f):
            c = here[f][h]
            total = 0.0
            for w, v in zip(sides, around[f]):
                total = total + w * (v[h] - c)
            return m * total

        u, v, e = here["U"][h], here["V"][h], here["E"][h]
        if "T" in names:
            rho = 0.8 * here["S"][h] - 0.2 * here["T"][h]
            near = [0.8 * s[h] - 0.2 * t[h] for s, t in zip(around["S"], around["T"])]
        else:
            rho = here["rho"][h]
            near = [r[h] for r in around["rho"]]
        grad_x = 0.5 * (sides[0] * (near[0] - rho) + sides[1] * (rho - near[1]))
        grad_y = 0.5 * (sides[2] * (near[2] - rho) + sides[3] * (rho - near[3]))
        out["U"].append(m * (u + DT * (0.5 * v - 0.5 * grad_x + 0.15 * lap("U") - 0.1 * u)))
        out["V"].append(m * (v + DT * (-0.5 * u - 0.5 * grad_y + 0.15 * lap("V") - 0.1 * v)))
        inner = jnp.where(levels() < NZ - 1.0, 1.0, 0.0)
        open_below = m * level_down(m) * inner
        du, dv = level_down(u) - u, level_down(v) - v
        shear = (du * du + dv * dv) * open_below
        out["E"].append(m * (e + DT * (0.5 * shear - 0.5 * e)))
        if "T" in names:
            out["T"].append(here["T"][h] * m + m * (DT * (0.15 * lap("T"))))
            out["S"].append(m * (here["S"][h] + DT * (0.15 * lap("S"))))
    return out


def put(ref, index, pair):
    ref[index + (slice(None), slice(0, 128))] = pair[0]
    ref[index + (slice(None), slice(128, 256))] = pair[1]


def column_edges(right_in, left_in):
    slot = {"U": 0, "V": 1, "T": 2, "S": 3, "E": 4}

    def edge(name, y, side, third):
        if name == "rho":
            return 0.8 * edge("S", y, side, third) - 0.2 * edge("T", y, side, third)
        ref = (right_in, left_in)[side]
        spot = 32 * lax.rem(y, 4) + 3 * slot[name] + third
        target = 0 if side == 0 else 127
        return pltpu.roll(ref[lax.div(y, 4)], lax.rem(target - spot + 256, 128), 1)

    return edge


def column_ends(west, east, mine_west, mine_east):
    q_1, q1, q255, q257 = west, mine_west, mine_east, east
    q_2, q0, q256 = pltpu.roll(q_1, 1, 1), pltpu.roll(q1, 1, 1), pltpu.roll(q257, 1, 1)
    d_2, d_1, d0 = 0.5 * (q_1 - q_2), 0.5 * (q0 - q_1), 0.5 * (q1 - q0)
    h_1, h0 = minmod(d_1, d_2), minmod(d0, d_1)
    high_east = q256 - minmod(0.5 * (q257 - q256), 0.5 * (q256 - q255))
    return d_1, q_1 + h_1, q0 - h0, 0.5 * q256, high_east


def column_slopes(q, p, half_east, d_west, high_east, first, last):
    p_e = east_of(p, half_east, last)
    d = [p_e[h] - p[h] for h in range(2)]
    d_w = west_of(d, d_west, first)
    slope = [minmod(d[h], d_w[h]) for h in range(2)]
    low = [q[h] + slope[h] for h in range(2)]
    return d, low, east_of([q[h] - slope[h] for h in range(2)], high_east, last)


def step_kernel(first_step, *refs):
    if first_step:
        (state_hbm, racc_hbm, slopes_hbm, recv_hbm, z_hbm, oa_hbm, ob_hbm, first_hbm, second_hbm, rim1, rim2, rim3, nb_hbm, mine_a_hbm, mine_b_hbm,
         out_ref, pair_a, pair_b, first_out, second_out, heat_ref, sun_out, flow_out,
         state_ref, racc, inflow, lowq, highq, rim, nb_ref, first_in, second_in, mine_a, mine_b,
         packed_out, slopes, fx, wx, dx, wy, dy, dz, mm, cin, sun2, heat2, green, sems, bands) = refs
    else:
        (state_ref, racc, pair_a, pair_b, first_in, second_in, nb_ref, mine_a, mine_b, flow_ref,
         out_hbm,
         fx, wx, dx, wy, dy, dz, mm, cin, out_ref, sems) = refs
    section, even, third = place()
    odd = chain_odd()
    lane = lanes()
    first, last = lane == 0, lane == 127

    def leave(c, h):
        return pltpu.make_async_copy(out_ref.at[h, c], out_hbm.at[c, :, pl.ds(128 * h, 128)], sems.at[h])

    def copy_rows(n, target, source):
        def body(i, carry):
            target(i)[...] = source(i)[...]
            return carry

        lax.fori_loop(0, n, body, 0)

    if first_step:
        def fetch(source, target, sem):
            copy = pltpu.make_async_copy(source, target, sem)
            copy.start()
            return copy

        small = [
            fetch(source, target, sems.at[i])
            for i, (source, target) in enumerate(
                ((nb_hbm, nb_ref), (first_hbm, first_in), (second_hbm, second_in), (mine_a_hbm, mine_a), (mine_b_hbm, mine_b))
            )
        ]

        @pl.when(section == 0)
        def _():
            for t in range(3):
                fetch(recv_hbm.at[jnp.where(even, t + 1, 3 - t), pl.ds(0, 4)], inflow.at[pl.ds(4 * t, 4)], sems.at[5])
            fetch(oa_hbm, highq.at[pl.ds(0, 5), 0], sems.at[6])
            fetch(ob_hbm, lowq.at[pl.ds(0, 5), 0], sems.at[7])

        @pl.when(section > 0)
        def _():
            fetch(recv_hbm.at[0], inflow, sems.at[5])
            for s, source in ((1, rim1), (2, rim2), (3, rim3)):
                @pl.when(section == s)
                def _():
                    fetch(source, rim, sems.at[8])
            below = jnp.where(even, section - 1, section + 1)
            above = jnp.where(even, section + 1, section - 1)
            for index, dest, sem in ((below, lowq, 6), (above, highq, 7)):
                end = (index < 1) | (index > 3)

                @pl.when(end)
                def _():
                    fetch(z_hbm.at[pl.ds(0, NC)], dest, sems.at[sem])

                @pl.when(jnp.logical_not(end))
                def _():
                    fetch(recv_hbm.at[jnp.clip(index, 0, 3), pl.ds(0, NC)], dest, sems.at[sem])

        def band(c):
            return (
                lambda: pltpu.make_async_copy(state_hbm.at[c], state_ref.at[c], bands.at[0, c]),
                lambda: pltpu.make_async_copy(racc_hbm.at[c], racc.at[c], bands.at[1, c]),
                lambda: pltpu.make_async_copy(slopes_hbm.at[:, c], slopes.at[:, c], bands.at[2, c]),
            )

        for c in range(NC):
            band(c)[0]().start()

            @pl.when(section > 0)
            def _():
                band(c)[1]().start()
                band(c)[2]().start()

        for copy in small:
            copy.wait()

    for g in range(2):
        half = slice(g * 128, g * 128 + 128)
        cin[0, g], cin[1, g] = by_parity(first_in[:, half], second_in[:, half])
    edges = column_edges(cin.at[0], cin.at[1])

    @pl.when(section == 0)
    def _():
        if first_step:
            pltpu.make_async_copy(recv_hbm.at[0, pl.ds(0, 12)], inflow.at[pl.ds(0, 12)], sems.at[5]).wait()
            pltpu.make_async_copy(oa_hbm, highq.at[pl.ds(0, 5), 0], sems.at[6]).wait()
            pltpu.make_async_copy(ob_hbm, lowq.at[pl.ds(0, 5), 0], sems.at[7]).wait()
            for c in range(NC):
                band(c)[0]().wait()
        for f in range(5):
            from_a, from_b = (highq[f, 0], lowq[f, 0]) if first_step else (pair_a[f, 0], pair_b[f, 0])
            fx[f, 0] = jnp.where(odd, from_a, from_b)
            fx[f, 25] = jnp.where(odd, from_b, from_a)
            for t in range(3):
                copy_rows(TY, lambda i: fx.at[f, 1 + TY * t + i], lambda i: state_ref.at[3 * f + t, i])
        names = ("U", "V", "T", "S", "E")

        def get(f, y):
            return halves(fx[names.index(f), y + 1])

        for t in range(3):
            def body(y, carry):
                r = TY * t + y
                out = flow_update(get, lambda f, row, side: edges(f, y, side, t), nb_ref, r, names)
                if first_step:
                    m = wet(nb_ref, 0, r)
                    warm = halves(inflow[4 * t + lax.div(y, 2), lax.rem(y, 2)])
                    out["T"] = [out["T"][h] + m[h] * (DT * 3.0 * warm[h]) for h in range(2)]
                for f, name in enumerate(names):
                    if first_step:
                        put(out_ref, (3 * f + t, y), out[name])
                    else:
                        for h in range(2):
                            out_ref[h, 3 * f + t, pl.ds(y, NZ, stride=TY), :] = out[name][h]
                return carry

            lax.fori_loop(0, TY, body, 0)
            if not first_step:
                for f in range(5):
                    for h in range(2):
                        leave(3 * f + t, h).start()
        if first_step:
            for f in range(5):
                top, base = out_ref[3 * f + 2, TY - 1], out_ref[3 * f, 0]
                pair_a[f, 0] = jnp.where(odd, base, top)
                pair_b[f, 0] = jnp.where(odd, top, base)

    @pl.when(section > 0)
    def _():
        if first_step:
            pltpu.make_async_copy(recv_hbm.at[0], inflow, sems.at[5]).wait()
            pltpu.make_async_copy(rim1, rim, sems.at[8]).wait()
            for f in range(4):
                copy_rows(TY, lambda i: fx.at[f, 1 + i], lambda i: inflow.at[4 * f + lax.div(i, 2), lax.rem(i, 2)])
                fx[f, 0] = rim[f]
                fx[f, TY + 1] = rim[4 + f]
            for g in range(2):
                ends = rim[8, :, g * 128 : g * 128 + 128]
                cin[2, g] = ends
                cin[3, g] = pltpu.roll(ends, 112, 1)
            for y in range(TY + 2):
                fx[4, y] = 0.05 + 0.15 * fx[3, y]
        else:
            for f, place_of in enumerate((0, 1, 4)):
                copy_rows(TY, lambda i: fx.at[place_of, 1 + i], lambda i: flow_ref.at[f, i])
            fx[1, 0] = jnp.where(odd, pair_a[NC, 0], pair_b[NC, 0])
            fx[4, 0] = jnp.where(odd, pair_a[NC, 1], pair_b[NC, 1])
            fx[4, TY + 1] = jnp.where(odd, pair_b[NC, 1], pair_a[NC, 1])
        flow_edges = column_edges(cin.at[2], cin.at[3])
        fields = {"U": 0, "V": 1, "rho": 2, "E": 3, "K": 4}

        def get(f, y):
            return halves(fx[fields[f], y + 1])

        def spread_lane(ref, side, y, spot):
            v = ref[side, y // 4]
            return jnp.broadcast_to(v[:, spot : spot + 1], (NZ, 128))

        edge_w = [jnp.zeros((NZ, 128), F32)] * 2
        edge_d = [jnp.zeros((NZ, 128), F32)] * 2
        k_index = levels()
        east_k = []
        if first_step:
            turned = [[pltpu.roll(cin[2 + side, g], lax.rem(128 - third, 128), 1) for g in range(2)] for side in range(2)]
        for y in range(TY):
            g, base = y // 4, 32 * (y % 4)
            if first_step:
                def column(side, slot):
                    v = turned[side][g]
                    return jnp.broadcast_to(v[:, base + 3 * slot : base + 3 * slot + 1], (NZ, 128))

                u_west = column(0, 0)
                k_west = 0.05 + 0.15 * column(0, 4)
                k_east = 0.05 + 0.15 * column(1, 4)
            else:
                u_west = spread_lane(cin, 0, y, base + 30)
                k_west = spread_lane(cin, 0, y, base + 31)
                k_east = spread_lane(cin, 1, y, base + 31)
            east_k.append(k_east)
            k_here = jnp.broadcast_to(fx[4, y + 1, :, 0:1], (NZ, 128))
            m_here = jnp.where(k_index < nb_ref[0, y + 8 : y + 9, 0:1], 1.0, 0.0)
            m_west = jnp.where(k_index < nb_ref[2, y + 8 : y + 9, 0:1], 1.0, 0.0)
            both = m_here * m_west
            group = (lane >= base) & (lane < base + 32)
            edge_w[g] = jnp.where(group, DT * both * u_west, edge_w[g])
            edge_d[g] = jnp.where(group, DT * both * (k_west + k_here), edge_d[g])
        packed = []
        for g in range(2):
            half = slice(g * 128, g * 128 + 128)
            q255, q1 = by_parity(mine_b[:, half], mine_a[:, half])
            d_1, low_west, high_west, half_east, high_east = column_ends(cin[0, g], cin[1, g], q1, q255)
            w = edge_w[g]
            flux = w * jnp.where(w > 0, low_west, high_west) - edge_d[g] * d_1
            packed.append((d_1, flux, half_east, high_east))
        for g in range(2):
            for n in range(4):
                cin[4 + n, g] = packed[g][n]

        for y in range(-1, TY):
            m, m_n = wet(nb_ref, 0, y), wet(nb_ref, 0, y + 1)
            v, k, k_n = get("V", y), get("K", y), get("K", y + 1)
            both = [m[h] * m_n[h] for h in range(2)]
            put(wy, (y + 1,), [DT * both[h] * v[h] for h in range(2)])
            put(dy, (y + 1,), [DT * both[h] * (k[h] + k_n[h]) for h in range(2)])
            if y < 0:
                continue
            m_e = wet(nb_ref, 1, y)
            both = [m[h] * m_e[h] for h in range(2)]
            u = get("U", y)
            k_e = east_of(k, east_k[y], last)
            put(wx, (y,), [DT * both[h] * u[h] for h in range(2)])
            put(dx, (y,), [DT * both[h] * (k[h] + k_e[h]) for h in range(2)])
            inner = jnp.where(k_index < NZ - 1.0, 0.5 * DT, 0.0)
            put(dz, (y,), [inner * (m[h] * level_down(m[h])) * (k[h] + level_down(k[h])) for h in range(2)])
            put(mm, (y,), m)

        if first_step:
            pltpu.make_async_copy(z_hbm.at[pl.ds(0, NC)], lowq, sems.at[6]).wait()
            pltpu.make_async_copy(z_hbm.at[pl.ds(0, NC)], highq, sems.at[7]).wait()

        def tracer(c, carry):
            if first_step:
                for copy in band(c):
                    copy().wait()
                packs = [packed_out[n] for n in range(4)]
                slot = lax.shift_right_arithmetic(lane - 2 * c, 1)
            q = {y: halves(state_ref[c, y]) for y in range(TY)}
            for y in range(2):
                if first_step:
                    low, high = lowq[c, y], highq[c, y]
                else:
                    low = jnp.where(odd, pair_a[c, y], pair_b[c, y])
                    high = jnp.where(odd, pair_b[c, y], pair_a[c, y])
                q[y - 2], q[y + TY] = halves(low), halves(high)
            p = {y: [0.5 * v for v in q[y]] for y in q}
            d = {y: [p[y + 1][h] - p[y][h] for h in range(2)] for y in range(-2, TY + 1)}
            s = {y: [minmod(d[y][h], d[y - 1][h]) for h in range(2)] for y in range(-1, TY + 1)}
            north = {}
            for y in range(-1, TY):
                w, f = halves(wy[y + 1]), halves(dy[y + 1])
                north[y] = [
                    w[h] * jnp.where(w[h] > 0, q[y][h] + s[y][h], q[y + 1][h] - s[y + 1][h]) - f[h] * d[y][h]
                    for h in range(2)
                ]
            for y in range(TY):
                g, spot = y // 4, 32 * (y % 4) + 2 * c
                to_first, to_last = 127 - spot, 126 - spot
                if first_step:
                    dxx, low, high_e = [halves(slopes[n, c, y]) for n in range(3)]
                else:
                    dxx, low, high_e = column_slopes(
                        q[y], p[y], pltpu.roll(cin[6, g], to_last, 1), pltpu.roll(cin[4, g], to_first, 1),
                        pltpu.roll(cin[7, g], to_last, 1), first, last,
                    )
                w, f = halves(wx[y]), halves(dx[y])
                flux = [w[h] * jnp.where(w[h] > 0, low[h], high_e[h]) - f[h] * dxx[h] for h in range(2)]
                flux_w = west_of(flux, pltpu.roll(cin[5, g], to_first, 1), first)
                base, z, m = halves(racc[c, y]), halves(dz[y]), halves(mm[y])
                new = []
                for h in range(2):
                    down = z[h] * (level_down(q[y][h]) - q[y][h])
                    vert = down - pltpu.roll(down, 1, 0)
                    new.append(m[h] * (base[h] + (flux_w[h] - flux[h]) + (north[y - 1][h] - north[y][h]) + vert))
                if first_step:
                    put(out_ref, (c, y), new)
                    here = slot == 16 * (y % 4)
                    packs[g] = jnp.where(here, pltpu.roll(new[0], spot, 1), packs[g])
                    packs[2 + g] = jnp.where(here, pltpu.roll(new[1], lax.rem(spot + 2, 128), 1), packs[2 + g])
                else:
                    for h in range(2):
                        out_ref[h, c, pl.ds(y, NZ, stride=TY), :] = new[h]
            if first_step:
                for n in range(4):
                    packed_out[n] = packs[n]
            else:
                for h in range(2):
                    leave(c, h).start()
            return carry

        if first_step:
            packed_out[...] = jnp.zeros((4, NZ, 128), F32)
        lax.fori_loop(0, NC, tracer, 0)

        if first_step:
            def flow(y, carry):
                out = flow_update(get, lambda f, row, side: flow_edges(f, y, side, third), nb_ref, y, ("U", "V", "rho", "E")[:2] + ("rho", "E"))
                put(flow_out, (0, y), out["U"])
                put(flow_out, (1, y), out["V"])
                put(flow_out, (2, y), [0.05 + 0.15 * e for e in out["E"]])
                return carry

            lax.fori_loop(0, TY, flow, 0)

            def edge_rows(c, carry):
                for j in range(2):
                    top, base = out_ref[c, TY - 2 + j], out_ref[c, j]
                    pair_a[c, j] = jnp.where(odd, base, top)
                    pair_b[c, j] = jnp.where(odd, top, base)
                return carry

            lax.fori_loop(0, NC, edge_rows, 0)
            for j, f in ((0, 1), (1, 2)):
                top, base = flow_out[f, TY - 1], flow_out[f, 0]
                pair_a[NC, j] = jnp.where(odd, base, top)
                pair_b[NC, j] = jnp.where(odd, top, base)
            for y in range(TY):
                for h in range(2):
                    green[h, NZ * y : NZ * y + NZ, :] = out_ref[2, y, :, h * 128 : h * 128 + 128]
            shade(lambda h, k: green[h, pl.ds(k, TY, stride=NZ), :], sun2, heat2)
            for y in range(TY):
                rows = slice(NZ * y, NZ * y + NZ)
                put(sun_out, (y,), [sun2[h, rows] for h in range(2)])
                put(heat_ref, (y,), [heat2[h, rows] for h in range(2)])

    if not first_step:
        for h in range(2):
            leave(slice(None), h).wait()
    if first_step:
        @pl.when(section == 0)
        def _():
            give_columns(pack_columns(lambda c, y: halves(out_ref[c, y]), 1), first_out, second_out)

        @pl.when(section > 0)
        def _():
            tiles = [packed_out[n] for n in range(4)]
            for y in range(TY):
                g, base = y // 4, 32 * (y % 4)
                k0 = jnp.broadcast_to(flow_out[2, y, :, 0:1], (NZ, 128))
                u255 = jnp.broadcast_to(flow_out[0, y, :, 255:256], (NZ, 128))
                k255 = jnp.broadcast_to(flow_out[2, y, :, 255:256], (NZ, 128))
                tiles[g] = jnp.where(lane == base + 31, k0, tiles[g])
                tiles[2 + g] = jnp.where(lane == base + 30, u255, tiles[2 + g])
                tiles[2 + g] = jnp.where(lane == base + 31, k255, tiles[2 + g])
            give_columns(tiles, first_out, second_out)


def heat_kernel(out_any, heat1, heat2, heat3, nb_ref, out_hbm, warm_ref, sems):
    section, even, _ = place()

    @pl.when(section == 0)
    def _():
        def moves(back):
            pairs = [(out_hbm.at[pl.ds(6, 3), :, pl.ds(128 * h, 128)], warm_ref.at[h]) for h in range(2)]
            return [pltpu.make_async_copy(*(p[::-1] if back else p), sems.at[h]) for h, p in enumerate(pairs)]

        for move in moves(False):
            move.start()
        for move in moves(False):
            move.wait()

        def body(y, carry):
            ends = [jnp.where(even, heat1[y], heat3[y]), heat2[y], jnp.where(even, heat3[y], heat1[y])]
            for t in range(3):
                m = wet(nb_ref, 0, TY * t + y)
                warm = halves(ends[t])
                for h in range(2):
                    spot = (h, t, pl.ds(y, NZ, stride=TY), slice(None))
                    warm_ref[spot] = warm_ref[spot] + m[h] * (DT * 3.0 * warm[h])
            return carry

        lax.fori_loop(0, TY, body, 0)
        for move in moves(True):
            move.start()
        for move in moves(True):
            move.wait()


def sds(*shape):
    return jax.ShapeDtypeStruct(shape, F32)


def vmem(n):
    return [pl.BlockSpec(memory_space=pltpu.VMEM)] * n


def step_scratch(first_step):
    row = (NZ, NX)
    scratch = []
    if first_step:
        scratch = [pltpu.VMEM((NC, TY) + row, F32)] * 2 + [pltpu.VMEM((16, 2) + row, F32)]
        scratch += [pltpu.VMEM((NC, 2) + row, F32)] * 2
        scratch += [pltpu.VMEM((9,) + row, F32), pltpu.VMEM((3, 40, NX), F32)] + [pltpu.VMEM(row, F32)] * 4
        scratch += [pltpu.VMEM((4, NZ, 128), F32), pltpu.VMEM((3, NC, TY) + row, F32)]
    scratch += [
        pltpu.VMEM((5, 26) + row, F32),
        pltpu.VMEM((TY,) + row, F32),
        pltpu.VMEM((TY,) + row, F32),
        pltpu.VMEM((TY + 1,) + row, F32),
        pltpu.VMEM((TY + 1,) + row, F32),
        pltpu.VMEM((TY,) + row, F32),
        pltpu.VMEM((TY,) + row, F32),
        pltpu.VMEM((8, 2, NZ, 128), F32),
    ]
    if first_step:
        scratch += [pltpu.VMEM((2, TY * NZ, 128), F32)] * 3
        return scratch + [pltpu.SemaphoreType.DMA((9,)), pltpu.SemaphoreType.DMA((3, NC))]
    return scratch + [pltpu.VMEM((2, NC, NZ * TY, 128), F32), pltpu.SemaphoreType.DMA((2,))]


def pairs_of(mesh):
    ns, ngy, ngx = (mesh.shape[a] for a in AXES)

    def at(s, g, x):
        return (s * ngy + g) * ngx + x

    cross, ocean, chain, swaps, heat = [], ([], []), ([], []), ([], []), {1: [], 2: [], 3: []}
    for x in range(ngx):
        for g in range(ngy):
            order = (1, 2, 3) if g % 2 == 0 else (3, 2, 1)
            for t, (a, b) in enumerate(zip(order, order[1:])):
                chain[(3 * g + t) % 2].append((at(a, g, x), at(b, g, x)))
            if g + 1 < ngy:
                cross.append((at(order[2], g, x), at(order[2], g + 1, x)))
                chain[(3 * g + 2) % 2].append(cross[-1])
                ocean[g % 2].append((at(0, g, x), at(0, g + 1, x)))
            for s in heat:
                heat[s].append((at(s, g, x), at(0, g, x)))
            if x + 1 < ngx:
                swaps[x % 2].extend((at(s, g, x), at(s, g, x + 1)) for s in range(ns))
    chain = [a + b for a, b in zip(chain, ocean)]
    return cross + turn(cross), *[[p + turn(p) for p in pairs] for pairs in (ocean, chain, swaps)], heat


def turn(pairs):
    return [(b, a) for a, b in pairs]


def solution(mesh):
    cross, ocean, chain, swaps, heat_pairs = pairs_of(mesh)

    def send(value, pairs):
        return lax.ppermute(value, AXES, pairs)

    def program(fields, sea_mask, bottom, reaction, growth):
        x = fields.reshape(NC, NZ * TY, NX)
        row = (NZ, NX)
        block = sds(NC, TY, *row)
        halo = sds(16, 2, *row)
        anywhere = pl.BlockSpec(memory_space=pltpu.HBM)
        loose = pl.BlockSpec(memory_space=pl.ANY)
        weights = jax.ShapeDtypeStruct((NC * NZ, NC * NZ), BF16)

        def call(body, out_shape, in_specs, out_specs, scratch=(), cost=None, limit=VMEM_LIMIT):
            def placed(shape, spec):
                return pltpu.HBM(shape.shape, shape.dtype) if spec is anywhere else shape

            if isinstance(out_specs, tuple):
                out_shape = tuple(placed(*pair) for pair in zip(out_shape, out_specs))
            kernel = pl.pallas_call(
                body,
                out_shape=out_shape,
                in_specs=in_specs,
                out_specs=out_specs,
                scratch_shapes=list(scratch),
                compiler_params=pltpu.CompilerParams(vmem_limit_bytes=limit),
                cost_estimate=cost,
            )

            def run(*operands):
                return kernel(*[
                    pltpu.with_memory_space_constraint(v, pltpu.HBM) if spec is anywhere else v
                    for v, spec in zip(operands, in_specs)
                ])

            return run

        x_scratch = pltpu.VMEM((2, NC, NZ * TY, 128), F32)
        rows = pltpu.VMEM((2, TY * NZ, 128), F32)
        a_out, z, oa, ob = call(
            send_kernel, (sds(4, 16, 2, *row), halo, sds(5, *row), sds(5, *row)), [anywhere],
            (anywhere,) * 2 + tuple(vmem(2)),
            [x_scratch, pltpu.VMEM((16, 2) + row, F32), pltpu.VMEM((16, 2) + row, F32), pltpu.VMEM((3, 16, 2) + row, F32),
             rows, rows, pltpu.SemaphoreType.DMA((5,)), pltpu.SemaphoreType.DMA((2, PARTS))],
        )(x)
        recv = lax.all_to_all(a_out, "section", split_axis=0, concat_axis=0, tiled=True)
        oa_in, ob_in = send(oa, ocean[0]), send(ob, ocean[1])
        mine_a, mine_b, ends = call(
            column_kernel, (sds(*row), sds(*row), sds(2, NC, *row)), [anywhere], tuple(vmem(3)),
            [x_scratch, pltpu.SemaphoreType.DMA((2, PARTS))],
        )(x)
        first_in, second_in = send(mine_a, swaps[0]), send(mine_b, swaps[1])
        z_in = send(z, cross)
        rims = call(rim_kernel, tuple([sds(9, *row)] * 3), vmem(5), tuple(vmem(3)))(ends, oa_in, ob_in, first_in, second_in)
        rims = [send(r, turn(heat_pairs[s])) for s, r in zip((1, 2, 3), rims)]
        react_cost = pl.CostEstimate(flops=6 * 240 * 240 * 2048, bytes_accessed=2 * NC * TY * NZ * NX * 4, transcendentals=0)
        window = pltpu.VMEM((5, TY, 512), jnp.int32)
        whole = pltpu.VMEM((NC, TY) + row, F32)
        square = pltpu.VMEM((NC * NZ, NC * NZ), BF16)
        state, grown, slopes, w_high, w_low, nb = call(
            functools.partial(react_kernel, True),
            (block, block, sds(3, NC, TY, *row), weights, weights, sds(3, 40, NX)),
            [anywhere] * 3 + vmem(6), (anywhere,) * 6,
            [pltpu.VMEM((3, NC, TY) + row, F32), pltpu.VMEM((3, 2, NZ, 128), F32), x_scratch, whole, whole, square, square, pltpu.VMEM((3, 40, NX), F32), pltpu.VMEM((TY,) + row, F32), window, window,
             rows, rows, pltpu.SemaphoreType.DMA((2, PARTS)), pltpu.SemaphoreType.DMA((2, 5, 3)), pltpu.SemaphoreType.DMA((6,))],
            cost=react_cost, limit=60 * 1024 * 1024,
        )(x, sea_mask, bottom, reaction, growth.reshape(1, NC), first_in, second_in, mine_a, mine_b)
        state1, pair_a, pair_b, next_a, next_b, heat1, sun1, flow1 = call(
            functools.partial(step_kernel, True),
            (block, halo, halo, sds(*row), sds(*row), sds(TY, *row), sds(TY, *row), sds(3, TY, *row)),
            [anywhere] * 3 + [loose] * 2 + [anywhere] * 4 + [loose] * 3 + [anywhere] * 3, tuple(vmem(8)), step_scratch(True),
        )(state, grown, slopes, recv, z_in, oa_in, ob_in, first_in, second_in, *rims, nb, mine_a, mine_b)
        pair_a_in, pair_b_in = send(pair_a, chain[0]), send(pair_b, chain[1])
        first1_in, second1_in = send(next_a, swaps[0]), send(next_b, swaps[1])
        heats = [send(heat1, heat_pairs[s]) for s in (1, 2, 3)]
        grown1 = call(
            functools.partial(react_kernel, False), block, vmem(4), vmem(1)[0], cost=react_cost,
        )(state1, sun1, w_high, w_low)
        out = call(
            functools.partial(step_kernel, False), sds(NC, NZ * TY, NX), vmem(10), anywhere, step_scratch(False),
        )(state1, grown1, pair_a_in, pair_b_in, first1_in, second1_in, nb, next_a, next_b, flow1)
        out = pl.pallas_call(
            heat_kernel,
            out_shape=sds(NC, NZ * TY, NX),
            in_specs=[anywhere] + vmem(4),
            out_specs=anywhere,
            scratch_shapes=[pltpu.VMEM((2, 3, NZ * TY, 128), F32), pltpu.SemaphoreType.DMA((2,))],
            input_output_aliases={0: 0},
            compiler_params=pltpu.CompilerParams(vmem_limit_bytes=VMEM_LIMIT),
            name="heating",
        )(out, *heats, nb)
        return out.reshape(1, NC, NZ, TY, NX)

    return jax.shard_map(
        program,
        mesh=mesh,
        in_specs=(P("section", None, None, "gy", "gx"), P(), P(), P(), P()),
        out_specs=P("section", None, None, "gy", "gx"),
        check_vma=False,
    )
```

```python
import functools

import jax
import jax.numpy as jnp
from jax import lax
from jax.experimental import pallas as pl
from jax.experimental.pallas import tpu as pltpu
from jax.sharding import PartitionSpec as P


AXES = ("section", "gy", "gx")
NC, NZ, TY, NX = 15, 16, 8, 256
DT = 0.2
F32 = jnp.float32
BF16 = jnp.bfloat16
VMEM_LIMIT = 24 * 1024 * 1024


def minmod(a, b):
    return jnp.maximum(jnp.minimum(a, b), jnp.minimum(jnp.maximum(a, b), 0.0))


def lanes():
    return lax.broadcasted_iota(jnp.int32, (NZ, 128), 1)


def levels():
    return lax.broadcasted_iota(jnp.int32, (NZ, 128), 0).astype(F32)


def halves(row):
    return row[:, :128], row[:, 128:]


def place():
    section = lax.axis_index("section")
    tile = lax.axis_index("gy")
    even = tile % 2 == 0
    third = jnp.where(even, section - 1, 3 - section)
    return section, even, third


def shade(read, sun_ref, heat_ref):
    for h in range(2):
        depth = jnp.zeros((TY, 128), F32)
        for k in range(NZ):
            chlorophyll = jnp.maximum(read(h, k), 0.0)
            sunlight = jnp.exp(-depth)
            depth = depth + (0.05 + 0.1 * chlorophyll)
            sun_ref[h, pl.ds(k, TY, stride=NZ), :] = sunlight
            heat_ref[h, pl.ds(k, TY, stride=NZ), :] = 0.1 * chlorophyll * sunlight


def pack_columns(read, per, loop=functools.partial(lax.fori_loop, 0, NC)):
    lane = lanes()

    def body(c, packs):
        packs = list(packs)
        for y in range(TY):
            left, right = read(c, y)
            spot = 32 * (y % 4) + per * c
            here = (lane >= spot) & (lane < spot + per)
            g = y // 4
            packs[g] = jnp.where(here, pltpu.roll(left, spot, 1), packs[g])
            packs[2 + g] = jnp.where(here, pltpu.roll(right, lax.rem(spot + per, 128), 1), packs[2 + g])
        return tuple(packs)

    zero = jnp.zeros((NZ, 128), F32)
    return loop(body, (zero,) * 4)


PARTS = 3


def load_block(x_hbm, x_ref, sems):
    size = NC // PARTS
    loads = [
        [
            pltpu.make_async_copy(
                x_hbm.at[pl.ds(size * i, size), :, pl.ds(128 * h, 128)], x_ref.at[h, pl.ds(size * i, size)], sems.at[h, i]
            )
            for h in range(2)
        ]
        for i in range(PARTS)
    ]
    for part in loads:
        for load in part:
            load.start()

    def wait(i):
        for load in loads[i]:
            load.wait()

    return wait


def over_parts(wait, body, carry):
    size = NC // PARTS
    for i in range(PARTS):
        wait(i)
        carry = lax.fori_loop(size * i, size * (i + 1), body, carry)
    return carry


def send_kernel(x_hbm, x1_hbm, x2_hbm, x3_hbm, z_hbm, oa_ref, ob_ref, x_ref, top_ref, base_ref, flow_ref, sun2, heat2, sems, loads):
    section, even, third = place()
    is_ocean = section == 0
    odd = chain_odd()
    wait = load_block(x_hbm, x_ref, loads)

    def to_section(target, source, part, sem, act):
        for n, out in ((1, x1_hbm), (2, x2_hbm), (3, x3_hbm)):
            @pl.when((section ^ target) == n)
            def _():
                act(pltpu.make_async_copy(source, out.at[part], sems.at[sem]))

    def start(copy):
        copy.start()

    def finish(copy):
        copy.wait()

    def turned(c, y):
        return [x_ref[h, c, pl.ds(y, NZ, stride=TY), :] for h in range(2)]

    @pl.when(is_ocean)
    def _():
        for i in range(PARTS):
            wait(i)
        for f in range(5):
            top, base = turned(3 * f + 2, TY - 1), turned(3 * f, 0)
            put(oa_ref, (f,), [jnp.where(odd, b, a) for a, b in zip(top, base)])
            put(ob_ref, (f,), [jnp.where(odd, a, b) for a, b in zip(top, base)])
        for t in range(3):
            def body(y, carry):
                i, j = lax.div(y, 2), lax.rem(y, 2)
                salt, warm = turned(9 + t, y), turned(6 + t, y)
                put(flow_ref, (t, i, j), turned(t, y))
                put(flow_ref, (t, 4 + i, j), turned(3 + t, y))
                put(flow_ref, (t, 8 + i, j), [0.8 * salt[h] - 0.2 * warm[h] for h in range(2)])
                put(flow_ref, (t, 12 + i, j), turned(12 + t, y))
                return carry

            lax.fori_loop(0, TY, body, 0)
        for act in (start, finish):
            for t in range(3):
                to_section(jnp.where(even, t + 1, 3 - t), flow_ref.at[t], slice(None), t, act)

    @pl.when(jnp.logical_not(is_ocean))
    def _():
        above = jnp.where(even, section + 1, section - 1)
        below = jnp.where(even, section - 1, section + 1)
        above = jnp.where((above < 1) | (above > 3), section, above)
        below = jnp.where((below < 1) | (below > 3), section, below)

        def body(c, carry):
            for j in range(2):
                put(top_ref, (c, j), turned(c, TY - 2 + j))
                put(base_ref, (c, j), turned(c, j))
            return carry

        wait(0)
        shade(lambda h, k: x_ref[h, 2, TY * k : TY * k + TY, :], sun2, heat2)
        for y in range(TY):
            rows = slice(NZ * y, NZ * y + NZ)
            put(flow_ref, (0, y // 2, y % 2), [heat2[h, rows] for h in range(2)])
        to_section(0, flow_ref.at[0, pl.ds(0, 4)], pl.ds(0, 4), 4, start)
        over_parts(lambda i: wait(i) if i else None, body, 0)
        to_section(above, top_ref, slice(None), 0, start)
        to_section(below, base_ref, slice(None), 1, start)

        @pl.when(third == 2)
        def _():
            pltpu.make_async_copy(top_ref, z_hbm, sems.at[2]).start()

        @pl.when(third == 0)
        def _():
            pltpu.make_async_copy(base_ref, z_hbm, sems.at[2]).start()

        to_section(above, top_ref, slice(None), 0, finish)
        to_section(below, base_ref, slice(None), 1, finish)
        to_section(0, flow_ref.at[0, pl.ds(0, 4)], pl.ds(0, 4), 4, finish)

        @pl.when(third != 1)
        def _():
            pltpu.make_async_copy(top_ref, z_hbm, sems.at[2]).wait()


def chain_odd():
    section, _, third = place()
    tile = lax.axis_index("gy")
    return lax.rem(jnp.where(section == 0, tile, 3 * tile + third), 2) == 1


def by_parity(first_in, second_in):
    odd = lax.rem(lax.axis_index("gx"), 2) == 1
    return jnp.where(odd, first_in, second_in), jnp.where(odd, second_in, first_in)


def give_columns(packs, first_ref, second_ref):
    odd = lax.rem(lax.axis_index("gx"), 2) == 1
    for g in range(2):
        half = slice(g * 128, g * 128 + 128)
        first_ref[:, half] = jnp.where(odd, packs[g], packs[2 + g])
        second_ref[:, half] = jnp.where(odd, packs[2 + g], packs[g])


def column_kernel(x_hbm, first_ref, second_ref, ends_ref, x_ref, sems):
    is_ocean = lax.axis_index("section") == 0
    wait = load_block(x_hbm, x_ref, sems)

    def read(c, y):
        return [x_ref[h, c, pl.ds(y, NZ, stride=TY), :] for h in range(2)]

    loop = functools.partial(over_parts, wait)
    give_columns(pack_columns(read, jnp.where(is_ocean, 1, 2), loop), first_ref, second_ref)

    @pl.when(is_ocean)
    def _():
        def body(c, carry):
            put(ends_ref, (0, c), read(c, 0))
            put(ends_ref, (1, c), read(c, TY - 1))
            return carry

        lax.fori_loop(0, NC, body, 0)


def cut_depths(sea_hbm, bottom_hbm, nb_ref, sea_buf, bottom_buf, wins):
    section, _, third = place()
    tile, column = lax.axis_index("gy"), lax.axis_index("gx")
    is_ocean = section == 0
    group = jnp.where(is_ocean, 3 * tile, 3 * tile + third)
    n_groups, n_cols = sea_hbm.shape[0] // TY, sea_hbm.shape[1]
    pieces = ((-128, 128), (0, 256), (256, 128))
    copies = []
    for n, (hbm, buf) in enumerate(((sea_hbm, sea_buf), (bottom_hbm, bottom_buf))):
        for g in range(5):
            row = pl.multiple_of(jnp.clip(group + g - 1, 0, n_groups - 1) * TY, TY)
            for i, (offset, width) in enumerate(pieces):
                col = pl.multiple_of(jnp.clip(column * NX + offset, 0, n_cols - width), 128)
                copies.append(
                    pltpu.make_async_copy(
                        hbm.at[pl.ds(row, TY), pl.ds(col, width)],
                        buf.at[g, :, pl.ds(offset + 128, width)],
                        wins.at[n, g, i],
                    )
                )
    for copy in copies:
        copy.start()

    def finish():
        for copy in copies:
            copy.wait()
        lane = lax.broadcasted_iota(jnp.int32, (TY, 128), 1)
        for g in range(5):
            inside = (group + g - 1 >= 0) & (group + g - 1 < n_groups)
            valid = (column > 0, True, True, column * NX + NX < n_cols)
            depth = []
            for i in range(4):
                part = slice(128 * i, 128 * i + 128)
                value = (sea_buf[g, :, part] * bottom_buf[g, :, part]).astype(F32)
                depth.append(jnp.where(inside & valid[i], value, 0.0))
            rows = slice(TY * g, TY * g + TY)
            for h in range(2):
                cols = slice(128 * h, 128 * h + 128)
                nb_ref[0, rows, cols] = depth[1 + h]
                nb_ref[1, rows, cols] = jnp.where(lane == 127, pltpu.roll(depth[2 + h], 127, 1), pltpu.roll(depth[1 + h], 127, 1))
                nb_ref[2, rows, cols] = jnp.where(lane == 0, pltpu.roll(depth[h], 1, 1), pltpu.roll(depth[1 + h], 1, 1))

    return finish


def build_weights(reaction_ref, growth_ref, wh_ref, wl_ref):
    size = NC * NZ
    matrix = reaction_ref[...] * growth_ref[...]
    level_of = lax.rem(lax.broadcasted_iota(jnp.int32, (size, size), 0), NZ)
    same = level_of == lax.rem(lax.broadcasted_iota(jnp.int32, (size, size), 1), NZ)
    up = lax.div(lax.broadcasted_iota(jnp.int32, (size, NC), 0), NZ) == lax.broadcasted_iota(jnp.int32, (size, NC), 1)
    across = lax.broadcasted_iota(jnp.int32, (NC, size), 0) == lax.div(lax.broadcasted_iota(jnp.int32, (NC, size), 1), NZ)
    up = jnp.where(up, 1.0, 0.0).astype(BF16)
    across = jnp.where(across, 1.0, 0.0).astype(BF16)
    high = matrix.astype(BF16)
    low = (matrix - high.astype(F32)).astype(BF16)
    for part, out in ((high, wh_ref), (low, wl_ref)):
        wide = jnp.dot(part, across, preferred_element_type=F32).astype(BF16)
        full = jnp.dot(up, wide, preferred_element_type=F32)
        out[...] = jnp.where(same, full, 0.0).astype(BF16)


def react_kernel(build, *refs):
    if build:
        (x_hbm, sea_hbm, bottom_hbm, reaction_ref, growth_ref, first_in, second_in, mine_a, mine_b,
         state_ref, out_ref, slopes, wh_ref, wl_ref, nb_ref,
         ends, x_ref, sun_ref, sea_buf, bottom_buf, sun2, heat2, sems, wins) = refs
        finish = cut_depths(sea_hbm, bottom_hbm, nb_ref, sea_buf, bottom_buf, wins)
        wait = load_block(x_hbm, x_ref, sems)

        def turn(c, carry):
            for y in range(TY):
                put(state_ref, (c, y), [x_ref[h, c, pl.ds(y, NZ, stride=TY), :] for h in range(2)])
            return carry

        over_parts(wait, turn, 0)
        finish()
    else:
        state_ref, sun_ref, wh_ref, wl_ref, out_ref = refs

    @pl.when(lax.axis_index("section") > 0)
    def _():
        if build:
            shade(lambda h, k: x_ref[h, 2, TY * k : TY * k + TY, :], sun2, heat2)
            for y in range(TY):
                put(sun_ref, (y,), [sun2[h, NZ * y : NZ * y + NZ] for h in range(2)])
            build_weights(reaction_ref, growth_ref, wh_ref, wl_ref)

        def react(y, carry):
            q = state_ref[:, y]
            x = jnp.maximum(q, 0.0).reshape(NC * NZ, NX)
            x_high = x.astype(BF16)
            x_low = (x - x_high.astype(F32)).astype(BF16)
            total = jnp.dot(wh_ref[...], x_high, preferred_element_type=F32)
            total = total + jnp.dot(wh_ref[...], x_low, preferred_element_type=F32)
            total = total + jnp.dot(wl_ref[...], x_high, preferred_element_type=F32)
            nutrient = jnp.maximum(q[0], 0.0)
            uptake = DT * (nutrient / (nutrient + 0.5) * sun_ref[y])
            out_ref[:, y] = q + total.reshape(NC, NZ, NX) * uptake[None]
            return carry

        lax.fori_loop(0, TY, react, 0)
        if build:
            lane = lanes()
            first, last = lane == 0, lane == 127
            for g in range(2):
                half = slice(g * 128, g * 128 + 128)
                west, east = by_parity(first_in[:, half], second_in[:, half])
                mine_east, mine_west = by_parity(mine_b[:, half], mine_a[:, half])
                d_1, _, _, half_east, high_east = column_ends(west, east, mine_west, mine_east)
                ends[0, g], ends[1, g], ends[2, g] = d_1, half_east, high_east

            def slope(c, carry):
                for y in range(TY):
                    g, spot = y // 4, 32 * (y % 4) + 2 * c
                    to_first, to_last = 127 - spot, 126 - spot
                    q = halves(state_ref[c, y])
                    parts = column_slopes(
                        q, [0.5 * v for v in q], pltpu.roll(ends[1, g], to_last, 1), pltpu.roll(ends[0, g], to_first, 1),
                        pltpu.roll(ends[2, g], to_last, 1), first, last,
                    )
                    for n, part in enumerate(parts):
                        put(slopes, (n, c, y), part)
                return carry

            lax.fori_loop(0, NC, slope, 0)


def rim_kernel(ends_ref, oa_ref, ob_ref, first_ref, second_ref, r1_ref, r2_ref, r3_ref):
    section, even, _ = place()
    odd = chain_odd()

    @pl.when(section == 0)
    def _():
        def row(t, f, y):
            if y < 0:
                return jnp.where(odd, oa_ref[f], ob_ref[f]) if t == 0 else ends_ref[1, 3 * f + t - 1]
            return jnp.where(odd, ob_ref[f], oa_ref[f]) if t == 2 else ends_ref[0, 3 * f + t + 1]

        def fill(out, t):
            for n, y in ((0, -1), (4, TY)):
                out[n] = row(t, 0, y)
                out[n + 1] = row(t, 1, y)
                out[n + 2] = 0.8 * row(t, 3, y) - 0.2 * row(t, 2, y)
                out[n + 3] = row(t, 4, y)
            for g in range(2):
                half = slice(g * 128, g * 128 + 128)
                west, east = by_parity(first_ref[:, half], second_ref[:, half])
                out[8, :, half] = west + pltpu.roll(east, 16, 1)

        fill(r2_ref, 1)

        @pl.when(even)
        def _():
            fill(r1_ref, 0)
            fill(r3_ref, 2)

        @pl.when(jnp.logical_not(even))
        def _():
            fill(r1_ref, 2)
            fill(r3_ref, 0)


def wet(nb_ref, shift, y):
    k = levels()
    row = nb_ref[shift, pl.ds(y + 8, 1), :]
    return tuple(jnp.where(k < row[:, h * 128 : h * 128 + 128], 1.0, 0.0) for h in range(2))


def east_of(pair, edge, last):
    a, b = (pltpu.roll(v, 127, 1) for v in pair)
    return jnp.where(last, b, a), jnp.where(last, edge, b)


def west_of(pair, edge, first):
    a, b = (pltpu.roll(v, 1, 1) for v in pair)
    return jnp.where(first, edge, a), jnp.where(first, a, b)


def level_down(v):
    a, b = (pltpu.roll(part, 7, 0) for part in (v[:8], v[8:]))
    end = lax.broadcasted_iota(jnp.int32, (8, 128), 0) == 7
    return jnp.concatenate([jnp.where(end, b, a), b], axis=0)


def level_up(v):
    a, b = (pltpu.roll(part, 1, 0) for part in (v[:8], v[8:]))
    start = lax.broadcasted_iota(jnp.int32, (8, 128), 0) == 0
    return jnp.concatenate([jnp.where(start, b, a), jnp.where(start, a, b)], axis=0)


def flow_update(get, edge, nb_ref, y, names):
    lane = lanes()
    first, last = lane == 0, lane == 127
    centre, east, west = (wet(nb_ref, s, y) for s in range(3))
    north, south = wet(nb_ref, 0, y + 1), wet(nb_ref, 0, y - 1)
    here = {f: get(f, y) for f in names}
    around = {}
    for f in names:
        if f == "E":
            continue
        around[f] = (
            east_of(here[f], edge(f, y, 1), last),
            west_of(here[f], edge(f, y, 0), first),
            get(f, y + 1),
            get(f, y - 1),
        )
    out = {f: [] for f in names}
    for h in range(2):
        m = centre[h]
        sides = (east[h], west[h], north[h], south[h])

        def lap(f):
            c = here[f][h]
            total = 0.0
            for w, v in zip(sides, around[f]):
                total = total + w * (v[h] - c)
            return m * total

        u, v, e = here["U"][h], here["V"][h], here["E"][h]
        if "T" in names:
            rho = 0.8 * here["S"][h] - 0.2 * here["T"][h]
            near = [0.8 * s[h] - 0.2 * t[h] for s, t in zip(around["S"], around["T"])]
        else:
            rho = here["rho"][h]
            near = [r[h] for r in around["rho"]]
        grad_x = 0.5 * (sides[0] * (near[0] - rho) + sides[1] * (rho - near[1]))
        grad_y = 0.5 * (sides[2] * (near[2] - rho) + sides[3] * (rho - near[3]))
        out["U"].append(m * (u + DT * (0.5 * v - 0.5 * grad_x + 0.15 * lap("U") - 0.1 * u)))
        out["V"].append(m * (v + DT * (-0.5 * u - 0.5 * grad_y + 0.15 * lap("V") - 0.1 * v)))
        inner = jnp.where(levels() < NZ - 1.0, 1.0, 0.0)
        open_below = m * level_down(m) * inner
        du, dv = level_down(u) - u, level_down(v) - v
        shear = (du * du + dv * dv) * open_below
        out["E"].append(m * (e + DT * (0.5 * shear - 0.5 * e)))
        if "T" in names:
            out["T"].append(here["T"][h] * m + m * (DT * (0.15 * lap("T"))))
            out["S"].append(m * (here["S"][h] + DT * (0.15 * lap("S"))))
    return out


def put(ref, index, pair):
    ref[index + (slice(None), slice(0, 128))] = pair[0]
    ref[index + (slice(None), slice(128, 256))] = pair[1]


def column_edges(right_in, left_in):
    slot = {"U": 0, "V": 1, "T": 2, "S": 3, "E": 4}

    def edge(name, y, side, third):
        if name == "rho":
            return 0.8 * edge("S", y, side, third) - 0.2 * edge("T", y, side, third)
        ref = (right_in, left_in)[side]
        spot = 32 * lax.rem(y, 4) + 3 * slot[name] + third
        target = 0 if side == 0 else 127
        return pltpu.roll(ref[lax.div(y, 4)], lax.rem(target - spot + 256, 128), 1)

    return edge


def column_ends(west, east, mine_west, mine_east):
    q_1, q1, q255, q257 = west, mine_west, mine_east, east
    q_2, q0, q256 = pltpu.roll(q_1, 1, 1), pltpu.roll(q1, 1, 1), pltpu.roll(q257, 1, 1)
    d_2, d_1, d0 = 0.5 * (q_1 - q_2), 0.5 * (q0 - q_1), 0.5 * (q1 - q0)
    h_1, h0 = minmod(d_1, d_2), minmod(d0, d_1)
    high_east = q256 - minmod(0.5 * (q257 - q256), 0.5 * (q256 - q255))
    return d_1, q_1 + h_1, q0 - h0, 0.5 * q256, high_east


def column_slopes(q, p, half_east, d_west, high_east, first, last):
    p_e = east_of(p, half_east, last)
    d = [p_e[h] - p[h] for h in range(2)]
    d_w = west_of(d, d_west, first)
    slope = [minmod(d[h], d_w[h]) for h in range(2)]
    low = [q[h] + slope[h] for h in range(2)]
    return d, low, east_of([q[h] - slope[h] for h in range(2)], high_east, last)


def step_kernel(first_step, *refs):
    if first_step:
        (state_ref, racc, slopes, x1_hbm, x2_hbm, x3_hbm, z_hbm, oa_hbm, ob_hbm, first_hbm, second_hbm, rim1, rim2, rim3, nb_hbm, mine_a_hbm, mine_b_hbm,
         out_ref, pair_a, pair_b, first_out, second_out, heat_ref, sun_out, flow_out,
         inflow, lowq, highq, rim, nb_ref, first_in, second_in, mine_a, mine_b,
         packed_out, fx, wx, dx, wy, dy, dz, mm, cin, sun2, heat2, green, sems) = refs
    else:
        (state_ref, racc, pair_a, pair_b, first_in, second_in, nb_ref, mine_a, mine_b, flow_ref,
         out_hbm,
         fx, wx, dx, wy, dy, dz, mm, cin, out_ref, sems) = refs
    section, even, third = place()
    odd = chain_odd()
    lane = lanes()
    first, last = lane == 0, lane == 127

    def leave(c, h):
        return pltpu.make_async_copy(out_ref.at[h, c], out_hbm.at[c, :, pl.ds(128 * h, 128)], sems.at[h])

    def copy_rows(n, target, source):
        def body(i, carry):
            target(i)[...] = source(i)[...]
            return carry

        lax.fori_loop(0, n, body, 0)

    if first_step:
        def fetch(source, target, sem):
            copy = pltpu.make_async_copy(source, target, sem)
            copy.start()
            return copy

        small = [
            fetch(source, target, sems.at[i])
            for i, (source, target) in enumerate(
                ((nb_hbm, nb_ref), (first_hbm, first_in), (second_hbm, second_in), (mine_a_hbm, mine_a), (mine_b_hbm, mine_b))
            )
        ]

        def from_section(source, part, target, sem):
            for n, swap in ((1, x1_hbm), (2, x2_hbm), (3, x3_hbm)):
                @pl.when((section ^ source) == n)
                def _():
                    fetch(swap.at[part], target, sem)

        @pl.when(section == 0)
        def _():
            for t in range(3):
                from_section(jnp.where(even, t + 1, 3 - t), pl.ds(0, 4), inflow.at[pl.ds(4 * t, 4)], sems.at[5])
            fetch(oa_hbm, highq.at[pl.ds(0, 5), 0], sems.at[6])
            fetch(ob_hbm, lowq.at[pl.ds(0, 5), 0], sems.at[7])

        @pl.when(section > 0)
        def _():
            from_section(0, slice(None), inflow, sems.at[5])
            for s, source in ((1, rim1), (2, rim2), (3, rim3)):
                @pl.when(section == s)
                def _():
                    fetch(source, rim, sems.at[8])
            below = jnp.where(even, section - 1, section + 1)
            above = jnp.where(even, section + 1, section - 1)
            for index, dest, sem in ((below, lowq, 6), (above, highq, 7)):
                end = (index < 1) | (index > 3)

                @pl.when(end)
                def _():
                    fetch(z_hbm.at[pl.ds(0, NC)], dest, sems.at[sem])

                @pl.when(jnp.logical_not(end))
                def _():
                    from_section(index, pl.ds(0, NC), dest, sems.at[sem])

        for copy in small:
            copy.wait()

    for g in range(2):
        half = slice(g * 128, g * 128 + 128)
        cin[0, g], cin[1, g] = by_parity(first_in[:, half], second_in[:, half])
    edges = column_edges(cin.at[0], cin.at[1])

    @pl.when(section == 0)
    def _():
        if first_step:
            pltpu.make_async_copy(x1_hbm.at[pl.ds(0, 12)], inflow.at[pl.ds(0, 12)], sems.at[5]).wait()
            pltpu.make_async_copy(oa_hbm, highq.at[pl.ds(0, 5), 0], sems.at[6]).wait()
            pltpu.make_async_copy(ob_hbm, lowq.at[pl.ds(0, 5), 0], sems.at[7]).wait()
        for f in range(5):
            from_a, from_b = (highq[f, 0], lowq[f, 0]) if first_step else (pair_a[f, 0], pair_b[f, 0])
            fx[f, 0] = jnp.where(odd, from_a, from_b)
            fx[f, 25] = jnp.where(odd, from_b, from_a)
            for t in range(3):
                copy_rows(TY, lambda i: fx.at[f, 1 + TY * t + i], lambda i: state_ref.at[3 * f + t, i])
        names = ("U", "V", "T", "S", "E")

        def get(f, y):
            return halves(fx[names.index(f), y + 1])

        for t in range(3):
            def body(y, carry):
                r = TY * t + y
                out = flow_update(get, lambda f, row, side: edges(f, y, side, t), nb_ref, r, names)
                if first_step:
                    m = wet(nb_ref, 0, r)
                    warm = halves(inflow[4 * t + lax.div(y, 2), lax.rem(y, 2)])
                    out["T"] = [out["T"][h] + m[h] * (DT * 3.0 * warm[h]) for h in range(2)]
                for f, name in enumerate(names):
                    if first_step:
                        put(out_ref, (3 * f + t, y), out[name])
                    else:
                        for h in range(2):
                            out_ref[h, 3 * f + t, pl.ds(y, NZ, stride=TY), :] = out[name][h]
                return carry

            lax.fori_loop(0, TY, body, 0)
            if not first_step:
                for f in range(5):
                    for h in range(2):
                        leave(3 * f + t, h).start()
        if first_step:
            for f in range(5):
                top, base = out_ref[3 * f + 2, TY - 1], out_ref[3 * f, 0]
                pair_a[f, 0] = jnp.where(odd, base, top)
                pair_b[f, 0] = jnp.where(odd, top, base)

    @pl.when(section > 0)
    def _():
        if first_step:
            pltpu.make_async_copy(x1_hbm, inflow, sems.at[5]).wait()
            pltpu.make_async_copy(rim1, rim, sems.at[8]).wait()
            for f in range(4):
                copy_rows(TY, lambda i: fx.at[f, 1 + i], lambda i: inflow.at[4 * f + lax.div(i, 2), lax.rem(i, 2)])
                fx[f, 0] = rim[f]
                fx[f, TY + 1] = rim[4 + f]
            for g in range(2):
                ends = rim[8, :, g * 128 : g * 128 + 128]
                cin[2, g] = ends
                cin[3, g] = pltpu.roll(ends, 112, 1)
            for y in range(TY + 2):
                fx[4, y] = 0.05 + 0.15 * fx[3, y]
        else:
            for f, place_of in enumerate((0, 1, 4)):
                copy_rows(TY, lambda i: fx.at[place_of, 1 + i], lambda i: flow_ref.at[f, i])
            fx[1, 0] = jnp.where(odd, pair_a[NC, 0], pair_b[NC, 0])
            fx[4, 0] = jnp.where(odd, pair_a[NC, 1], pair_b[NC, 1])
            fx[4, TY + 1] = jnp.where(odd, pair_b[NC, 1], pair_a[NC, 1])
        flow_edges = column_edges(cin.at[2], cin.at[3])
        fields = {"U": 0, "V": 1, "rho": 2, "E": 3, "K": 4}

        def get(f, y):
            return halves(fx[fields[f], y + 1])

        def spread_lane(ref, side, y, spot):
            v = ref[side, y // 4]
            return jnp.broadcast_to(v[:, spot : spot + 1], (NZ, 128))

        edge_w = [jnp.zeros((NZ, 128), F32)] * 2
        edge_d = [jnp.zeros((NZ, 128), F32)] * 2
        k_index = levels()
        east_k = []
        if first_step:
            turned = [[pltpu.roll(cin[2 + side, g], lax.rem(128 - third, 128), 1) for g in range(2)] for side in range(2)]
        for y in range(TY):
            g, base = y // 4, 32 * (y % 4)
            if first_step:
                def column(side, slot):
                    v = turned[side][g]
                    return jnp.broadcast_to(v[:, base + 3 * slot : base + 3 * slot + 1], (NZ, 128))

                u_west = column(0, 0)
                k_west = 0.05 + 0.15 * column(0, 4)
                k_east = 0.05 + 0.15 * column(1, 4)
            else:
                u_west = spread_lane(cin, 0, y, base + 30)
                k_west = spread_lane(cin, 0, y, base + 31)
                k_east = spread_lane(cin, 1, y, base + 31)
            east_k.append(k_east)
            k_here = jnp.broadcast_to(fx[4, y + 1, :, 0:1], (NZ, 128))
            m_here = jnp.where(k_index < nb_ref[0, y + 8 : y + 9, 0:1], 1.0, 0.0)
            m_west = jnp.where(k_index < nb_ref[2, y + 8 : y + 9, 0:1], 1.0, 0.0)
            both = m_here * m_west
            group = (lane >= base) & (lane < base + 32)
            edge_w[g] = jnp.where(group, DT * both * u_west, edge_w[g])
            edge_d[g] = jnp.where(group, DT * both * (k_west + k_here), edge_d[g])
        packed = []
        for g in range(2):
            half = slice(g * 128, g * 128 + 128)
            q255, q1 = by_parity(mine_b[:, half], mine_a[:, half])
            d_1, low_west, high_west, half_east, high_east = column_ends(cin[0, g], cin[1, g], q1, q255)
            w = edge_w[g]
            flux = w * jnp.where(w > 0, low_west, high_west) - edge_d[g] * d_1
            packed.append((d_1, flux, half_east, high_east))
        for g in range(2):
            for n in range(4):
                cin[4 + n, g] = packed[g][n]

        for y in range(-1, TY):
            m, m_n = wet(nb_ref, 0, y), wet(nb_ref, 0, y + 1)
            v, k, k_n = get("V", y), get("K", y), get("K", y + 1)
            both = [m[h] * m_n[h] for h in range(2)]
            put(wy, (y + 1,), [DT * both[h] * v[h] for h in range(2)])
            put(dy, (y + 1,), [DT * both[h] * (k[h] + k_n[h]) for h in range(2)])
            if y < 0:
                continue
            m_e = wet(nb_ref, 1, y)
            both = [m[h] * m_e[h] for h in range(2)]
            u = get("U", y)
            k_e = east_of(k, east_k[y], last)
            put(wx, (y,), [DT * both[h] * u[h] for h in range(2)])
            put(dx, (y,), [DT * both[h] * (k[h] + k_e[h]) for h in range(2)])
            inner = jnp.where(k_index < NZ - 1.0, 0.5 * DT, 0.0)
            put(dz, (y,), [inner * (m[h] * level_down(m[h])) * (k[h] + level_down(k[h])) for h in range(2)])
            put(mm, (y,), m)

        if first_step:
            pltpu.make_async_copy(z_hbm.at[pl.ds(0, NC)], lowq, sems.at[6]).wait()
            pltpu.make_async_copy(z_hbm.at[pl.ds(0, NC)], highq, sems.at[7]).wait()

        def tracer(c, carry):
            if first_step:
                packs = [packed_out[n] for n in range(4)]
                slot = lax.shift_right_arithmetic(lane - 2 * c, 1)
            q = {y: halves(state_ref[c, y]) for y in range(TY)}
            for y in range(2):
                if first_step:
                    low, high = lowq[c, y], highq[c, y]
                else:
                    low = jnp.where(odd, pair_a[c, y], pair_b[c, y])
                    high = jnp.where(odd, pair_b[c, y], pair_a[c, y])
                q[y - 2], q[y + TY] = halves(low), halves(high)
            p = {y: [0.5 * v for v in q[y]] for y in q}
            d = {y: [p[y + 1][h] - p[y][h] for h in range(2)] for y in range(-2, TY + 1)}
            s = {y: [minmod(d[y][h], d[y - 1][h]) for h in range(2)] for y in range(-1, TY + 1)}
            north = {}
            for y in range(-1, TY):
                w, f = halves(wy[y + 1]), halves(dy[y + 1])
                north[y] = [
                    w[h] * jnp.where(w[h] > 0, q[y][h] + s[y][h], q[y + 1][h] - s[y + 1][h]) - f[h] * d[y][h]
                    for h in range(2)
                ]
            for y in range(TY):
                g, spot = y // 4, 32 * (y % 4) + 2 * c
                to_first, to_last = 127 - spot, 126 - spot
                if first_step:
                    dxx, low, high_e = [halves(slopes[n, c, y]) for n in range(3)]
                else:
                    dxx, low, high_e = column_slopes(
                        q[y], p[y], pltpu.roll(cin[6, g], to_last, 1), pltpu.roll(cin[4, g], to_first, 1),
                        pltpu.roll(cin[7, g], to_last, 1), first, last,
                    )
                w, f = halves(wx[y]), halves(dx[y])
                flux = [w[h] * jnp.where(w[h] > 0, low[h], high_e[h]) - f[h] * dxx[h] for h in range(2)]
                flux_w = west_of(flux, pltpu.roll(cin[5, g], to_first, 1), first)
                base, z, m = halves(racc[c, y]), halves(dz[y]), halves(mm[y])
                new = []
                for h in range(2):
                    down = z[h] * (level_down(q[y][h]) - q[y][h])
                    vert = down - level_up(down)
                    new.append(m[h] * (base[h] + (flux_w[h] - flux[h]) + (north[y - 1][h] - north[y][h]) + vert))
                if first_step:
                    put(out_ref, (c, y), new)
                    here = slot == 16 * (y % 4)
                    packs[g] = jnp.where(here, pltpu.roll(new[0], spot, 1), packs[g])
                    packs[2 + g] = jnp.where(here, pltpu.roll(new[1], lax.rem(spot + 2, 128), 1), packs[2 + g])
                else:
                    for h in range(2):
                        out_ref[h, c, pl.ds(y, NZ, stride=TY), :] = new[h]
            if first_step:
                for n in range(4):
                    packed_out[n] = packs[n]
            else:
                for h in range(2):
                    leave(c, h).start()
            return carry

        if first_step:
            packed_out[...] = jnp.zeros((4, NZ, 128), F32)
        lax.fori_loop(0, NC, tracer, 0)

        if first_step:
            def flow(y, carry):
                out = flow_update(get, lambda f, row, side: flow_edges(f, y, side, third), nb_ref, y, ("U", "V", "rho", "E")[:2] + ("rho", "E"))
                put(flow_out, (0, y), out["U"])
                put(flow_out, (1, y), out["V"])
                put(flow_out, (2, y), [0.05 + 0.15 * e for e in out["E"]])
                return carry

            lax.fori_loop(0, TY, flow, 0)

            def edge_rows(c, carry):
                for j in range(2):
                    top, base = out_ref[c, TY - 2 + j], out_ref[c, j]
                    pair_a[c, j] = jnp.where(odd, base, top)
                    pair_b[c, j] = jnp.where(odd, top, base)
                return carry

            lax.fori_loop(0, NC, edge_rows, 0)
            for j, f in ((0, 1), (1, 2)):
                top, base = flow_out[f, TY - 1], flow_out[f, 0]
                pair_a[NC, j] = jnp.where(odd, base, top)
                pair_b[NC, j] = jnp.where(odd, top, base)
            for y in range(TY):
                for h in range(2):
                    green[h, NZ * y : NZ * y + NZ, :] = out_ref[2, y, :, h * 128 : h * 128 + 128]
            shade(lambda h, k: green[h, pl.ds(k, TY, stride=NZ), :], sun2, heat2)
            for y in range(TY):
                rows = slice(NZ * y, NZ * y + NZ)
                put(sun_out, (y,), [sun2[h, rows] for h in range(2)])
                put(heat_ref, (y,), [heat2[h, rows] for h in range(2)])

    if not first_step:
        for h in range(2):
            leave(slice(None), h).wait()
    if first_step:
        @pl.when(section == 0)
        def _():
            give_columns(pack_columns(lambda c, y: halves(out_ref[c, y]), 1), first_out, second_out)

        @pl.when(section > 0)
        def _():
            tiles = [packed_out[n] for n in range(4)]
            for y in range(TY):
                g, base = y // 4, 32 * (y % 4)
                k0 = jnp.broadcast_to(flow_out[2, y, :, 0:1], (NZ, 128))
                u255 = jnp.broadcast_to(flow_out[0, y, :, 255:256], (NZ, 128))
                k255 = jnp.broadcast_to(flow_out[2, y, :, 255:256], (NZ, 128))
                tiles[g] = jnp.where(lane == base + 31, k0, tiles[g])
                tiles[2 + g] = jnp.where(lane == base + 30, u255, tiles[2 + g])
                tiles[2 + g] = jnp.where(lane == base + 31, k255, tiles[2 + g])
            give_columns(tiles, first_out, second_out)


def heat_kernel(out_any, heat1, heat2, heat3, nb_ref, out_hbm, warm_ref, sems):
    section, even, _ = place()

    @pl.when(section == 0)
    def _():
        def moves(back):
            pairs = [(out_hbm.at[pl.ds(6, 3), :, pl.ds(128 * h, 128)], warm_ref.at[h]) for h in range(2)]
            return [pltpu.make_async_copy(*(p[::-1] if back else p), sems.at[h]) for h, p in enumerate(pairs)]

        for move in moves(False):
            move.start()
        for move in moves(False):
            move.wait()

        def body(y, carry):
            ends = [jnp.where(even, heat1[y], heat3[y]), heat2[y], jnp.where(even, heat3[y], heat1[y])]
            for t in range(3):
                m = wet(nb_ref, 0, TY * t + y)
                warm = halves(ends[t])
                for h in range(2):
                    spot = (h, t, pl.ds(y, NZ, stride=TY), slice(None))
                    warm_ref[spot] = warm_ref[spot] + m[h] * (DT * 3.0 * warm[h])
            return carry

        lax.fori_loop(0, TY, body, 0)
        for move in moves(True):
            move.start()
        for move in moves(True):
            move.wait()


def sds(*shape):
    return jax.ShapeDtypeStruct(shape, F32)


def vmem(n):
    return [pl.BlockSpec(memory_space=pltpu.VMEM)] * n


def step_scratch(first_step):
    row = (NZ, NX)
    scratch = []
    if first_step:
        scratch = [pltpu.VMEM((16, 2) + row, F32)]
        scratch += [pltpu.VMEM((NC, 2) + row, F32)] * 2
        scratch += [pltpu.VMEM((9,) + row, F32), pltpu.VMEM((3, 40, NX), F32)] + [pltpu.VMEM(row, F32)] * 4
        scratch += [pltpu.VMEM((4, NZ, 128), F32)]
    scratch += [
        pltpu.VMEM((5, 26) + row, F32),
        pltpu.VMEM((TY,) + row, F32),
        pltpu.VMEM((TY,) + row, F32),
        pltpu.VMEM((TY + 1,) + row, F32),
        pltpu.VMEM((TY + 1,) + row, F32),
        pltpu.VMEM((TY,) + row, F32),
        pltpu.VMEM((TY,) + row, F32),
        pltpu.VMEM((8, 2, NZ, 128), F32),
    ]
    if first_step:
        scratch += [pltpu.VMEM((2, TY * NZ, 128), F32)] * 3
        return scratch + [pltpu.SemaphoreType.DMA((9,))]
    return scratch + [pltpu.VMEM((2, NC, NZ * TY, 128), F32), pltpu.SemaphoreType.DMA((2,))]


def pairs_of(mesh):
    ns, ngy, ngx = (mesh.shape[a] for a in AXES)

    def at(s, g, x):
        return (s * ngy + g) * ngx + x

    cross, ocean, chain, swaps, heat = [], ([], []), ([], []), ([], []), {1: [], 2: [], 3: []}
    for x in range(ngx):
        for g in range(ngy):
            order = (1, 2, 3) if g % 2 == 0 else (3, 2, 1)
            for t, (a, b) in enumerate(zip(order, order[1:])):
                chain[(3 * g + t) % 2].append((at(a, g, x), at(b, g, x)))
            if g + 1 < ngy:
                cross.append((at(order[2], g, x), at(order[2], g + 1, x)))
                chain[(3 * g + 2) % 2].append(cross[-1])
                ocean[g % 2].append((at(0, g, x), at(0, g + 1, x)))
            for s in heat:
                heat[s].append((at(s, g, x), at(0, g, x)))
            if x + 1 < ngx:
                swaps[x % 2].extend((at(s, g, x), at(s, g, x + 1)) for s in range(ns))
    chain = [a + b for a, b in zip(chain, ocean)]
    both = {1: ((0, 1), (2, 3)), 2: ((0, 2),), 3: ((0, 3), (1, 2))}
    for n, sections in both.items():
        pairs = [(at(a, g, x), at(b, g, x)) for a, b in sections for g in range(ngy) for x in range(ngx)]
        both[n] = pairs + turn(pairs)
    return cross + turn(cross), *[[p + turn(p) for p in pairs] for pairs in (ocean, chain, swaps)], heat, both


def turn(pairs):
    return [(b, a) for a, b in pairs]


def solution(mesh):
    cross, ocean, chain, swaps, heat_pairs, section_swaps = pairs_of(mesh)

    def send(value, pairs):
        return lax.ppermute(value, AXES, pairs)

    def program(fields, sea_mask, bottom, reaction, growth):
        x = fields.reshape(NC, NZ * TY, NX)
        row = (NZ, NX)
        block = sds(NC, TY, *row)
        halo = sds(16, 2, *row)
        anywhere = pl.BlockSpec(memory_space=pltpu.HBM)
        loose = pl.BlockSpec(memory_space=pl.ANY)
        weights = jax.ShapeDtypeStruct((NC * NZ, NC * NZ), BF16)

        def call(body, out_shape, in_specs, out_specs, scratch=(), cost=None, limit=VMEM_LIMIT):
            def placed(shape, spec):
                return pltpu.HBM(shape.shape, shape.dtype) if spec is anywhere else shape

            if isinstance(out_specs, tuple):
                out_shape = tuple(placed(*pair) for pair in zip(out_shape, out_specs))
            kernel = pl.pallas_call(
                body,
                out_shape=out_shape,
                in_specs=in_specs,
                out_specs=out_specs,
                scratch_shapes=list(scratch),
                compiler_params=pltpu.CompilerParams(vmem_limit_bytes=limit),
                cost_estimate=cost,
            )

            def run(*operands):
                return kernel(*[
                    pltpu.with_memory_space_constraint(v, pltpu.HBM) if spec is anywhere else v
                    for v, spec in zip(operands, in_specs)
                ])

            return run

        x_scratch = pltpu.VMEM((2, NC, NZ * TY, 128), F32)
        rows = pltpu.VMEM((2, TY * NZ, 128), F32)
        x1, x2, x3, z, oa, ob = call(
            send_kernel, (halo, halo, halo, halo, sds(5, *row), sds(5, *row)), [anywhere],
            (anywhere,) * 4 + tuple(vmem(2)),
            [x_scratch, pltpu.VMEM((16, 2) + row, F32), pltpu.VMEM((16, 2) + row, F32), pltpu.VMEM((3, 16, 2) + row, F32),
             rows, rows, pltpu.SemaphoreType.DMA((5,)), pltpu.SemaphoreType.DMA((2, PARTS))],
        )(x)
        x_in = [send(v, section_swaps[n]) for n, v in ((1, x1), (2, x2), (3, x3))]
        oa_in, ob_in = send(oa, ocean[0]), send(ob, ocean[1])
        mine_a, mine_b, ends = call(
            column_kernel, (sds(*row), sds(*row), sds(2, NC, *row)), [anywhere], tuple(vmem(3)),
            [x_scratch, pltpu.SemaphoreType.DMA((2, PARTS))],
        )(x)
        first_in, second_in = send(mine_a, swaps[0]), send(mine_b, swaps[1])
        z_in = send(z, cross)
        rims = call(rim_kernel, tuple([sds(9, *row)] * 3), vmem(5), tuple(vmem(3)))(ends, oa_in, ob_in, first_in, second_in)
        rims = [send(r, turn(heat_pairs[s])) for s, r in zip((1, 2, 3), rims)]
        react_cost = pl.CostEstimate(flops=6 * 240 * 240 * 2048, bytes_accessed=2 * NC * TY * NZ * NX * 4, transcendentals=0)
        window = pltpu.VMEM((5, TY, 512), jnp.int32)
        state, grown, slopes, w_high, w_low, nb = call(
            functools.partial(react_kernel, True),
            (block, block, sds(3, NC, TY, *row), weights, weights, sds(3, 40, NX)),
            [anywhere] * 3 + vmem(6), tuple(vmem(6)),
            [pltpu.VMEM((3, 2, NZ, 128), F32), x_scratch, pltpu.VMEM((TY,) + row, F32), window, window,
             rows, rows, pltpu.SemaphoreType.DMA((2, PARTS)), pltpu.SemaphoreType.DMA((2, 5, 3))],
            cost=react_cost,
        )(x, sea_mask, bottom, reaction, growth.reshape(1, NC), first_in, second_in, mine_a, mine_b)
        state1, pair_a, pair_b, next_a, next_b, heat1, sun1, flow1 = call(
            functools.partial(step_kernel, True),
            (block, halo, halo, sds(*row), sds(*row), sds(TY, *row), sds(TY, *row), sds(3, TY, *row)),
            vmem(3) + [loose] * 14, tuple(vmem(8)), step_scratch(True),
        )(state, grown, slopes, *x_in, z_in, oa_in, ob_in, first_in, second_in, *rims, nb, mine_a, mine_b)
        pair_a_in, pair_b_in = send(pair_a, chain[0]), send(pair_b, chain[1])
        first1_in, second1_in = send(next_a, swaps[0]), send(next_b, swaps[1])
        heats = [send(heat1, heat_pairs[s]) for s in (1, 2, 3)]
        grown1 = call(
            functools.partial(react_kernel, False), block, vmem(4), vmem(1)[0], cost=react_cost,
        )(state1, sun1, w_high, w_low)
        out = call(
            functools.partial(step_kernel, False), sds(NC, NZ * TY, NX), vmem(10), anywhere, step_scratch(False),
        )(state1, grown1, pair_a_in, pair_b_in, first1_in, second1_in, nb, next_a, next_b, flow1)
        out = pl.pallas_call(
            heat_kernel,
            out_shape=sds(NC, NZ * TY, NX),
            in_specs=[anywhere] + vmem(4),
            out_specs=anywhere,
            scratch_shapes=[pltpu.VMEM((2, 3, NZ * TY, 128), F32), pltpu.SemaphoreType.DMA((2,))],
            input_output_aliases={0: 0},
            compiler_params=pltpu.CompilerParams(vmem_limit_bytes=VMEM_LIMIT),
            name="heating",
        )(out, *heats, nb)
        return out.reshape(1, NC, NZ, TY, NX)

    return jax.shard_map(
        program,
        mesh=mesh,
        in_specs=(P("section", None, None, "gy", "gx"), P(), P(), P(), P()),
        out_specs=P("section", None, None, "gy", "gx"),
        check_vma=False,
    )
```
